256 devices in a mesh: gx: 8 (over y, core), gy: 32 (over z, x).
Axes of the slice: x: 4, y: 4, z: 8, core: 2. Of those that a mesh axis runs over, the one named last changes fastest.
Arguments:
- source: float32 [512, 2, 8, 2048], P('gy', None, None, 'gx'), may hold values from -6 to 6
- lower_coef: float32 [512], P('gy'), may hold values from 0.2 to 36
- upper_coef: float32 [512], P('gy'), may hold values from 0.2 to 36
- span_wave: float32 [8], replicated, may hold values from 0.01 to 0.04
Outputs:
- pressure: float32 [512, 2, 8, 2048], P('gy', None, None, 'gx')
The draws below stay inside these ranges and needn't reach their ends.
All inputs are finite; a program needn't handle non-finite values.
Results may differ from the reference program's by a relative error of at most 0.00075.
Values sent between devices are 32-bit elements; how exact they have to be, the bound alone decides.
A program may use at most 64 MiB of HBM per device.

```python
import math
import jax
import jax.numpy as jnp
from jax import lax

NX = 2048
NY = 512
SZ = 8


def curvature_stencil(rough_field):
    along_x = jnp.roll(rough_field, 1, axis=3) + jnp.roll(rough_field, -1, axis=3) - 2.0 * rough_field
    padded_field = jnp.pad(rough_field, ((1, 1), (0, 0), (0, 0), (0, 0)))
    along_y = padded_field[2:] + padded_field[:-2] - 2.0 * rough_field
    return along_x + along_y


def draw_source(key, part):
    field_key = jax.random.fold_in(key, 0)
    noise_key = jax.random.fold_in(key, 1)
    wave_key = jax.random.fold_in(key, 3)
    phase_key = jax.random.fold_in(key, 4)
    full_shape = (NY, 2, SZ, NX)
    rough_field = jnp.clip(jax.random.normal(field_key, full_shape, jnp.float32), -5.0, 5.0)
    white_noise = jnp.clip(jax.random.normal(noise_key, full_shape, jnp.float32), -5.0, 5.0)
    positions = jnp.arange(NX, dtype=jnp.int32)
    wave_ids = jax.random.randint(wave_key, (SZ,), NX * 3 // 16, NX * 3 // 8 + 1)
    unit_root_radians = (wave_ids[:, None] * positions[None, :] % NX).astype(jnp.float32) * (2.0 * math.pi / NX)
    rotation_exponents = jax.random.uniform(phase_key, (2, SZ, 1), jnp.float32, -math.pi, math.pi)
    elimination_running_state = jnp.cos(unit_root_radians[None] + rotation_exponents)
    heights = (jnp.arange(NY, dtype=jnp.float32) + 0.5) / NY
    boundary_normal_grading = 0.6 + 0.4 * jnp.sin(math.pi * heights)
    gentle_source_grid = 0.5 * boundary_normal_grading[:, None, None, None] * elimination_running_state[None]
    combined = 0.25 * curvature_stencil(rough_field) + 0.05 * white_noise + gentle_source_grid
    return jnp.clip(combined, -6.0, 6.0)


def coupling_draw(key):
    row_pos = (jnp.arange(NY, dtype=jnp.float32) + 0.5) / NY
    stretch = 0.75
    rough_factor = jnp.exp(jax.random.uniform(key, (NY,), jnp.float32, math.log(0.7), math.log(1.4)))
    spacing = 1.0 - stretch * jnp.cos(2.0 * math.pi * row_pos)
    return rough_factor / (spacing * spacing)


def draw_lower_coef(key, part):
    return coupling_draw(jax.random.fold_in(key, 11))


def draw_upper_coef(key, part):
    return coupling_draw(jax.random.fold_in(key, 23))


def setup_inputs(seed: int = 0) -> dict:
    key_of = jax.random.split(jax.random.key(seed), 5)
    source = draw_source(jax.random.fold_in(key_of[4], 71), 0)
    lower_coef = draw_lower_coef(jax.random.fold_in(key_of[4], 71), 0)
    upper_coef = draw_upper_coef(jax.random.fold_in(key_of[4], 71), 0)
    span_wave = jnp.clip(jnp.exp(jax.random.uniform(key_of[3], (SZ,), jnp.float32, math.log(0.01), math.log(0.04))), 0.01, 0.04)
    return {"source": source, "lower_coef": lower_coef, "upper_coef": upper_coef, "span_wave": span_wave}


def reference(source, lower_coef, upper_coef, span_wave):
    complex_field = lax.complex(source[:, 0], source[:, 1])
    transformed = jnp.fft.fft(complex_field, axis=-1)
    spectrum = jnp.stack([jnp.real(transformed), jnp.imag(transformed)], axis=1)
    mode_ids = jnp.arange(NX, dtype=jnp.int32)
    signed_ids = jnp.where(mode_ids < NX // 2, mode_ids, mode_ids - NX).astype(jnp.float32)
    kappa = span_wave[:, None] ** 2 + ((2.0 * signed_ids / NX) ** 2)[None, :]
    row_ids = jnp.arange(NY, dtype=jnp.int32)
    lower_eff = jnp.where(row_ids == 0, jnp.zeros_like(lower_coef), lower_coef)
    upper_eff = jnp.where(row_ids == NY - 1, jnp.zeros_like(upper_coef), upper_coef)

    def downward(carried, inputs):
        factor_prev, solved_prev = carried
        lower_here, upper_here, rhs_here = inputs
        divisor = -(lower_here + upper_here) - kappa - lower_here * factor_prev
        factor = upper_here / divisor
        solved = (rhs_here - lower_here * solved_prev) / divisor
        return (factor, solved), (factor, solved)

    start = (jnp.zeros_like(kappa), jnp.zeros_like(spectrum[0]))
    _, stacked = lax.scan(downward, start, (lower_eff, upper_eff, spectrum))

    def upward(next_sol, inputs):
        factor, solved = inputs
        solution = solved - factor * next_sol
        return solution, solution

    _, modes = lax.scan(upward, jnp.zeros_like(spectrum[0]), stacked, reverse=True)
    back = jnp.fft.ifft(lax.complex(modes[:, 0], modes[:, 1]), axis=-1)
    return jnp.stack([jnp.real(back), jnp.imag(back)], axis=1)
```

```python
import functools
import math

import jax
import jax.numpy as jnp
import numpy as np
from jax import lax
from jax.experimental import pallas as pl
from jax.experimental.pallas import tpu as pltpu
from jax.sharding import PartitionSpec as P

MESH = pl.DeviceIdType.MESH
HIGHEST = lax.Precision.HIGHEST

ROWS = 16
PLANES = 8
NX = 2048
LANES = 128
RADIX = 16
NZ = 8
NXP = 4
BLOCKS = NZ * NXP


def transform_constants():
    lanes = np.arange(LANES)
    angle = 2.0 * np.pi * (np.outer(lanes, lanes) % LANES) / LANES
    c, s = np.cos(angle), np.sin(angle)
    matrix = np.block([[c, -s], [s, c]]).astype(np.float32)
    twist = 2.0 * np.pi * (np.outer(np.arange(RADIX), lanes) % NX) / NX
    twiddle = np.concatenate([np.cos(twist), np.sin(twist)]).astype(np.float32)
    return matrix, twiddle


def rotated(value, index, size, inverse):
    re, im = value
    index = index % size
    if index == 0:
        return value
    if 4 * index == size:
        return (-im, re) if inverse else (im, -re)
    c = math.cos(2.0 * math.pi * index / size)
    s = math.sin(2.0 * math.pi * index / size)
    if not inverse:
        s = -s
    return (re * c - im * s, re * s + im * c)


def butterflies(values, inverse):
    size = len(values)
    if size == 1:
        return values
    even = butterflies(values[0::2], inverse)
    odd = butterflies(values[1::2], inverse)
    odd = [rotated(o, k, size, inverse) for k, o in enumerate(odd)]
    low = [(e[0] + o[0], e[1] + o[1]) for e, o in zip(even, odd)]
    high = [(e[0] - o[0], e[1] - o[1]) for e, o in zip(even, odd)]
    return low + high


def kernel(
    source, lower_hbm, upper_hbm, span_hbm, matrix_hbm, twiddle_hbm, fbuf,
    src, sbuf, rbuf, ure, uim, spec, matrix, twiddle, lower, upper, span,
    coef, mbuf, abuf, wbuf, gbuf, gin, alone, factors,
    raw, gz, zrecv, obuf,
    load_sem, fs_sem, fr_sem, cxs_sem, cxr_sem, czs_sem, czr_sem,
    zs_sem, zr_sem, xs_sem, xr_sem, bs_sem, br_sem, near_sem, far_sem,
):
    gx = lax.axis_index("gx")
    gy = lax.axis_index("gy")
    zi = gy // NXP
    xi = gy % NXP
    base = zi * NXP

    chip, core = gx // 2, gx % 2
    gx_peers = [lax.rem(chip + d, PLANES // 2) * 2 + lax.rem(core + c, 2)
                for d, c in ((2, 0), (2, 1), (1, 0), (3, 0), (1, 1), (3, 1), (0, 1))]
    x_peers = [lax.rem(xi + d, NXP) for d in (2, 1, 3)]
    z_peers = [lax.rem(zi + d, NZ) for d in (4, 3, 5, 2, 6, 1, 7)]

    def at_gx(q):
        return (q, gy)

    def at_x(q):
        return (gx, base + q)

    def at_z(q):
        return (gx, q * NXP + xi)

    z_near = [lax.rem(zi + d, NZ) for d in (1, NZ - 1)]
    z_far = [lax.rem(zi + d, NZ) for d in (2, NZ - 2)]
    near = [at_z(q) for q in z_near] + [at_x(q) for q in x_peers] + [at_gx(q) for q in gx_peers]
    barrier = pltpu.get_barrier_semaphore()
    for device in near:
        pl.semaphore_signal(barrier, inc=1, device_id=device, device_id_type=MESH)

    loads = []
    for part in range(2):
        for xt in range(2):
            loads.append(pltpu.make_async_copy(
                source.at[:, part, :, pl.ds(xt * LANES, LANES)], src.at[xt, part],
                load_sem.at[2 * xt + part]))
    for n, (there, here) in enumerate(((lower_hbm, lower), (upper_hbm, upper), (span_hbm, span),
                                       (matrix_hbm, matrix), (twiddle_hbm, twiddle))):
        loads.append(pltpu.make_async_copy(there, here, load_sem.at[4 + n]))
    for load in loads:
        load.start()

    for load in loads[:4]:
        load.wait()
    flat = src.reshape(4 * ROWS * PLANES, LANES)
    for q in range(PLANES):
        sbuf[q] = flat[pl.ds(q, 4 * ROWS, stride=PLANES), :]
    rbuf[gx] = sbuf[gx]

    for load in loads[4:]:
        load.wait()
    first, last = gy == 0, gy == BLOCKS - 1
    low = [lower[i] for i in range(ROWS)]
    upp = [upper[i] for i in range(ROWS)]
    low[0] = jnp.where(first, 0.0, low[0])
    upp[-1] = jnp.where(last, 0.0, upp[-1])
    sums, lost = [], []
    for l, u in zip(low, upp):
        total = l + u
        rest = total - l
        sums.append(total)
        lost.append(-((l - (total - rest)) + (u - rest)))
    lane = lax.broadcasted_iota(jnp.int32, (1, LANES), 1)
    row = jnp.zeros((1, LANES), jnp.float32)
    for i, value in enumerate(low + upp + sums + lost + upp[::-1] + low[::-1] + sums[::-1] + lost[::-1]):
        row = jnp.where(lane == i, value, row)
    coef[gy] = row

    pl.semaphore_wait(barrier, len(near))

    def remote(src_ref, dst_ref, send, recv, device):
        return pltpu.make_async_remote_copy(
            src_ref=src_ref, dst_ref=dst_ref, send_sem=send, recv_sem=recv,
            device_id=device, device_id_type=MESH)

    forward = [remote(sbuf.at[q], rbuf.at[gx], fs_sem.at[q], fr_sem.at[gx], at_gx(q)) for q in gx_peers]
    coef_x = [remote(coef.at[gy], coef.at[gy], cxs_sem.at[q], cxr_sem.at[xi], at_x(q)) for q in x_peers]
    for copy in coef_x + forward:
        copy.start()
    for q in z_near:
        pl.semaphore_signal(near_sem, inc=1, device_id=at_z(q), device_id_type=MESH)

    k1 = lax.broadcasted_iota(jnp.int32, (RADIX, LANES), 0)
    k2 = lax.broadcasted_iota(jnp.int32, (RADIX, LANES), 1)
    mode = k1 + RADIX * k2
    signed = jnp.where(mode < NX // 2, mode, mode - NX).astype(jnp.float32)
    wave = 2.0 * signed / NX
    kappa = span[gx] * span[gx] + wave * wave
    one = jnp.ones((RADIX, LANES), jnp.float32)

    def pivots(order, ahead, behind, g, keep, into):
        for i in order:
            l, u = ahead[i], behind[i]
            s = (((sums[i] + kappa) - sums[i]) + lost[i]) + l * g
            inv = 1.0 / (u + s)
            g = s * inv
            keep[into, i] = l * inv
            keep[into + 1, i] = inv
            if keep is factors:
                keep[into + 2, i] = u * inv
        return g

    pivots(range(ROWS), low, upp, one, alone, 0)
    pivots(range(ROWS - 1, -1, -1), upp, low, one, alone, 2)

    pl.semaphore_wait(near_sem, 2)
    for q in z_far:
        pl.semaphore_signal(far_sem, inc=1, device_id=at_z(q), device_id_type=MESH)

    for q in x_peers:
        there = coef.at[base + q]
        remote(there, there, cxs_sem.at[q], cxr_sem.at[q], at_x(q)).wait_recv()
    pl.semaphore_wait(far_sem, 2)
    group = coef.at[pl.ds(base, NXP)]
    coef_z = [remote(group, group, czs_sem.at[q], czr_sem.at[zi], at_z(q)) for q in z_peers]
    for copy in coef_z:
        copy.start()

    def block_product(t, way):
        row = jnp.broadcast_to(coef[t], (8, LANES))
        turned = pltpu.roll(row, LANES // 2, 1)
        row = jnp.where(way == 0, row, turned)

        def splat(i):
            one = jnp.broadcast_to(row[:, i : i + 1], (8, LANES))
            return one, jnp.concatenate([one, one], axis=0)

        scale = None
        for i in range(ROWS):
            one, l = splat(i)
            _, u = splat(ROWS + i)
            _, total = splat(2 * ROWS + i)
            _, gained = splat(3 * ROWS + i)
            rounded = ((total + kappa) - total) + gained
            if i == 0:
                scale, a, b, c, d = one, l, rounded, l, u + rounded
                continue
            scale = scale * one
            a = l * a + rounded * c
            b = l * b + rounded * d
            c = a + u * c
            d = b + u * d
        mbuf[way, t, 0] = a
        mbuf[way, t, 1] = b
        mbuf[way, t, 2] = c
        mbuf[way, t, 3] = d
        mbuf[way, t, 4] = jnp.concatenate([scale, scale], axis=0)

    @pl.loop(0, 2)
    def _(way):
        for j in range(NXP):
            block_product(base + j, way)

    for q in gx_peers:
        remote(sbuf.at[q], rbuf.at[q], fs_sem.at[q], fr_sem.at[q], at_gx(q)).wait_recv()
    values = []
    for a in range(RADIX):
        at = (a % 2) * 32
        values.append((rbuf[a // 2, at : at + ROWS, :], rbuf[a // 2, at + ROWS : at + 2 * ROWS, :]))
    values = butterflies(values, False)
    for k in range(RADIX):
        re, im = values[k]
        c, s = twiddle[k : k + 1, :], twiddle[RADIX + k : RADIX + k + 1, :]
        ure[pl.ds(k, ROWS, stride=RADIX), :] = re * c + im * s
        uim[pl.ds(k, ROWS, stride=RADIX), :] = im * c - re * s
    both = jnp.concatenate([ure[...], uim[...]], axis=1)
    spec[...] = jnp.dot(both, matrix[...], precision=HIGHEST, preferred_element_type=jnp.float32)

    def rhs(i, part):
        return spec[i * RADIX : (i + 1) * RADIX, part * LANES : (part + 1) * LANES]

    for way, order in enumerate((range(ROWS), range(ROWS - 1, -1, -1))):
        for part in range(2):
            y = None
            for i in order:
                r = rhs(i, part) * alone[2 * way + 1, i]
                y = -r if y is None else alone[2 * way, i] * y - r
            raw[xi, (2 * way + part) * RADIX : (2 * way + part + 1) * RADIX, :] = y
    to_x = [remote(raw.at[xi], raw.at[xi], xs_sem.at[q], xr_sem.at[xi], at_x(q)) for q in x_peers]
    for copy in to_x:
        copy.start()

    @pl.loop(0, NZ - 1)
    def _(n):
        step = n // 2 + 1
        q = lax.rem(zi + jnp.where(n % 2 == 0, step, NZ - step), NZ)
        there = coef.at[pl.ds(q * NXP, NXP)]
        remote(there, there, czs_sem.at[q], czr_sem.at[q], at_z(q)).wait_recv()
        for j in range(NXP):
            block_product(q * NXP + j, (q > zi).astype(jnp.int32))

    gbuf[...] = jnp.zeros_like(gbuf)

    def advance(t, way):
        g = gbuf[way]
        inv = 1.0 / (mbuf[way, t, 2] * g + mbuf[way, t, 3])
        gbuf[way] = (mbuf[way, t, 0] * g + mbuf[way, t, 1]) * inv
        abuf[way, t] = mbuf[way, t, 4] * inv
        return g

    @pl.loop(0, BLOCKS - NXP)
    def _(n):
        above = (n >= base).astype(jnp.int32)
        advance(jnp.where(n < base, n, BLOCKS - 1 - (n - base)), above)

    for j in range(NXP):
        gin[0, j] = advance(base + j, 0)
        gin[1, NXP - 1 - j] = advance(base + NXP - 1 - j, 1)

    for q in x_peers:
        remote(raw.at[q], raw.at[q], xs_sem.at[q], xr_sem.at[q], at_x(q)).wait_recv()
    entering = []
    for way, order in enumerate((range(NXP), range(NXP - 1, -1, -1))):
        run, mine = [jnp.zeros_like(one)] * 2, [jnp.zeros_like(one)] * 2
        for j in order:
            here = xi == j
            a = abuf[way, base + j]
            ae = a * (1.0 - gin[way, j])
            for part in range(2):
                end = raw[j, (2 * way + part) * RADIX : (2 * way + part + 1) * RADIX, :]
                start = raw[j, (2 - 2 * way + part) * RADIX : (3 - 2 * way + part) * RADIX, :]
                mine[part] = jnp.where(here, run[part], mine[part])
                run[part] = a * run[part] + (end + ae * start)
        for part in range(2):
            gz[way, part * RADIX : (part + 1) * RADIX, :] = run[part]
        entering.append(mine)

    to_z = []
    for q in z_peers:
        which = jnp.where(q > zi, 0, 1)
        to_z.append(remote(gz.at[which], zrecv.at[zi], zs_sem.at[q], zr_sem.at[zi], at_z(q)))
    for copy in to_z:
        copy.start()

    def down(n, run):
        t = gy - 1 - n
        wbuf[t] = run
        return run * abuf[0, t]

    def below(n, run):
        t = base - 1 - n
        wbuf[t] = run
        return run * abuf[0, t]

    pre = lax.fori_loop(0, xi, down, one)
    lax.fori_loop(0, base, below, one)

    def up(n, run):
        return run * abuf[1, gy + 1 + n]

    def above(n, run):
        t = base + NXP + n
        wbuf[t] = run
        return run * abuf[1, t]

    post = lax.fori_loop(0, NXP - 1 - xi, up, one)
    lax.fori_loop(0, BLOCKS - NXP - base, above, one)

    g_end = pivots(range(ROWS), low, upp, gin[0, xi], factors, 0)
    h_in = gin[1, xi]
    scale = 1.0 / (g_end + h_in * factors[2, ROWS - 1])

    sy = [jnp.zeros_like(one)] * 2
    sz = [jnp.zeros_like(one)] * 2
    for q in z_peers[::-1]:
        remote(gz.at[0], zrecv.at[q], zs_sem.at[q], zr_sem.at[q], at_z(q)).wait_recv()
        lower_side = q < zi
        w = wbuf[q * NXP + jnp.where(lower_side, NXP - 1, 0)]
        wy = jnp.where(lower_side, w, 0.0)
        wz = jnp.where(lower_side, 0.0, w)
        for part in range(2):
            v = zrecv[q, part * RADIX : (part + 1) * RADIX, :]
            sy[part] = sy[part] + wy * v
            sz[part] = sz[part] + wz * v

    ends = [[], []]
    for part in range(2):
        y = entering[0][part] + pre * sy[part]
        for i in range(ROWS):
            y = factors[0, i] * y - factors[1, i] * rhs(i, part)
            ends[part].append(y)
    for part in range(2):
        ref = uim if part else ure
        z_in = entering[1][part] + post * sz[part]
        x = (factors[2, ROWS - 1] * z_in + ends[part][-1]) * scale
        for i in range(ROWS - 1, -1, -1):
            if i < ROWS - 1:
                x = factors[2, i] * x + ends[part][i]
            ref[i * RADIX : (i + 1) * RADIX, :] = x

    both = jnp.concatenate([ure[...], uim[...]], axis=1)
    back = lax.dot_general(both, matrix[...], (((1,), (1,)), ((), ())), precision=HIGHEST,
                           preferred_element_type=jnp.float32)
    ure[...] = back[:, :LANES]
    uim[...] = back[:, LANES:]
    values = []
    for k in range(RADIX):
        re = ure[pl.ds(k, ROWS, stride=RADIX), :]
        im = uim[pl.ds(k, ROWS, stride=RADIX), :]
        c = twiddle[k : k + 1, :] * (1.0 / NX)
        s = twiddle[RADIX + k : RADIX + k + 1, :] * (1.0 / NX)
        values.append((re * c - im * s, im * c + re * s))
    values = butterflies(values, True)
    for a in range(RADIX):
        at = (a % 2) * 32
        obuf[a // 2, at : at + ROWS, :] = values[a][0]
        obuf[a // 2, at + ROWS : at + 2 * ROWS, :] = values[a][1]
    backward = [remote(obuf.at[q], fbuf.at[gx], bs_sem.at[q], br_sem.at[gx], at_gx(q)) for q in gx_peers]
    for copy in backward:
        copy.start()
    own = pltpu.make_async_copy(obuf.at[gx], fbuf.at[gx], load_sem.at[0])
    own.start()
    for copy in coef_x + forward + coef_z + to_z + to_x:
        copy.wait_send()
    own.wait()
    for q in gx_peers:
        remote(obuf.at[q], fbuf.at[q], bs_sem.at[q], br_sem.at[q], at_gx(q)).wait_recv()
    for copy in backward:
        copy.wait_send()


def assemble(fbuf, out):
    for q in range(PLANES):
        for xt in range(2):
            for part in range(2):
                at = (xt * 2 + part) * ROWS
                out[pl.ds((part * 2 + xt) * PLANES + q, ROWS, stride=4 * PLANES), :] = fbuf[q, at : at + ROWS, :]


def local(source, lower, upper, span):
    matrix, twiddle = transform_constants()
    f32 = jnp.float32
    dma = pltpu.SemaphoreType.DMA
    vmem = lambda *shape: pltpu.VMEM(shape, f32)
    smem = lambda *shape: pltpu.SMEM(shape, f32)
    any_spec = pl.BlockSpec(memory_space=pl.ANY)
    planes = pl.pallas_call(
        kernel,
        out_shape=jax.ShapeDtypeStruct((PLANES, 64, LANES), f32),
        in_specs=[pl.BlockSpec(memory_space=pltpu.HBM)] * 6,
        out_specs=any_spec,
        scratch_shapes=[
            vmem(2, 2, ROWS, PLANES, LANES), vmem(PLANES, 64, LANES), vmem(PLANES, 64, LANES),
            vmem(256, LANES), vmem(256, LANES), vmem(256, 256), vmem(256, 256), vmem(2 * RADIX, LANES),
            smem(ROWS), smem(ROWS), smem(PLANES),
            vmem(BLOCKS, 1, LANES), vmem(2, BLOCKS, 5, RADIX, LANES), vmem(2, BLOCKS, RADIX, LANES),
            vmem(BLOCKS, RADIX, LANES), vmem(2, RADIX, LANES), vmem(2, NXP, RADIX, LANES),
            vmem(4, ROWS, RADIX, LANES), vmem(3, ROWS, RADIX, LANES),
            vmem(NXP, 64, LANES), vmem(2, 32, LANES), vmem(NZ, 32, LANES), vmem(PLANES, 64, LANES),
            dma((9,)), dma((PLANES,)), dma((PLANES,)), dma((NXP,)), dma((NXP,)), dma((NZ,)), dma((NZ,)),
            dma((NZ,)), dma((NZ,)), dma((NXP,)), dma((NXP,)), dma((PLANES,)), dma((PLANES,)),
            pltpu.SemaphoreType.REGULAR, pltpu.SemaphoreType.REGULAR,
        ],
        compiler_params=pltpu.CompilerParams(
            collective_id=0, has_side_effects=True, vmem_limit_bytes=16 * 1024 * 1024),
    )(*[pltpu.with_memory_space_constraint(x, pltpu.HBM)
        for x in (source, lower, upper, span, jnp.asarray(matrix), jnp.asarray(twiddle))])
    result = pl.pallas_call(
        assemble,
        out_shape=jax.ShapeDtypeStruct((ROWS * 4 * PLANES, LANES), f32),
        in_specs=[pl.BlockSpec(memory_space=pltpu.VMEM)],
        out_specs=pl.BlockSpec(memory_space=pltpu.VMEM),
        compiler_params=pltpu.CompilerParams(vmem_limit_bytes=4 * 1024 * 1024),
    )(planes)
    result = result.reshape(ROWS, 2, 2, PLANES, LANES)
    return result.transpose(0, 1, 3, 2, 4).reshape(source.shape)


def solution(mesh):
    in_specs = (P("gy", None, None, "gx"), P("gy"), P("gy"), P())
    out_specs = P("gy", None, None, "gx")
    return jax.shard_map(local, mesh=mesh, in_specs=in_specs, out_specs=out_specs, check_vma=False)
```

```python
import math

import jax
import jax.numpy as jnp
import ml_dtypes
import numpy as np
from jax import lax
from jax.experimental import pallas as pl
from jax.experimental.pallas import tpu as pltpu
from jax.sharding import PartitionSpec as P

MESH = pl.DeviceIdType.MESH

ROWS = 16
PLANES = 8
NX = 2048
LANES = 128
RADIX = 16
NZ = 8
NXP = 4
BLOCKS = NZ * NXP


def transform_constants():
    lanes = np.arange(LANES)
    angle = 2.0 * np.pi * (np.outer(lanes, lanes) % LANES) / LANES
    c, s = np.cos(angle), np.sin(angle)
    matrix = np.block([[c, -s], [s, c]]).astype(np.float32)
    terms, rest = [], matrix
    for _ in range(3):
        terms.append(rest.astype(ml_dtypes.bfloat16))
        rest = rest - terms[-1].astype(np.float32)
    matrix = np.concatenate([terms[0], terms[1], terms[2], terms[0], terms[1], terms[0]])
    twist = 2.0 * np.pi * (np.outer(np.arange(RADIX), lanes) % NX) / NX
    twiddle = np.concatenate([np.cos(twist), np.sin(twist)]).astype(np.float32)
    return matrix, twiddle


def rotated(value, index, size, inverse):
    re, im = value
    index = index % size
    if index == 0:
        return value
    if 4 * index == size:
        return (-im, re) if inverse else (im, -re)
    c = math.cos(2.0 * math.pi * index / size)
    s = math.sin(2.0 * math.pi * index / size)
    if not inverse:
        s = -s
    return (re * c - im * s, re * s + im * c)


def butterflies(values, inverse):
    size = len(values)
    if size == 1:
        return values
    even = butterflies(values[0::2], inverse)
    odd = butterflies(values[1::2], inverse)
    odd = [rotated(o, k, size, inverse) for k, o in enumerate(odd)]
    low = [(e[0] + o[0], e[1] + o[1]) for e, o in zip(even, odd)]
    high = [(e[0] - o[0], e[1] - o[1]) for e, o in zip(even, odd)]
    return low + high


def product(x, matrix):
    high = x.astype(jnp.bfloat16)
    rest = x - high.astype(jnp.float32)
    middle = rest.astype(jnp.bfloat16)
    low = (rest - middle.astype(jnp.float32)).astype(jnp.bfloat16)
    terms = jnp.concatenate([high, high, high, middle, middle, low], axis=1)
    return jnp.dot(terms, matrix, preferred_element_type=jnp.float32)


def times(x, y):
    a, b, c, d = x
    e, f, g, h = y
    return (a * e + b * g, a * f + b * h, c * e + d * g, c * f + d * h)


def scaled(x):
    r = pl.reciprocal(x[2] + x[3], approx=True)
    return tuple(v * r for v in x)


def kernel(
    source, lower_hbm, upper_hbm, span_hbm, matrix_hbm, twiddle_hbm, fbuf,
    src, sbuf, rbuf, ure, uim, spec, matrix, twiddle, lower, upper, span,
    coef, mbuf, abuf, wbuf, gbuf, gin, chain, alone, factors,
    raw, gz, zrecv, obuf,
    load_sem, send_sem, recv_sem, cxr_sem, czr_sem, near_sem, far_sem,
):
    gx = lax.axis_index("gx")
    gy = lax.axis_index("gy")
    zi = gy // NXP
    xi = gy % NXP
    base = zi * NXP

    chip, core = gx // 2, gx % 2
    gx_peers = [lax.rem(chip + d, PLANES // 2) * 2 + lax.rem(core + c, 2)
                for d, c in ((2, 0), (2, 1), (1, 0), (3, 0), (1, 1), (3, 1), (0, 1))]
    x_peers = [lax.rem(xi + d, NXP) for d in (2, 1, 3)]
    z_peers = [lax.rem(zi + d, NZ) for d in (4, 3, 5, 2, 6, 1, 7)]

    def at_gx(q):
        return (q, gy)

    def at_x(q):
        return (gx, base + q)

    def at_z(q):
        return (gx, q * NXP + xi)

    z_near = [lax.rem(zi + d, NZ) for d in (1, NZ - 1)]
    z_far = [lax.rem(zi + d, NZ) for d in (2, NZ - 2)]
    near = [at_z(q) for q in z_near] + [at_x(q) for q in x_peers] + [at_gx(q) for q in gx_peers]
    loads = [pltpu.make_async_copy(there, here, load_sem.at[n]) for n, (there, here) in enumerate((
        (source, src), (lower_hbm, lower), (upper_hbm, upper), (span_hbm, span),
        (twiddle_hbm, twiddle), (matrix_hbm, matrix)))]
    loads[0].start()
    barrier = pltpu.get_barrier_semaphore()
    for device in near:
        pl.semaphore_signal(barrier, inc=1, device_id=device, device_id_type=MESH)
    for load in loads[1:]:
        load.start()

    loads[0].wait()
    for q in range(PLANES):
        for xt in range(2):
            for part in range(2):
                at = (xt * 2 + part) * ROWS
                sbuf[q, at : at + ROWS, :] = src[pl.ds((part * 2 + xt) * PLANES + q, ROWS, stride=4 * PLANES), :]

    pl.semaphore_wait(barrier, len(near))

    def remote(src_ref, dst_ref, send, recv, device):
        return pltpu.make_async_remote_copy(
            src_ref=src_ref, dst_ref=dst_ref, send_sem=send, recv_sem=recv,
            device_id=device, device_id_type=MESH)

    forward = [remote(sbuf.at[q], rbuf.at[gx], send_sem.at[0], recv_sem.at[0], at_gx(q)) for q in gx_peers]
    for copy in forward:
        copy.start()
    for q in z_near:
        pl.semaphore_signal(near_sem, inc=1, device_id=at_z(q), device_id_type=MESH)
    rbuf[gx] = sbuf[gx]

    for load in loads[1:4]:
        load.wait()
    first, last = gy == 0, gy == BLOCKS - 1
    low = [lower[i] for i in range(ROWS)]
    upp = [upper[i] for i in range(ROWS)]
    low[0] = jnp.where(first, 0.0, low[0])
    upp[-1] = jnp.where(last, 0.0, upp[-1])
    sums, lost = [], []
    for l, u in zip(low, upp):
        total = l + u
        rest = total - l
        sums.append(total)
        lost.append(-((l - (total - rest)) + (u - rest)))
    lane = lax.broadcasted_iota(jnp.int32, (1, LANES), 1)
    row = jnp.zeros((1, LANES), jnp.float32)
    for i, value in enumerate(low + upp + sums + lost + upp[::-1] + low[::-1] + sums[::-1] + lost[::-1]):
        row = jnp.where(lane == i, value, row)
    coef[gy] = row

    coef_x = [remote(coef.at[gy], coef.at[gy], send_sem.at[1], cxr_sem.at[xi], at_x(q)) for q in x_peers]
    for copy in coef_x:
        copy.start()

    k1 = lax.broadcasted_iota(jnp.int32, (RADIX, LANES), 0)
    k2 = lax.broadcasted_iota(jnp.int32, (RADIX, LANES), 1)
    mode = k1 + RADIX * k2
    signed = jnp.where(mode < NX // 2, mode, mode - NX).astype(jnp.float32)
    wave = 2.0 * signed / NX
    kappa = span[gx] * span[gx] + wave * wave
    one = jnp.ones((RADIX, LANES), jnp.float32)

    def pivots(order, ahead, behind, g, keep, into):
        for i in order:
            l, u = ahead[i], behind[i]
            s = (((sums[i] + kappa) - sums[i]) + lost[i]) + l * g
            inv = 1.0 / (u + s)
            g = s * inv
            keep[into, i] = l * inv
            keep[into + 1, i] = inv
            if keep is factors:
                keep[into + 2, i] = u * inv
        return g

    pivots(range(ROWS), low, upp, one, alone, 0)
    pivots(range(ROWS - 1, -1, -1), upp, low, one, alone, 2)

    pl.semaphore_wait(near_sem, 2)
    for q in z_far:
        pl.semaphore_signal(far_sem, inc=1, device_id=at_z(q), device_id_type=MESH)

    for q in x_peers:
        there = coef.at[base + q]
        remote(there, there, send_sem.at[1], cxr_sem.at[q], at_x(q)).wait_recv()
    pl.semaphore_wait(far_sem, 2)
    group = coef.at[pl.ds(base, NXP)]
    coef_z = [remote(group, group, send_sem.at[2], czr_sem.at[zi], at_z(q)) for q in z_peers]
    for copy in coef_z:
        copy.start()

    def block_product(t, way):
        row = jnp.broadcast_to(coef[t], (8, LANES))
        turned = pltpu.roll(row, LANES // 2, 1)
        row = jnp.where(way == 0, row, turned)

        def splat(i):
            one = jnp.broadcast_to(row[:, i : i + 1], (8, LANES))
            return one, jnp.concatenate([one, one], axis=0)

        scale = None
        for i in range(ROWS):
            one, l = splat(i)
            _, u = splat(ROWS + i)
            _, total = splat(2 * ROWS + i)
            _, gained = splat(3 * ROWS + i)
            rounded = ((total + kappa) - total) + gained
            if i == 0:
                scale, a, b, c, d = one, l, rounded, l, u + rounded
                continue
            scale = scale * one
            a = l * a + rounded * c
            b = l * b + rounded * d
            c = a + u * c
            d = b + u * d
        mbuf[way, t, 0] = a
        mbuf[way, t, 1] = b
        mbuf[way, t, 2] = c
        mbuf[way, t, 3] = d
        mbuf[way, t, 4] = jnp.concatenate([scale, scale], axis=0)
        return scaled((a, b, c, d))

    @pl.loop(0, 2)
    def _(way):
        for j in range(NXP):
            block_product(base + j, way)

    def wait_for(ref, sem):
        pltpu.make_async_copy(ref, ref, sem).wait()

    wait_for(rbuf.at[pl.ds(0, PLANES - 1)], recv_sem.at[0])
    loads[4].wait()
    loads[5].wait()
    values = []
    for a in range(RADIX):
        at = (a % 2) * 32
        values.append((rbuf[a // 2, at : at + ROWS, :], rbuf[a // 2, at + ROWS : at + 2 * ROWS, :]))
    values = butterflies(values, False)
    for k in range(RADIX):
        re, im = values[k]
        c, s = twiddle[k : k + 1, :], twiddle[RADIX + k : RADIX + k + 1, :]
        ure[pl.ds(k, ROWS, stride=RADIX), :] = re * c + im * s
        uim[pl.ds(k, ROWS, stride=RADIX), :] = im * c - re * s
    both = jnp.concatenate([ure[...], uim[...]], axis=1)
    spec[...] = product(both, matrix[...])

    def rhs(i, part):
        return spec[i * RADIX : (i + 1) * RADIX, part * LANES : (part + 1) * LANES]

    for way, order in enumerate((range(ROWS), range(ROWS - 1, -1, -1))):
        for part in range(2):
            y = None
            for i in order:
                r = rhs(i, part) * alone[2 * way + 1, i]
                y = -r if y is None else alone[2 * way, i] * y - r
            raw[xi, (2 * way + part) * RADIX : (2 * way + part + 1) * RADIX, :] = y
    to_x = [remote(raw.at[xi], raw.at[xi], send_sem.at[3], recv_sem.at[1], at_x(q)) for q in x_peers]
    for copy in to_x:
        copy.start()

    for slot in range(4):
        for k in range(4):
            chain[slot, k] = jnp.zeros_like(one) if k in (1, 2) else one

    @pl.loop(0, NZ - 1)
    def _(n):
        step = n // 2 + 1
        q = lax.rem(zi + jnp.where(n % 2 == 0, step, NZ - step), NZ)
        there = coef.at[pl.ds(q * NXP, NXP)]
        remote(there, there, send_sem.at[2], czr_sem.at[q], at_z(q)).wait_recv()
        way = (q > zi).astype(jnp.int32)
        far = jnp.logical_xor(way == 1, n % 2 == 0)
        slot = way + 2 * far.astype(jnp.int32)
        whole = None
        for j in range(NXP):
            this = block_product(q * NXP + jnp.where(way == 0, j, NXP - 1 - j), way)
            whole = this if whole is None else times(this, whole)
        old = tuple(chain[slot, k] for k in range(4))
        outer = tuple(jnp.where(far, w, o) for w, o in zip(whole, old))
        inner = tuple(jnp.where(far, o, w) for w, o in zip(whole, old))
        for k, v in enumerate(scaled(times(outer, inner))):
            chain[slot, k] = v

    def advance(t, way, g):
        inv = 1.0 / (mbuf[way, t, 2] * g + mbuf[way, t, 3])
        abuf[way, t] = mbuf[way, t, 4] * inv
        return (mbuf[way, t, 0] * g + mbuf[way, t, 1]) * inv

    enter = []
    for way in range(2):
        top, bottom = chain[way + 2, 1], chain[way + 2, 3]
        enter.append((chain[way, 0] * top + chain[way, 1] * bottom) / (chain[way, 2] * top + chain[way, 3] * bottom))
    for j in range(NXP):
        for way in range(2):
            t = j if way == 0 else NXP - 1 - j
            gin[way, t] = enter[way]
            enter[way] = advance(base + t, way, enter[way])

    wait_for(raw.at[pl.ds(0, NXP - 1)], recv_sem.at[1])
    entering = []
    for way, order in enumerate((range(NXP), range(NXP - 1, -1, -1))):
        run, mine = [jnp.zeros_like(one)] * 2, [jnp.zeros_like(one)] * 2
        for j in order:
            here = xi == j
            a = abuf[way, base + j]
            ae = a * (1.0 - gin[way, j])
            for part in range(2):
                end = raw[j, (2 * way + part) * RADIX : (2 * way + part + 1) * RADIX, :]
                start = raw[j, (2 - 2 * way + part) * RADIX : (3 - 2 * way + part) * RADIX, :]
                mine[part] = jnp.where(here, run[part], mine[part])
                run[part] = a * run[part] + (end + ae * start)
        for part in range(2):
            gz[way, part * RADIX : (part + 1) * RADIX, :] = run[part]
        entering.append(mine)

    to_z = []
    for q in z_peers:
        which = jnp.where(q > zi, 0, 1)
        to_z.append(remote(gz.at[which], zrecv.at[zi], send_sem.at[4], recv_sem.at[2], at_z(q)))
    for copy in to_z:
        copy.start()

    gbuf[...] = jnp.zeros_like(gbuf)

    @pl.loop(0, BLOCKS - NXP)
    def _(n):
        way = (n >= base).astype(jnp.int32)
        gbuf[way] = advance(jnp.where(n < base, n, BLOCKS - 1 - (n - base)), way, gbuf[way])

    def down(n, run):
        t = gy - 1 - n
        wbuf[t] = run
        return run * abuf[0, t]

    def below(n, run):
        t = base - 1 - n
        wbuf[t] = run
        return run * abuf[0, t]

    pre = lax.fori_loop(0, xi, down, one)
    lax.fori_loop(0, base, below, one)

    def up(n, run):
        return run * abuf[1, gy + 1 + n]

    def above(n, run):
        t = base + NXP + n
        wbuf[t] = run
        return run * abuf[1, t]

    post = lax.fori_loop(0, NXP - 1 - xi, up, one)
    lax.fori_loop(0, BLOCKS - NXP - base, above, one)

    g_end = pivots(range(ROWS), low, upp, gin[0, xi], factors, 0)
    h_in = gin[1, xi]
    scale = 1.0 / (g_end + h_in * factors[2, ROWS - 1])

    sy = [jnp.zeros_like(one)] * 2
    sz = [jnp.zeros_like(one)] * 2
    wait_for(zrecv.at[pl.ds(0, NZ - 1)], recv_sem.at[2])
    for q in z_peers:
        lower_side = q < zi
        w = wbuf[q * NXP + jnp.where(lower_side, NXP - 1, 0)]
        wy = jnp.where(lower_side, w, 0.0)
        wz = jnp.where(lower_side, 0.0, w)
        for part in range(2):
            v = zrecv[q, part * RADIX : (part + 1) * RADIX, :]
            sy[part] = sy[part] + wy * v
            sz[part] = sz[part] + wz * v

    ends = [[], []]
    for part in range(2):
        y = entering[0][part] + pre * sy[part]
        for i in range(ROWS):
            y = factors[0, i] * y - factors[1, i] * rhs(i, part)
            ends[part].append(y)
    for part in range(2):
        ref = uim if part else ure
        z_in = entering[1][part] + post * sz[part]
        x = (factors[2, ROWS - 1] * z_in + ends[part][-1]) * scale
        for i in range(ROWS - 1, -1, -1):
            if i < ROWS - 1:
                x = factors[2, i] * x + ends[part][i]
            ref[i * RADIX : (i + 1) * RADIX, :] = x

    both = jnp.concatenate([uim[...], ure[...]], axis=1)
    back = product(both, matrix[...])
    uim[...] = back[:, :LANES]
    ure[...] = back[:, LANES:]
    values = []
    for k in range(RADIX):
        re = ure[pl.ds(k, ROWS, stride=RADIX), :]
        im = uim[pl.ds(k, ROWS, stride=RADIX), :]
        c = twiddle[k : k + 1, :] * (1.0 / NX)
        s = twiddle[RADIX + k : RADIX + k + 1, :] * (1.0 / NX)
        values.append((re * c - im * s, im * c + re * s))
    values = butterflies(values, True)
    for a in range(RADIX):
        at = (a % 2) * 32
        obuf[a // 2, at : at + ROWS, :] = values[a][0]
        obuf[a // 2, at + ROWS : at + 2 * ROWS, :] = values[a][1]
    backward = [remote(obuf.at[q], fbuf.at[gx], send_sem.at[5], recv_sem.at[3], at_gx(q)) for q in gx_peers]
    for copy in backward:
        copy.start()
    own = pltpu.make_async_copy(obuf.at[gx], fbuf.at[gx], load_sem.at[0])
    own.start()
    wait_for(sbuf.at[pl.ds(0, PLANES - 1)], send_sem.at[0])
    wait_for(coef.at[pl.ds(0, NXP - 1)], send_sem.at[1])
    wait_for(coef.at[pl.ds(0, NXP * (NZ - 1))], send_sem.at[2])
    wait_for(raw.at[pl.ds(0, NXP - 1)], send_sem.at[3])
    wait_for(zrecv.at[pl.ds(0, NZ - 1)], send_sem.at[4])
    own.wait()
    wait_for(obuf.at[pl.ds(0, PLANES - 1)], send_sem.at[5])
    wait_for(fbuf.at[pl.ds(0, PLANES - 1)], recv_sem.at[3])


def assemble(fbuf, out):
    for q in range(PLANES):
        for xt in range(2):
            for part in range(2):
                at = (xt * 2 + part) * ROWS
                out[pl.ds((part * 2 + xt) * PLANES + q, ROWS, stride=4 * PLANES), :] = fbuf[q, at : at + ROWS, :]


def local(source, lower, upper, span):
    matrix, twiddle = transform_constants()
    f32 = jnp.float32
    dma = pltpu.SemaphoreType.DMA
    vmem = lambda *shape: pltpu.VMEM(shape, f32)
    smem = lambda *shape: pltpu.SMEM(shape, f32)
    any_spec = pl.BlockSpec(memory_space=pl.ANY)
    shape = source.shape
    source = source.reshape(ROWS, 2, PLANES, 2, LANES).transpose(0, 1, 3, 2, 4).reshape(4 * ROWS * PLANES, LANES)
    planes = pl.pallas_call(
        kernel,
        out_shape=jax.ShapeDtypeStruct((PLANES, 64, LANES), f32),
        in_specs=[pl.BlockSpec(memory_space=pltpu.HBM)] * 6,
        out_specs=any_spec,
        scratch_shapes=[
            vmem(4 * ROWS * PLANES, LANES), vmem(PLANES, 64, LANES), vmem(PLANES, 64, LANES),
            vmem(256, LANES), vmem(256, LANES), vmem(256, 256),
            pltpu.VMEM((6 * 256, 256), jnp.bfloat16), vmem(2 * RADIX, LANES),
            smem(ROWS), smem(ROWS), smem(PLANES),
            vmem(BLOCKS, 1, LANES), vmem(2, BLOCKS, 5, RADIX, LANES), vmem(2, BLOCKS, RADIX, LANES),
            vmem(BLOCKS, RADIX, LANES), vmem(2, RADIX, LANES), vmem(2, NXP, RADIX, LANES), vmem(4, 4, RADIX, LANES),
            vmem(4, ROWS, RADIX, LANES), vmem(3, ROWS, RADIX, LANES),
            vmem(NXP, 64, LANES), vmem(2, 32, LANES), vmem(NZ, 32, LANES), vmem(PLANES, 64, LANES),
            dma((6,)), dma((6,)), dma((4,)), dma((NXP,)), dma((NZ,)),
            pltpu.SemaphoreType.REGULAR, pltpu.SemaphoreType.REGULAR,
        ],
        compiler_params=pltpu.CompilerParams(
            collective_id=0, has_side_effects=True, vmem_limit_bytes=16 * 1024 * 1024),
    )(*[pltpu.with_memory_space_constraint(x, pltpu.HBM)
        for x in (source, lower, upper, span, jnp.asarray(matrix), jnp.asarray(twiddle))])
    result = pl.pallas_call(
        assemble,
        out_shape=jax.ShapeDtypeStruct((ROWS * 4 * PLANES, LANES), f32),
        in_specs=[pl.BlockSpec(memory_space=pltpu.VMEM)],
        out_specs=pl.BlockSpec(memory_space=pltpu.VMEM),
        compiler_params=pltpu.CompilerParams(vmem_limit_bytes=4 * 1024 * 1024),
    )(planes)
    result = result.reshape(ROWS, 2, 2, PLANES, LANES)
    return result.transpose(0, 1, 3, 2, 4).reshape(shape)


def solution(mesh):
    in_specs = (P("gy", None, None, "gx"), P("gy"), P("gy"), P())
    out_specs = P("gy", None, None, "gx")
    return jax.shard_map(local, mesh=mesh, in_specs=in_specs, out_specs=out_specs, check_vma=False)
```

```python
import math

import jax
import jax.numpy as jnp
import ml_dtypes
import numpy as np
from jax import lax
from jax.experimental import pallas as pl
from jax.experimental.pallas import tpu as pltpu
from jax.sharding import PartitionSpec as P

MESH = pl.DeviceIdType.MESH

ROWS = 16
PLANES = 8
NX = 2048
LANES = 128
RADIX = 16
NZ = 8
NXP = 4
BLOCKS = NZ * NXP
HALF = RADIX // 2 + 1


def transform_constants():
    lanes = np.arange(LANES)
    angle = 2.0 * np.pi * (np.outer(lanes, lanes) % LANES) / LANES
    c, s = np.cos(angle), np.sin(angle)
    matrix = np.block([[c, -s], [s, c]]).astype(np.float32)
    terms, rest = [], matrix
    for _ in range(3):
        terms.append(rest.astype(ml_dtypes.bfloat16))
        rest = rest - terms[-1].astype(np.float32)
    matrix = np.concatenate([terms[0], terms[1], terms[2], terms[0], terms[1], terms[0]])
    twist = 2.0 * np.pi * (np.outer(np.arange(RADIX), lanes) % NX) / NX
    twiddle = np.concatenate([np.cos(twist), np.sin(twist)]).astype(np.float32)
    return matrix, twiddle


def rotated(value, index, size, inverse):
    re, im = value
    index = index % size
    if index == 0:
        return value
    if 4 * index == size:
        return (-im, re) if inverse else (im, -re)
    c = math.cos(2.0 * math.pi * index / size)
    s = math.sin(2.0 * math.pi * index / size)
    if not inverse:
        s = -s
    return (re * c - im * s, re * s + im * c)


def butterflies(values, inverse):
    size = len(values)
    if size == 1:
        return values
    even = butterflies(values[0::2], inverse)
    odd = butterflies(values[1::2], inverse)
    odd = [rotated(o, k, size, inverse) for k, o in enumerate(odd)]
    low = [(e[0] + o[0], e[1] + o[1]) for e, o in zip(even, odd)]
    high = [(e[0] - o[0], e[1] - o[1]) for e, o in zip(even, odd)]
    return low + high


def product(x, matrix):
    high = x.astype(jnp.bfloat16)
    rest = x - high.astype(jnp.float32)
    middle = rest.astype(jnp.bfloat16)
    low = (rest - middle.astype(jnp.float32)).astype(jnp.bfloat16)
    terms = jnp.concatenate([high, high, high, middle, middle, low], axis=1)
    return jnp.dot(terms, matrix, preferred_element_type=jnp.float32)


def times(x, y):
    a, b, c, d = x
    e, f, g, h = y
    return (a * e + b * g, a * f + b * h, c * e + d * g, c * f + d * h)


def scaled(x):
    r = pl.reciprocal(x[2] + x[3], approx=True)
    return tuple(v * r for v in x)


def mirrored(x):
    sub = lax.broadcasted_iota(jnp.int32, (8, LANES), 0)
    lane = lax.broadcasted_iota(jnp.int32, (8, LANES), 1)
    top = x[0:8, :]
    turned = jnp.take_along_axis(top, LANES - 1 - lane, axis=1)
    turned = jnp.take_along_axis(turned, (8 - sub) % 8, axis=0)
    return jnp.concatenate([top, jnp.where(sub == 0, x[8:16, :], turned)], axis=0)


def transposed(k):
    return pl.ds((k // 8) * 8 * ROWS + k % 8, ROWS, stride=8)


def kernel(
    source, lower_hbm, upper_hbm, span_hbm, matrix_hbm, twiddle_hbm, fbuf,
    src, sbuf, rbuf, ure, uim, spec, matrix, twiddle, lower, upper, span,
    coef, splats, kbuf, own_products, groups, abuf, wbuf, gbuf, gin, chain, alone, factors,
    raw, gz, zrecv, obuf,
    load_sem, send_sem, recv_sem, cxr_sem, czr_sem, near_sem, far_sem,
):
    gx = lax.axis_index("gx")
    gy = lax.axis_index("gy")
    zi = gy // NXP
    xi = gy % NXP
    base = zi * NXP

    chip, core = gx // 2, gx % 2
    gx_peers = [lax.rem(chip + d, PLANES // 2) * 2 + lax.rem(core + c, 2)
                for d, c in ((2, 0), (2, 1), (1, 0), (3, 0), (1, 1), (3, 1), (0, 1))]
    x_peers = [lax.rem(xi + d, NXP) for d in (2, 1, 3)]
    z_peers = [lax.rem(zi + d, NZ) for d in (4, 3, 5, 2, 6, 1, 7)]

    def at_gx(q):
        return (q, gy)

    def at_x(q):
        return (gx, base + q)

    def at_z(q):
        return (gx, q * NXP + xi)

    z_near = [lax.rem(zi + d, NZ) for d in (1, NZ - 1)]
    z_far = [lax.rem(zi + d, NZ) for d in (2, NZ - 2)]
    near = [at_z(q) for q in z_near] + [at_x(q) for q in x_peers] + [at_gx(q) for q in gx_peers]
    loads = [pltpu.make_async_copy(there, here, load_sem.at[n]) for n, (there, here) in enumerate((
        (source, src), (lower_hbm, lower), (upper_hbm, upper), (span_hbm, span),
        (twiddle_hbm, twiddle), (matrix_hbm, matrix)))]
    loads[0].start()
    barrier = pltpu.get_barrier_semaphore()
    for device in near:
        pl.semaphore_signal(barrier, inc=1, device_id=device, device_id_type=MESH)
    for load in loads[1:]:
        load.start()

    loads[0].wait()
    for q in range(PLANES):
        sbuf[q] = src[pl.ds(q, 4 * ROWS, stride=PLANES), :]

    pl.semaphore_wait(barrier, len(near))

    def remote(src_ref, dst_ref, send, recv, device):
        return pltpu.make_async_remote_copy(
            src_ref=src_ref, dst_ref=dst_ref, send_sem=send, recv_sem=recv,
            device_id=device, device_id_type=MESH)

    forward = [remote(sbuf.at[q], rbuf.at[gx], send_sem.at[0], recv_sem.at[0], at_gx(q)) for q in gx_peers]
    for copy in forward:
        copy.start()
    for q in z_near:
        pl.semaphore_signal(near_sem, inc=1, device_id=at_z(q), device_id_type=MESH)
    rbuf[gx] = sbuf[gx]

    for load in loads[1:4]:
        load.wait()
    first, last = gy == 0, gy == BLOCKS - 1
    low = [lower[i] for i in range(ROWS)]
    upp = [upper[i] for i in range(ROWS)]
    low[0] = jnp.where(first, 0.0, low[0])
    upp[-1] = jnp.where(last, 0.0, upp[-1])
    sums, lost = [], []
    for l, u in zip(low, upp):
        total = l + u
        rest = total - l
        sums.append(total)
        lost.append(-((l - (total - rest)) + (u - rest)))
    lane = lax.broadcasted_iota(jnp.int32, (1, LANES), 1)
    row = jnp.zeros((1, LANES), jnp.float32)
    for i, value in enumerate(low + upp + sums + lost + upp[::-1] + low[::-1] + sums[::-1] + lost[::-1]):
        row = jnp.where(lane == i, value, row)
    coef[gy] = row

    coef_x = [remote(coef.at[gy], coef.at[gy], send_sem.at[1], cxr_sem.at[xi], at_x(q)) for q in x_peers]
    for copy in coef_x:
        copy.start()

    k1 = lax.broadcasted_iota(jnp.int32, (RADIX, LANES), 0)
    k2 = lax.broadcasted_iota(jnp.int32, (RADIX, LANES), 1)
    mode = k1 + RADIX * k2
    signed = jnp.where(mode < NX // 2, mode, mode - NX).astype(jnp.float32)
    wave = 2.0 * signed / NX
    kappa = span[gx] * span[gx] + wave * wave
    one = jnp.ones((RADIX, LANES), jnp.float32)

    def pivots(order, ahead, behind, g, keep, into):
        for i in order:
            l, u = ahead[i], behind[i]
            s = (((sums[i] + kappa) - sums[i]) + lost[i]) + l * g
            inv = 1.0 / (u + s)
            g = s * inv
            keep[into, i] = l * inv
            keep[into + 1, i] = inv
            if keep is factors:
                keep[into + 2, i] = u * inv
        return g

    pivots(range(ROWS), low, upp, one, alone, 0)
    pivots(range(ROWS - 1, -1, -1), upp, low, one, alone, 2)

    pl.semaphore_wait(near_sem, 2)
    for q in z_far:
        pl.semaphore_signal(far_sem, inc=1, device_id=at_z(q), device_id_type=MESH)

    for q in x_peers:
        there = coef.at[base + q]
        remote(there, there, send_sem.at[1], cxr_sem.at[q], at_x(q)).wait_recv()
    pl.semaphore_wait(far_sem, 2)
    group = coef.at[pl.ds(base, NXP)]
    coef_z = [remote(group, group, send_sem.at[2], czr_sem.at[zi], at_z(q)) for q in z_peers]
    for copy in coef_z:
        copy.start()

    kbuf[...] = kappa

    def block_products(blocks, ways, finish):
        rows = jnp.concatenate([coef[t] for t in blocks], axis=0)
        sub = lax.broadcasted_iota(jnp.int32, (8, LANES), 0)
        turn = jnp.where(sub < NXP, ways[0], ways[1]) == 1
        rows = jnp.where(turn, pltpu.roll(rows, LANES // 2, 1), rows)
        scale = None
        for k in range(4 * ROWS):
            one = jnp.broadcast_to(rows[:, k : k + 1], (8, LANES))
            splats[k] = one
            if k < ROWS:
                scale = one if scale is None else scale * one
        for k in range(0, HALF, 3):
            waves = [jnp.broadcast_to(kbuf[n : n + 1, :], (8, LANES)) for n in range(k, k + 3)]
            state = [None] * 3
            for i in range(ROWS):
                l, u, total, gained = [splats[n * ROWS + i] for n in range(4)]
                for n in range(3):
                    rounded = ((total + waves[n]) - total) + gained
                    if i == 0:
                        state[n] = (l, rounded, l, u + rounded)
                        continue
                    a, b, c, d = state[n]
                    a = l * a + rounded * c
                    b = l * b + rounded * d
                    state[n] = (a, b, a + u * c, b + u * d)
            for n in range(3):
                finish(k + n, scaled(state[n] + (scale,)))

    def keep_own(k, values):
        for n, v in enumerate(values):
            own_products[n, 8 * k : 8 * k + 8, :] = v

    block_products([base + j for j in range(NXP)] * 2, (0, 1), keep_own)

    def wait_for(ref, sem):
        pltpu.make_async_copy(ref, ref, sem).wait()

    wait_for(rbuf.at[pl.ds(0, PLANES - 1)], recv_sem.at[0])
    loads[4].wait()
    loads[5].wait()
    values = []
    for a in range(RADIX):
        values.append(tuple(rbuf[a // 2, pl.ds(2 * part + a % 2, ROWS, stride=4), :] for part in range(2)))
    values = butterflies(values, False)
    for k in range(RADIX):
        re, im = values[k]
        c, s = twiddle[k : k + 1, :], twiddle[RADIX + k : RADIX + k + 1, :]
        ure[transposed(k), :] = re * c + im * s
        uim[transposed(k), :] = im * c - re * s
    both = jnp.concatenate([ure[...], uim[...]], axis=1)
    spec[...] = product(both, matrix[...])

    def rhs(i, part):
        lanes = slice(part * LANES, (part + 1) * LANES)
        return jnp.concatenate([spec[h * 128 + i * 8 : h * 128 + i * 8 + 8, lanes] for h in range(2)], axis=0)

    for way, order in enumerate((range(ROWS), range(ROWS - 1, -1, -1))):
        for part in range(2):
            y = None
            for i in order:
                r = rhs(i, part) * alone[2 * way + 1, i]
                y = -r if y is None else alone[2 * way, i] * y - r
            raw[xi, (2 * way + part) * RADIX : (2 * way + part + 1) * RADIX, :] = y
    to_x = [remote(raw.at[xi], raw.at[xi], send_sem.at[3], recv_sem.at[1], at_x(q)) for q in x_peers]
    for copy in to_x:
        copy.start()

    for slot in range(4):
        for k in range(4):
            chain[slot, k] = jnp.zeros_like(one) if k in (1, 2) else one

    def next_block(x, shift):
        return tuple(pltpu.roll(v, 8 - shift, 0) for v in x)

    @pl.loop(0, NZ // 2)
    def _(n):
        pair = (lax.rem(zi + n + 1, NZ), lax.rem(zi + NZ - 1 - n, NZ))
        ways = [(q > zi).astype(jnp.int32) for q in pair]

        def arrive(q):
            there = coef.at[pl.ds(q * NXP, NXP)]
            remote(there, there, send_sem.at[2], czr_sem.at[q], at_z(q)).wait_recv()

        arrive(pair[0])

        @pl.when(n < NZ // 2 - 1)
        def _():
            arrive(pair[1])

        def keep_groups(k, values):
            for shift in (1, 2):
                later = next_block(values, shift)
                values = times(later[:4], values[:4]) + (later[4] * values[4],)
            values = scaled(values)
            for m, v in enumerate(values):
                for g in range(2):
                    groups[pair[g], m, k : k + 1, :] = v[NXP * g : NXP * g + 1, :]

        blocks = [q * NXP + jnp.where(w == 0, j, NXP - 1 - j) for q, w in zip(pair, ways) for j in range(NXP)]
        block_products(blocks, ways, keep_groups)

        def join(g):
            far = ways[g] != 1 - g
            slot = ways[g] + 2 * far.astype(jnp.int32)
            whole = tuple(groups[pair[g], k] for k in range(4))
            old = tuple(chain[slot, k] for k in range(4))
            outer = tuple(jnp.where(far, w, o) for w, o in zip(whole, old))
            inner = tuple(jnp.where(far, o, w) for w, o in zip(whole, old))
            for k, v in enumerate(scaled(times(outer, inner))):
                chain[slot, k] = v

        join(0)

        @pl.when(n < NZ // 2 - 1)
        def _():
            join(1)

    enter = []
    for way in range(2):
        top, bottom = chain[way + 2, 1], chain[way + 2, 3]
        enter.append((chain[way, 0] * top + chain[way, 1] * bottom) / (chain[way, 2] * top + chain[way, 3] * bottom))
    for j in range(NXP):
        for way in range(2):
            t = j if way == 0 else NXP - 1 - j
            g = enter[way]
            a, b, c, d, scale = [own_products[n, pl.ds(NXP * way + t, RADIX, stride=8), :] for n in range(5)]
            inv = 1.0 / (c * g + d)
            gin[way, t] = mirrored(g)
            abuf[way, t] = mirrored(scale * inv)
            enter[way] = (a * g + b) * inv

    wait_for(raw.at[pl.ds(0, NXP - 1)], recv_sem.at[1])
    entering = []
    for way, order in enumerate((range(NXP), range(NXP - 1, -1, -1))):
        run, mine = [jnp.zeros_like(one)] * 2, [jnp.zeros_like(one)] * 2
        for j in order:
            here = xi == j
            a = abuf[way, j]
            ae = a * (1.0 - gin[way, j])
            for part in range(2):
                end = raw[j, (2 * way + part) * RADIX : (2 * way + part + 1) * RADIX, :]
                start = raw[j, (2 - 2 * way + part) * RADIX : (3 - 2 * way + part) * RADIX, :]
                mine[part] = jnp.where(here, run[part], mine[part])
                run[part] = a * run[part] + (end + ae * start)
        for part in range(2):
            gz[way, part * RADIX : (part + 1) * RADIX, :] = run[part]
        entering.append(mine)

    to_z = []
    for q in z_peers:
        which = jnp.where(q > zi, 0, 1)
        to_z.append(remote(gz.at[which], zrecv.at[zi], send_sem.at[4], recv_sem.at[2], at_z(q)))
    for copy in to_z:
        copy.start()

    gbuf[...] = jnp.zeros_like(gbuf)

    @pl.loop(0, NZ - 1)
    def _(n):
        way = (n >= zi).astype(jnp.int32)
        q = jnp.where(n < zi, n, NZ - 1 - (n - zi))
        g = gbuf[way]
        inv = 1.0 / (groups[q, 2] * g + groups[q, 3])
        gbuf[way] = (groups[q, 0] * g + groups[q, 1]) * inv
        wbuf[q] = groups[q, 4] * inv

    def below(n, run):
        q = zi - 1 - n
        a = wbuf[q]
        wbuf[q] = mirrored(run)
        return run * a

    lax.fori_loop(0, zi, below, one)

    def above(n, run):
        q = zi + 1 + n
        a = wbuf[q]
        wbuf[q] = mirrored(run)
        return run * a

    lax.fori_loop(0, NZ - 1 - zi, above, one)
    pre, post = one, one
    for j in range(NXP):
        pre = pre * jnp.where(j < xi, abuf[0, j], 1.0)
        post = post * jnp.where(j > xi, abuf[1, j], 1.0)

    g_end = pivots(range(ROWS), low, upp, gin[0, xi], factors, 0)
    h_in = gin[1, xi]
    scale = 1.0 / (g_end + h_in * factors[2, ROWS - 1])

    sy = [jnp.zeros_like(one)] * 2
    sz = [jnp.zeros_like(one)] * 2
    wait_for(zrecv.at[pl.ds(0, NZ - 1)], recv_sem.at[2])
    for q in z_peers:
        lower_side = q < zi
        w = wbuf[q]
        wy = jnp.where(lower_side, w, 0.0)
        wz = jnp.where(lower_side, 0.0, w)
        for part in range(2):
            v = zrecv[q, part * RADIX : (part + 1) * RADIX, :]
            sy[part] = sy[part] + wy * v
            sz[part] = sz[part] + wz * v

    ends = [[], []]
    for part in range(2):
        y = entering[0][part] + pre * sy[part]
        for i in range(ROWS):
            y = factors[0, i] * y - factors[1, i] * rhs(i, part)
            ends[part].append(y)
    for part in range(2):
        ref = uim if part else ure
        z_in = entering[1][part] + post * sz[part]
        x = (factors[2, ROWS - 1] * z_in + ends[part][-1]) * scale
        for i in range(ROWS - 1, -1, -1):
            if i < ROWS - 1:
                x = factors[2, i] * x + ends[part][i]
            for h in range(2):
                ref[h * 128 + i * 8 : h * 128 + i * 8 + 8, :] = x[8 * h : 8 * h + 8, :]

    both = jnp.concatenate([uim[...], ure[...]], axis=1)
    back = product(both, matrix[...])
    uim[...] = back[:, :LANES]
    ure[...] = back[:, LANES:]
    values = []
    for k in range(RADIX):
        re = ure[transposed(k), :]
        im = uim[transposed(k), :]
        c = twiddle[k : k + 1, :] * (1.0 / NX)
        s = twiddle[RADIX + k : RADIX + k + 1, :] * (1.0 / NX)
        values.append((re * c - im * s, im * c + re * s))
    values = butterflies(values, True)
    for a in range(RADIX):
        for part in range(2):
            obuf[a // 2, pl.ds(2 * part + a % 2, ROWS, stride=4), :] = values[a][part]
    backward = [remote(obuf.at[q], fbuf.at[gx], send_sem.at[5], recv_sem.at[3], at_gx(q)) for q in gx_peers]
    for copy in backward:
        copy.start()
    own = pltpu.make_async_copy(obuf.at[gx], fbuf.at[gx], load_sem.at[0])
    own.start()
    wait_for(sbuf.at[pl.ds(0, PLANES - 1)], send_sem.at[0])
    wait_for(coef.at[pl.ds(0, NXP - 1)], send_sem.at[1])
    wait_for(coef.at[pl.ds(0, NXP * (NZ - 1))], send_sem.at[2])
    wait_for(raw.at[pl.ds(0, NXP - 1)], send_sem.at[3])
    wait_for(zrecv.at[pl.ds(0, NZ - 1)], send_sem.at[4])
    own.wait()
    wait_for(obuf.at[pl.ds(0, PLANES - 1)], send_sem.at[5])
    wait_for(fbuf.at[pl.ds(0, PLANES - 1)], recv_sem.at[3])


def assemble(fbuf, out):
    for q in range(PLANES):
        out[pl.ds(q, 4 * ROWS, stride=PLANES), :] = fbuf[q]


def local(source, lower, upper, span):
    matrix, twiddle = transform_constants()
    f32 = jnp.float32
    dma = pltpu.SemaphoreType.DMA
    vmem = lambda *shape: pltpu.VMEM(shape, f32)
    smem = lambda *shape: pltpu.SMEM(shape, f32)
    any_spec = pl.BlockSpec(memory_space=pl.ANY)
    shape = source.shape
    source = source.reshape(ROWS, 2, PLANES, 2, LANES).transpose(0, 1, 3, 2, 4).reshape(4 * ROWS * PLANES, LANES)
    planes = pl.pallas_call(
        kernel,
        out_shape=jax.ShapeDtypeStruct((PLANES, 64, LANES), f32),
        in_specs=[pl.BlockSpec(memory_space=pltpu.HBM)] * 6,
        out_specs=any_spec,
        scratch_shapes=[
            vmem(4 * ROWS * PLANES, LANES), vmem(PLANES, 64, LANES), vmem(PLANES, 64, LANES),
            vmem(256, LANES), vmem(256, LANES), vmem(256, 256),
            pltpu.VMEM((6 * 256, 256), jnp.bfloat16), vmem(2 * RADIX, LANES),
            smem(ROWS), smem(ROWS), smem(PLANES),
            vmem(BLOCKS, 1, LANES), vmem(4 * ROWS, 8, LANES), vmem(RADIX, LANES), vmem(5, 8 * RADIX, LANES),
            vmem(NZ, 5, RADIX, LANES), vmem(2, NXP, RADIX, LANES), vmem(NZ, RADIX, LANES),
            vmem(2, RADIX, LANES), vmem(2, NXP, RADIX, LANES), vmem(4, 4, RADIX, LANES),
            vmem(4, ROWS, RADIX, LANES), vmem(3, ROWS, RADIX, LANES),
            vmem(NXP, 64, LANES), vmem(2, 32, LANES), vmem(NZ, 32, LANES), vmem(PLANES, 64, LANES),
            dma((6,)), dma((6,)), dma((4,)), dma((NXP,)), dma((NZ,)),
            pltpu.SemaphoreType.REGULAR, pltpu.SemaphoreType.REGULAR,
        ],
        compiler_params=pltpu.CompilerParams(
            collective_id=0, has_side_effects=True, vmem_limit_bytes=16 * 1024 * 1024),
    )(*[pltpu.with_memory_space_constraint(x, pltpu.HBM)
        for x in (source, lower, upper, span, jnp.asarray(matrix), jnp.asarray(twiddle))])
    result = pl.pallas_call(
        assemble,
        out_shape=jax.ShapeDtypeStruct((ROWS * 4 * PLANES, LANES), f32),
        in_specs=[pl.BlockSpec(memory_space=pltpu.VMEM)],
        out_specs=pl.BlockSpec(memory_space=pltpu.VMEM),
        compiler_params=pltpu.CompilerParams(vmem_limit_bytes=4 * 1024 * 1024),
    )(planes)
    result = result.reshape(ROWS, 2, 2, PLANES, LANES)
    return result.transpose(0, 1, 3, 2, 4).reshape(shape)


def solution(mesh):
    in_specs = (P("gy", None, None, "gx"), P("gy"), P("gy"), P())
    out_specs = P("gy", None, None, "gx")
    return jax.shard_map(local, mesh=mesh, in_specs=in_specs, out_specs=out_specs, check_vma=False)
```

```python
import math

import jax
import jax.numpy as jnp
import ml_dtypes
import numpy as np
from jax import lax
from jax.experimental import pallas as pl
from jax.experimental.pallas import tpu as pltpu
from jax.sharding import PartitionSpec as P

MESH = pl.DeviceIdType.MESH

ROWS = 16
PLANES = 8
NX = 2048
LANES = 128
RADIX = 16
NZ = 8
NXP = 4
BLOCKS = NZ * NXP
HALF = RADIX // 2 + 1


def transform_constants():
    lanes = np.arange(LANES)
    angle = 2.0 * np.pi * (np.outer(lanes, lanes) % LANES) / LANES
    c, s = np.cos(angle), np.sin(angle)
    matrix = np.block([[c, -s], [s, c]]).astype(np.float32)
    terms, rest = [], matrix
    for _ in range(3):
        terms.append(rest.astype(ml_dtypes.bfloat16))
        rest = rest - terms[-1].astype(np.float32)
    matrix = np.concatenate([terms[0], terms[1], terms[2], terms[0], terms[1], terms[0]])
    twist = 2.0 * np.pi * (np.outer(np.arange(RADIX), lanes) % NX) / NX
    twiddle = np.concatenate([np.cos(twist), np.sin(twist)]).astype(np.float32)
    return matrix, twiddle


def rotated(value, index, size, inverse):
    re, im = value
    index = index % size
    if index == 0:
        return value
    if 4 * index == size:
        return (-im, re) if inverse else (im, -re)
    c = math.cos(2.0 * math.pi * index / size)
    s = math.sin(2.0 * math.pi * index / size)
    if not inverse:
        s = -s
    return (re * c - im * s, re * s + im * c)


def butterflies(values, inverse):
    size = len(values)
    if size == 1:
        return values
    even = butterflies(values[0::2], inverse)
    odd = butterflies(values[1::2], inverse)
    odd = [rotated(o, k, size, inverse) for k, o in enumerate(odd)]
    low = [(e[0] + o[0], e[1] + o[1]) for e, o in zip(even, odd)]
    high = [(e[0] - o[0], e[1] - o[1]) for e, o in zip(even, odd)]
    return low + high


def product(x, matrix):
    high = x.astype(jnp.bfloat16)
    rest = x - high.astype(jnp.float32)
    middle = rest.astype(jnp.bfloat16)
    low = (rest - middle.astype(jnp.float32)).astype(jnp.bfloat16)
    terms = jnp.concatenate([high, high, high, middle, middle, low], axis=1)
    return jnp.dot(terms, matrix, preferred_element_type=jnp.float32)


def times(x, y):
    a, b, c, d = x
    e, f, g, h = y
    return (a * e + b * g, a * f + b * h, c * e + d * g, c * f + d * h)


def scaled(x):
    r = pl.reciprocal(x[2] + x[3], approx=True)
    return tuple(v * r for v in x)


def mirrored(x):
    sub = lax.broadcasted_iota(jnp.int32, (8, LANES), 0)
    lane = lax.broadcasted_iota(jnp.int32, (8, LANES), 1)
    top = x[0:8, :]
    turned = jnp.take_along_axis(top, LANES - 1 - lane, axis=1)
    turned = jnp.take_along_axis(turned, (8 - sub) % 8, axis=0)
    return jnp.concatenate([top, jnp.where(sub == 0, x[8:16, :], turned)], axis=0)


def transposed(o, k):
    return pl.ds(o * 128 + (k // 8) * 64 + k % 8, 8, stride=8)


def kernel(
    source, lower_hbm, upper_hbm, span_hbm, matrix_hbm, twiddle_hbm, fbuf,
    src, sbuf, rbuf, ure, uim, spec, matrix, twiddle, lower, upper, span,
    coef, splats, kbuf, own_products, groups, abuf, wbuf, gbuf, gin, chain, alone, factors,
    raw, gz, zrecv, obuf,
    load_sem, send_sem, recv_sem, arrived, cxr_sem, czr_sem, near_sem, far_sem,
):
    gx = lax.axis_index("gx")
    gy = lax.axis_index("gy")
    zi = gy // NXP
    xi = gy % NXP
    base = zi * NXP

    chip, core = gx // 2, gx % 2
    gx_peers = [lax.rem(chip + d, PLANES // 2) * 2 + lax.rem(core + c, 2)
                for d, c in ((2, 0), (2, 1), (1, 0), (3, 0), (1, 1), (3, 1), (0, 1))]
    x_peers = [lax.rem(xi + d, NXP) for d in (2, 1, 3)]
    z_peers = [lax.rem(zi + d, NZ) for d in (4, 3, 5, 2, 6, 1, 7)]

    def at_gx(q):
        return (q, gy)

    def at_x(q):
        return (gx, base + q)

    def at_z(q):
        return (gx, q * NXP + xi)

    z_near = [lax.rem(zi + d, NZ) for d in (1, NZ - 1)]
    z_far = [lax.rem(zi + d, NZ) for d in (2, NZ - 2)]
    near = [at_z(q) for q in z_near] + [at_x(q) for q in x_peers] + [at_gx(q) for q in gx_peers]
    loads = [pltpu.make_async_copy(there, here, load_sem.at[n]) for n, (there, here) in enumerate((
        (source, src), (lower_hbm, lower), (upper_hbm, upper), (span_hbm, span),
        (twiddle_hbm, twiddle), (matrix_hbm, matrix)))]
    loads[0].start()
    barrier = pltpu.get_barrier_semaphore()
    for device in near:
        pl.semaphore_signal(barrier, inc=1, device_id=device, device_id_type=MESH)
    for load in loads[1:]:
        load.start()

    loads[0].wait()
    for q in range(PLANES):
        sbuf[q] = src[pl.ds(q, 4 * ROWS, stride=PLANES), :]

    pl.semaphore_wait(barrier, len(near))

    def remote(src_ref, dst_ref, send, recv, device):
        return pltpu.make_async_remote_copy(
            src_ref=src_ref, dst_ref=dst_ref, send_sem=send, recv_sem=recv,
            device_id=device, device_id_type=MESH)

    def octet(ref, q, o):
        return ref.at[q, pl.ds(32 * o, 32)]

    for o in range(2):
        for q in gx_peers:
            remote(octet(sbuf, q, o), octet(rbuf, gx, o), send_sem.at[0], arrived.at[o], at_gx(q)).start()
    for q in z_near:
        pl.semaphore_signal(near_sem, inc=1, device_id=at_z(q), device_id_type=MESH)
    rbuf[gx] = sbuf[gx]

    for load in loads[1:4]:
        load.wait()
    first, last = gy == 0, gy == BLOCKS - 1
    low = [lower[i] for i in range(ROWS)]
    upp = [upper[i] for i in range(ROWS)]
    low[0] = jnp.where(first, 0.0, low[0])
    upp[-1] = jnp.where(last, 0.0, upp[-1])
    sums, lost = [], []
    for l, u in zip(low, upp):
        total = l + u
        rest = total - l
        sums.append(total)
        lost.append(-((l - (total - rest)) + (u - rest)))
    lane = lax.broadcasted_iota(jnp.int32, (1, LANES), 1)
    row = jnp.zeros((1, LANES), jnp.float32)
    for i, value in enumerate(low + upp + sums + lost + upp[::-1] + low[::-1] + sums[::-1] + lost[::-1]):
        row = jnp.where(lane == i, value, row)
    coef[gy] = row

    coef_x = [remote(coef.at[gy], coef.at[gy], send_sem.at[1], cxr_sem.at[xi], at_x(q)) for q in x_peers]
    for copy in coef_x:
        copy.start()

    k1 = lax.broadcasted_iota(jnp.int32, (RADIX, LANES), 0)
    k2 = lax.broadcasted_iota(jnp.int32, (RADIX, LANES), 1)
    mode = k1 + RADIX * k2
    signed = jnp.where(mode < NX // 2, mode, mode - NX).astype(jnp.float32)
    wave = 2.0 * signed / NX
    kappa = span[gx] * span[gx] + wave * wave
    one = jnp.ones((RADIX, LANES), jnp.float32)

    def pivots(order, ahead, behind, g, keep, into):
        for i in order:
            l, u = ahead[i], behind[i]
            s = (((sums[i] + kappa) - sums[i]) + lost[i]) + l * g
            inv = 1.0 / (u + s)
            g = s * inv
            keep[into, i] = l * inv
            keep[into + 1, i] = inv
            if keep is factors:
                keep[into + 2, i] = u * inv
        return g

    pivots(range(ROWS), low, upp, one, alone, 0)
    pivots(range(ROWS - 1, -1, -1), upp, low, one, alone, 2)

    pl.semaphore_wait(near_sem, 2)
    for q in z_far:
        pl.semaphore_signal(far_sem, inc=1, device_id=at_z(q), device_id_type=MESH)

    for q in x_peers:
        there = coef.at[base + q]
        remote(there, there, send_sem.at[1], cxr_sem.at[q], at_x(q)).wait_recv()
    pl.semaphore_wait(far_sem, 2)
    group = coef.at[pl.ds(base, NXP)]
    coef_z = [remote(group, group, send_sem.at[2], czr_sem.at[zi], at_z(q)) for q in z_peers]
    for copy in coef_z:
        copy.start()

    kbuf[...] = kappa

    def block_products(blocks, ways, finish):
        rows = jnp.concatenate([coef[t] for t in blocks], axis=0)
        sub = lax.broadcasted_iota(jnp.int32, (8, LANES), 0)
        turn = jnp.where(sub < NXP, ways[0], ways[1]) == 1
        rows = jnp.where(turn, pltpu.roll(rows, LANES // 2, 1), rows)
        scale = None
        for k in range(4 * ROWS):
            one = jnp.broadcast_to(rows[:, k : k + 1], (8, LANES))
            splats[k] = one
            if k < ROWS:
                scale = one if scale is None else scale * one
        for k in range(0, HALF, 3):
            waves = [jnp.broadcast_to(kbuf[n : n + 1, :], (8, LANES)) for n in range(k, k + 3)]
            state = [None] * 3
            for i in range(ROWS):
                l, u, total, gained = [splats[n * ROWS + i] for n in range(4)]
                for n in range(3):
                    rounded = ((total + waves[n]) - total) + gained
                    if i == 0:
                        state[n] = (l, rounded, l, u + rounded)
                        continue
                    a, b, c, d = state[n]
                    a = l * a + rounded * c
                    b = l * b + rounded * d
                    state[n] = (a, b, a + u * c, b + u * d)
            for n in range(3):
                finish(k + n, scaled(state[n] + (scale,)))

    def keep_own(k, values):
        for n, v in enumerate(values):
            own_products[n, 8 * k : 8 * k + 8, :] = v

    block_products([base + j for j in range(NXP)] * 2, (0, 1), keep_own)

    def wait_for(ref, sem):
        pltpu.make_async_copy(ref, ref, sem).wait()

    def wait_for_octet(ref, sem):
        wait_for(ref.at[pl.ds(0, PLANES - 1), pl.ds(0, 32)], sem)

    for o in range(2):
        wait_for_octet(rbuf, arrived.at[o])
        if o == 0:
            loads[4].wait()
            loads[5].wait()
        values = []
        for a in range(RADIX):
            values.append(tuple(rbuf[a // 2, pl.ds(32 * o + 2 * part + a % 2, 8, stride=4), :] for part in range(2)))
        values = butterflies(values, False)
        for k in range(RADIX):
            re, im = values[k]
            c, s = twiddle[k : k + 1, :], twiddle[RADIX + k : RADIX + k + 1, :]
            ure[transposed(o, k), :] = re * c + im * s
            uim[transposed(o, k), :] = im * c - re * s
        rows = slice(128 * o, 128 * o + 128)
        spec[rows, :] = product(jnp.concatenate([ure[rows, :], uim[rows, :]], axis=1), matrix[...])

    def rhs(i, part):
        lanes = slice(part * LANES, (part + 1) * LANES)
        at = [(i // 8) * 128 + h * 64 + (i % 8) * 8 for h in range(2)]
        return jnp.concatenate([spec[n : n + 8, lanes] for n in at], axis=0)

    for way, order in enumerate((range(ROWS), range(ROWS - 1, -1, -1))):
        for part in range(2):
            y = None
            for i in order:
                r = rhs(i, part) * alone[2 * way + 1, i]
                y = -r if y is None else alone[2 * way, i] * y - r
            raw[xi, (2 * way + part) * RADIX : (2 * way + part + 1) * RADIX, :] = y
    to_x = [remote(raw.at[xi], raw.at[xi], send_sem.at[3], recv_sem.at[0], at_x(q)) for q in x_peers]
    for copy in to_x:
        copy.start()

    for slot in range(4):
        for k in range(4):
            chain[slot, k] = jnp.zeros_like(one) if k in (1, 2) else one

    def next_block(x, shift):
        return tuple(pltpu.roll(v, 8 - shift, 0) for v in x)

    @pl.loop(0, NZ // 2)
    def _(n):
        pair = (lax.rem(zi + n + 1, NZ), lax.rem(zi + NZ - 1 - n, NZ))
        ways = [(q > zi).astype(jnp.int32) for q in pair]

        def arrive(q):
            there = coef.at[pl.ds(q * NXP, NXP)]
            remote(there, there, send_sem.at[2], czr_sem.at[q], at_z(q)).wait_recv()

        arrive(pair[0])

        @pl.when(n < NZ // 2 - 1)
        def _():
            arrive(pair[1])

        def keep_groups(k, values):
            for shift in (1, 2):
                later = next_block(values, shift)
                values = times(later[:4], values[:4]) + (later[4] * values[4],)
            values = scaled(values)
            for m, v in enumerate(values):
                for g in range(2):
                    groups[pair[g], m, k : k + 1, :] = v[NXP * g : NXP * g + 1, :]

        blocks = [q * NXP + jnp.where(w == 0, j, NXP - 1 - j) for q, w in zip(pair, ways) for j in range(NXP)]
        block_products(blocks, ways, keep_groups)

        def join(g):
            far = ways[g] != 1 - g
            slot = ways[g] + 2 * far.astype(jnp.int32)
            whole = tuple(groups[pair[g], k] for k in range(4))
            old = tuple(chain[slot, k] for k in range(4))
            outer = tuple(jnp.where(far, w, o) for w, o in zip(whole, old))
            inner = tuple(jnp.where(far, o, w) for w, o in zip(whole, old))
            for k, v in enumerate(scaled(times(outer, inner))):
                chain[slot, k] = v

        join(0)

        @pl.when(n < NZ // 2 - 1)
        def _():
            join(1)

    enter = []
    for way in range(2):
        top, bottom = chain[way + 2, 1], chain[way + 2, 3]
        enter.append((chain[way, 0] * top + chain[way, 1] * bottom) / (chain[way, 2] * top + chain[way, 3] * bottom))
    for j in range(NXP):
        for way in range(2):
            t = j if way == 0 else NXP - 1 - j
            g = enter[way]
            a, b, c, d, scale = [own_products[n, pl.ds(NXP * way + t, RADIX, stride=8), :] for n in range(5)]
            inv = 1.0 / (c * g + d)
            gin[way, t] = mirrored(g)
            abuf[way, t] = mirrored(scale * inv)
            enter[way] = (a * g + b) * inv

    wait_for(raw.at[pl.ds(0, NXP - 1)], recv_sem.at[0])
    entering = []
    for way, order in enumerate((range(NXP), range(NXP - 1, -1, -1))):
        run, mine = [jnp.zeros_like(one)] * 2, [jnp.zeros_like(one)] * 2
        for j in order:
            here = xi == j
            a = abuf[way, j]
            ae = a * (1.0 - gin[way, j])
            for part in range(2):
                end = raw[j, (2 * way + part) * RADIX : (2 * way + part + 1) * RADIX, :]
                start = raw[j, (2 - 2 * way + part) * RADIX : (3 - 2 * way + part) * RADIX, :]
                mine[part] = jnp.where(here, run[part], mine[part])
                run[part] = a * run[part] + (end + ae * start)
        for part in range(2):
            gz[way, part * RADIX : (part + 1) * RADIX, :] = run[part]
        entering.append(mine)

    to_z = []
    for q in z_peers:
        which = jnp.where(q > zi, 0, 1)
        to_z.append(remote(gz.at[which], zrecv.at[zi], send_sem.at[4], recv_sem.at[1], at_z(q)))
    for copy in to_z:
        copy.start()

    gbuf[...] = jnp.zeros_like(gbuf)

    @pl.loop(0, NZ - 1)
    def _(n):
        way = (n >= zi).astype(jnp.int32)
        q = jnp.where(n < zi, n, NZ - 1 - (n - zi))
        g = gbuf[way]
        inv = 1.0 / (groups[q, 2] * g + groups[q, 3])
        gbuf[way] = (groups[q, 0] * g + groups[q, 1]) * inv
        wbuf[q] = groups[q, 4] * inv

    def below(n, run):
        q = zi - 1 - n
        a = wbuf[q]
        wbuf[q] = mirrored(run)
        return run * a

    lax.fori_loop(0, zi, below, one)

    def above(n, run):
        q = zi + 1 + n
        a = wbuf[q]
        wbuf[q] = mirrored(run)
        return run * a

    lax.fori_loop(0, NZ - 1 - zi, above, one)
    pre, post = one, one
    for j in range(NXP):
        pre = pre * jnp.where(j < xi, abuf[0, j], 1.0)
        post = post * jnp.where(j > xi, abuf[1, j], 1.0)

    g_end = pivots(range(ROWS), low, upp, gin[0, xi], factors, 0)
    h_in = gin[1, xi]
    scale = 1.0 / (g_end + h_in * factors[2, ROWS - 1])

    sy = [jnp.zeros_like(one)] * 2
    sz = [jnp.zeros_like(one)] * 2
    wait_for(zrecv.at[pl.ds(0, NZ - 1)], recv_sem.at[1])
    for q in z_peers:
        lower_side = q < zi
        w = wbuf[q]
        wy = jnp.where(lower_side, w, 0.0)
        wz = jnp.where(lower_side, 0.0, w)
        for part in range(2):
            v = zrecv[q, part * RADIX : (part + 1) * RADIX, :]
            sy[part] = sy[part] + wy * v
            sz[part] = sz[part] + wz * v

    ends = [[], []]
    for part in range(2):
        y = entering[0][part] + pre * sy[part]
        for i in range(ROWS):
            y = factors[0, i] * y - factors[1, i] * rhs(i, part)
            ends[part].append(y)
    solved = []
    for part in range(2):
        z_in = entering[1][part] + post * sz[part]
        solved.append((factors[2, ROWS - 1] * z_in + ends[part][-1]) * scale)

    for o in (1, 0):
        for i in range(8 * o + 7, 8 * o - 1, -1):
            for part, ref in enumerate((ure, uim)):
                if i < ROWS - 1:
                    solved[part] = factors[2, i] * solved[part] + ends[part][i]
                for h in range(2):
                    at = o * 128 + h * 64 + (i % 8) * 8
                    ref[at : at + 8, :] = solved[part][8 * h : 8 * h + 8, :]
        rows = slice(128 * o, 128 * o + 128)
        back = product(jnp.concatenate([uim[rows, :], ure[rows, :]], axis=1), matrix[...])
        uim[rows, :] = back[:, :LANES]
        ure[rows, :] = back[:, LANES:]
        values = []
        for k in range(RADIX):
            re = ure[transposed(o, k), :]
            im = uim[transposed(o, k), :]
            c = twiddle[k : k + 1, :] * (1.0 / NX)
            s = twiddle[RADIX + k : RADIX + k + 1, :] * (1.0 / NX)
            values.append((re * c - im * s, im * c + re * s))
        values = butterflies(values, True)
        for a in range(RADIX):
            for part in range(2):
                obuf[a // 2, pl.ds(32 * o + 2 * part + a % 2, 8, stride=4), :] = values[a][part]
        for q in gx_peers:
            remote(octet(obuf, q, o), octet(fbuf, gx, o), send_sem.at[5], arrived.at[2 + o], at_gx(q)).start()
    own = pltpu.make_async_copy(obuf.at[gx], fbuf.at[gx], load_sem.at[0])
    own.start()
    wait_for(sbuf.at[pl.ds(0, PLANES - 1)], send_sem.at[0])
    wait_for(coef.at[pl.ds(0, NXP - 1)], send_sem.at[1])
    wait_for(coef.at[pl.ds(0, NXP * (NZ - 1))], send_sem.at[2])
    wait_for(raw.at[pl.ds(0, NXP - 1)], send_sem.at[3])
    wait_for(zrecv.at[pl.ds(0, NZ - 1)], send_sem.at[4])
    own.wait()
    wait_for(obuf.at[pl.ds(0, PLANES - 1)], send_sem.at[5])
    for o in range(2):
        wait_for_octet(fbuf, arrived.at[2 + o])


def assemble(fbuf, out):
    for q in range(PLANES):
        out[pl.ds(q, 4 * ROWS, stride=PLANES), :] = fbuf[q]


def local(source, lower, upper, span):
    matrix, twiddle = transform_constants()
    f32 = jnp.float32
    dma = pltpu.SemaphoreType.DMA
    vmem = lambda *shape: pltpu.VMEM(shape, f32)
    smem = lambda *shape: pltpu.SMEM(shape, f32)
    any_spec = pl.BlockSpec(memory_space=pl.ANY)
    shape = source.shape
    source = source.reshape(ROWS, 2, PLANES, 2, LANES).transpose(0, 1, 3, 2, 4).reshape(4 * ROWS * PLANES, LANES)
    planes = pl.pallas_call(
        kernel,
        out_shape=jax.ShapeDtypeStruct((PLANES, 64, LANES), f32),
        in_specs=[pl.BlockSpec(memory_space=pltpu.HBM)] * 6,
        out_specs=any_spec,
        scratch_shapes=[
            vmem(4 * ROWS * PLANES, LANES), vmem(PLANES, 64, LANES), vmem(PLANES, 64, LANES),
            vmem(256, LANES), vmem(256, LANES), vmem(256, 256),
            pltpu.VMEM((6 * 256, 256), jnp.bfloat16), vmem(2 * RADIX, LANES),
            smem(ROWS), smem(ROWS), smem(PLANES),
            vmem(BLOCKS, 1, LANES), vmem(4 * ROWS, 8, LANES), vmem(RADIX, LANES), vmem(5, 8 * RADIX, LANES),
            vmem(NZ, 5, RADIX, LANES), vmem(2, NXP, RADIX, LANES), vmem(NZ, RADIX, LANES),
            vmem(2, RADIX, LANES), vmem(2, NXP, RADIX, LANES), vmem(4, 4, RADIX, LANES),
            vmem(4, ROWS, RADIX, LANES), vmem(3, ROWS, RADIX, LANES),
            vmem(NXP, 64, LANES), vmem(2, 32, LANES), vmem(NZ, 32, LANES), vmem(PLANES, 64, LANES),
            dma((6,)), dma((6,)), dma((2,)), dma((4,)), dma((NXP,)), dma((NZ,)),
            pltpu.SemaphoreType.REGULAR, pltpu.SemaphoreType.REGULAR,
        ],
        compiler_params=pltpu.CompilerParams(
            collective_id=0, has_side_effects=True, vmem_limit_bytes=16 * 1024 * 1024),
    )(*[pltpu.with_memory_space_constraint(x, pltpu.HBM)
        for x in (source, lower, upper, span, jnp.asarray(matrix), jnp.asarray(twiddle))])
    result = pl.pallas_call(
        assemble,
        out_shape=jax.ShapeDtypeStruct((ROWS * 4 * PLANES, LANES), f32),
        in_specs=[pl.BlockSpec(memory_space=pltpu.VMEM)],
        out_specs=pl.BlockSpec(memory_space=pltpu.VMEM),
        compiler_params=pltpu.CompilerParams(vmem_limit_bytes=4 * 1024 * 1024),
    )(planes)
    result = result.reshape(ROWS, 2, 2, PLANES, LANES)
    return result.transpose(0, 1, 3, 2, 4).reshape(shape)


def solution(mesh):
    in_specs = (P("gy", None, None, "gx"), P("gy"), P("gy"), P())
    out_specs = P("gy", None, None, "gx")
    return jax.shard_map(local, mesh=mesh, in_specs=in_specs, out_specs=out_specs, check_vma=False)
```

```python
import math

import jax
import jax.numpy as jnp
import ml_dtypes
import numpy as np
from jax import lax
from jax.experimental import pallas as pl
from jax.experimental.pallas import tpu as pltpu
from jax.sharding import PartitionSpec as P

MESH = pl.DeviceIdType.MESH

ROWS = 16
PLANES = 8
NX = 2048
LANES = 128
RADIX = 16
NZ = 8
NXP = 4
BLOCKS = NZ * NXP
HALF = RADIX // 2 + 1
PARTS = 4


def transform_constants():
    lanes = np.arange(LANES)
    angle = 2.0 * np.pi * (np.outer(lanes, lanes) % LANES) / LANES
    c, s = np.cos(angle), np.sin(angle)
    matrix = np.block([[c, -s], [s, c]]).astype(np.float32)
    terms, rest = [], matrix
    for _ in range(3):
        terms.append(rest.astype(ml_dtypes.bfloat16))
        rest = rest - terms[-1].astype(np.float32)
    matrix = np.concatenate([terms[0], terms[1], terms[2], terms[0], terms[1], terms[0]])
    twist = 2.0 * np.pi * (np.outer(np.arange(RADIX), lanes) % NX) / NX
    twiddle = np.concatenate([np.cos(twist), np.sin(twist)]).astype(np.float32)
    return matrix, twiddle


def rotated(value, index, size, inverse):
    re, im = value
    index = index % size
    if index == 0:
        return value
    if 4 * index == size:
        return (-im, re) if inverse else (im, -re)
    c = math.cos(2.0 * math.pi * index / size)
    s = math.sin(2.0 * math.pi * index / size)
    if not inverse:
        s = -s
    return (re * c - im * s, re * s + im * c)


def butterflies(values, inverse):
    size = len(values)
    if size == 1:
        return values
    even = butterflies(values[0::2], inverse)
    odd = butterflies(values[1::2], inverse)
    odd = [rotated(o, k, size, inverse) for k, o in enumerate(odd)]
    low = [(e[0] + o[0], e[1] + o[1]) for e, o in zip(even, odd)]
    high = [(e[0] - o[0], e[1] - o[1]) for e, o in zip(even, odd)]
    return low + high


def product(x, matrix):
    high = x.astype(jnp.bfloat16)
    rest = x - high.astype(jnp.float32)
    middle = rest.astype(jnp.bfloat16)
    low = (rest - middle.astype(jnp.float32)).astype(jnp.bfloat16)
    terms = jnp.concatenate([high, high, high, middle, middle, low], axis=1)
    return jnp.dot(terms, matrix, preferred_element_type=jnp.float32)


def times(x, y):
    a, b, c, d = x
    e, f, g, h = y
    return (a * e + b * g, a * f + b * h, c * e + d * g, c * f + d * h)


def scaled(x):
    r = pl.reciprocal(x[2] + x[3], approx=True)
    return tuple(v * r for v in x)


def mirrored(x):
    sub = lax.broadcasted_iota(jnp.int32, (8, LANES), 0)
    lane = lax.broadcasted_iota(jnp.int32, (8, LANES), 1)
    top = x[0:8, :]
    turned = jnp.take_along_axis(top, LANES - 1 - lane, axis=1)
    turned = jnp.take_along_axis(turned, (8 - sub) % 8, axis=0)
    return jnp.concatenate([top, jnp.where(sub == 0, x[8:16, :], turned)], axis=0)


def transposed(o, k):
    return pl.ds(o * 128 + (k // 8) * 64 + k % 8, 8, stride=8)


def kernel(
    source, lower_hbm, upper_hbm, span_hbm, matrix_hbm, twiddle_hbm, fbuf,
    src, sbuf, rbuf, ure, uim, spec, matrix, twiddle, lower, upper, span,
    coef, splats, kbuf, own_products, groups, abuf, wbuf, gbuf, gin, chain, alone, factors, known,
    raw, gz, zrecv, obuf,
    load_sem, send_sem, recv_sem, arrived, cxr_sem, czr_sem, near_sem, far_sem,
):
    gx = lax.axis_index("gx")
    gy = lax.axis_index("gy")
    zi = gy // NXP
    xi = gy % NXP
    base = zi * NXP

    chip, core = gx // 2, gx % 2
    gx_peers = [lax.rem(chip + d, PLANES // 2) * 2 + lax.rem(core + c, 2)
                for d, c in ((2, 0), (2, 1), (1, 0), (3, 0), (1, 1), (3, 1), (0, 1))]
    x_peers = [lax.rem(xi + d, NXP) for d in (2, 1, 3)]
    z_peers = [lax.rem(zi + d, NZ) for d in (4, 3, 5, 2, 6, 1, 7)]

    def at_gx(q):
        return (q, gy)

    def at_x(q):
        return (gx, base + q)

    def at_z(q):
        return (gx, q * NXP + xi)

    z_near = [lax.rem(zi + d, NZ) for d in (1, NZ - 1)]
    z_far = [lax.rem(zi + d, NZ) for d in (2, NZ - 2)]
    near = [at_z(q) for q in z_near] + [at_x(q) for q in x_peers] + [at_gx(q) for q in gx_peers]
    loads = [pltpu.make_async_copy(there, here, load_sem.at[n]) for n, (there, here) in enumerate((
        (source, src), (lower_hbm, lower), (upper_hbm, upper), (span_hbm, span),
        (twiddle_hbm, twiddle), (matrix_hbm, matrix)))]
    loads[0].start()
    barrier = pltpu.get_barrier_semaphore()
    for device in near:
        pl.semaphore_signal(barrier, inc=1, device_id=device, device_id_type=MESH)
    for load in loads[1:]:
        load.start()

    loads[0].wait()
    for q in range(PLANES):
        sbuf[q] = src[pl.ds(q, 4 * ROWS, stride=PLANES), :]

    pl.semaphore_wait(barrier, len(near))

    def remote(src_ref, dst_ref, send, recv, device):
        return pltpu.make_async_remote_copy(
            src_ref=src_ref, dst_ref=dst_ref, send_sem=send, recv_sem=recv,
            device_id=device, device_id_type=MESH)

    def octet(ref, q, o):
        return ref.at[q, pl.ds(32 * o, 32)]

    for o in range(2):
        for q in gx_peers:
            remote(octet(sbuf, q, o), octet(rbuf, gx, o), send_sem.at[0], arrived.at[o], at_gx(q)).start()
    for q in z_near:
        pl.semaphore_signal(near_sem, inc=1, device_id=at_z(q), device_id_type=MESH)
    rbuf[gx] = sbuf[gx]

    for load in loads[1:4]:
        load.wait()
    first, last = gy == 0, gy == BLOCKS - 1
    low = [lower[i] for i in range(ROWS)]
    upp = [upper[i] for i in range(ROWS)]
    low[0] = jnp.where(first, 0.0, low[0])
    upp[-1] = jnp.where(last, 0.0, upp[-1])
    sums, lost = [], []
    for l, u in zip(low, upp):
        total = l + u
        rest = total - l
        sums.append(total)
        lost.append(-((l - (total - rest)) + (u - rest)))
    lane = lax.broadcasted_iota(jnp.int32, (1, LANES), 1)
    row = jnp.zeros((1, LANES), jnp.float32)
    for i, value in enumerate(low + upp + sums + lost + upp[::-1] + low[::-1] + sums[::-1] + lost[::-1]):
        row = jnp.where(lane == i, value, row)
    coef[gy] = row

    coef_x = [remote(coef.at[gy], coef.at[gy], send_sem.at[1], cxr_sem.at[xi], at_x(q)) for q in x_peers]
    for copy in coef_x:
        copy.start()

    k1 = lax.broadcasted_iota(jnp.int32, (RADIX, LANES), 0)
    k2 = lax.broadcasted_iota(jnp.int32, (RADIX, LANES), 1)
    mode = k1 + RADIX * k2
    signed = jnp.where(mode < NX // 2, mode, mode - NX).astype(jnp.float32)
    wave = 2.0 * signed / NX
    kappa = span[gx] * span[gx] + wave * wave
    one = jnp.ones((RADIX, LANES), jnp.float32)

    def pivots(order, ahead, behind, g, keep, into):
        for i in order:
            l, u = ahead[i], behind[i]
            s = (((sums[i] + kappa) - sums[i]) + lost[i]) + l * g
            inv = 1.0 / (u + s)
            g = s * inv
            keep[into, i] = l * inv
            keep[into + 1, i] = inv
            if keep is factors:
                keep[into + 2, i] = u * inv
        return g

    pivots(range(ROWS), low, upp, one, alone, 0)
    pivots(range(ROWS - 1, -1, -1), upp, low, one, alone, 2)

    pl.semaphore_wait(near_sem, 2)
    for q in z_far:
        pl.semaphore_signal(far_sem, inc=1, device_id=at_z(q), device_id_type=MESH)

    for q in x_peers:
        there = coef.at[base + q]
        remote(there, there, send_sem.at[1], cxr_sem.at[q], at_x(q)).wait_recv()
    pl.semaphore_wait(far_sem, 2)
    group = coef.at[pl.ds(base, NXP)]
    coef_z = [remote(group, group, send_sem.at[2], czr_sem.at[zi], at_z(q)) for q in z_peers]
    for copy in coef_z:
        copy.start()

    kbuf[...] = kappa

    def block_products(blocks, ways, finish):
        rows = jnp.concatenate([coef[t] for t in blocks], axis=0)
        sub = lax.broadcasted_iota(jnp.int32, (8, LANES), 0)
        turn = jnp.where(sub < NXP, ways[0], ways[1]) == 1
        rows = jnp.where(turn, pltpu.roll(rows, LANES // 2, 1), rows)
        scale = None
        for k in range(4 * ROWS):
            one = jnp.broadcast_to(rows[:, k : k + 1], (8, LANES))
            splats[k] = one
            if k < ROWS:
                scale = one if scale is None else scale * one
        for k in range(0, HALF, 3):
            waves = [jnp.broadcast_to(kbuf[n : n + 1, :], (8, LANES)) for n in range(k, k + 3)]
            state = [None] * 3
            for i in range(ROWS):
                l, u, total, gained = [splats[n * ROWS + i] for n in range(4)]
                for n in range(3):
                    rounded = ((total + waves[n]) - total) + gained
                    if i == 0:
                        state[n] = (l, rounded, l, u + rounded)
                        continue
                    a, b, c, d = state[n]
                    a = l * a + rounded * c
                    b = l * b + rounded * d
                    state[n] = (a, b, a + u * c, b + u * d)
            for n in range(3):
                finish(k + n, scaled(state[n] + (scale,)))

    def keep_own(k, values):
        for n, v in enumerate(values):
            own_products[n, 8 * k : 8 * k + 8, :] = v

    block_products([base + j for j in range(NXP)] * 2, (0, 1), keep_own)

    def wait_for(ref, sem):
        pltpu.make_async_copy(ref, ref, sem).wait()

    def wait_for_octet(ref, sem):
        wait_for(ref.at[pl.ds(0, PLANES - 1), pl.ds(0, 32)], sem)

    for o in range(2):
        wait_for_octet(rbuf, arrived.at[o])
        if o == 0:
            loads[4].wait()
            loads[5].wait()
        values = []
        for a in range(RADIX):
            values.append(tuple(rbuf[a // 2, pl.ds(32 * o + 2 * part + a % 2, 8, stride=4), :] for part in range(2)))
        values = butterflies(values, False)
        for k in range(RADIX):
            re, im = values[k]
            c, s = twiddle[k : k + 1, :], twiddle[RADIX + k : RADIX + k + 1, :]
            ure[transposed(o, k), :] = re * c + im * s
            uim[transposed(o, k), :] = im * c - re * s
        rows = slice(128 * o, 128 * o + 128)
        spec[rows, :] = product(jnp.concatenate([ure[rows, :], uim[rows, :]], axis=1), matrix[...])

    def rhs(i, part):
        lanes = slice(part * LANES, (part + 1) * LANES)
        at = [(i // 8) * 128 + h * 64 + (i % 8) * 8 for h in range(2)]
        return jnp.concatenate([spec[n : n + 8, lanes] for n in at], axis=0)

    for way, order in enumerate((range(ROWS), range(ROWS - 1, -1, -1))):
        for part in range(2):
            y = None
            for i in order:
                r = rhs(i, part) * alone[2 * way + 1, i]
                y = -r if y is None else alone[2 * way, i] * y - r
            raw[xi, (2 * way + part) * RADIX : (2 * way + part + 1) * RADIX, :] = y
    to_x = [remote(raw.at[xi], raw.at[xi], send_sem.at[3], recv_sem.at[0], at_x(q)) for q in x_peers]
    for copy in to_x:
        copy.start()

    for slot in range(4):
        for k in range(4):
            chain[slot, k] = jnp.zeros_like(one) if k in (1, 2) else one

    def next_block(x, shift):
        return tuple(pltpu.roll(v, 8 - shift, 0) for v in x)

    @pl.loop(0, NZ // 2)
    def _(n):
        pair = (lax.rem(zi + n + 1, NZ), lax.rem(zi + NZ - 1 - n, NZ))
        ways = [(q > zi).astype(jnp.int32) for q in pair]

        def arrive(q):
            there = coef.at[pl.ds(q * NXP, NXP)]
            remote(there, there, send_sem.at[2], czr_sem.at[q], at_z(q)).wait_recv()

        arrive(pair[0])

        @pl.when(n < NZ // 2 - 1)
        def _():
            arrive(pair[1])

        def keep_groups(k, values):
            for shift in (1, 2):
                later = next_block(values, shift)
                values = times(later[:4], values[:4]) + (later[4] * values[4],)
            values = scaled(values)
            for m, v in enumerate(values):
                for g in range(2):
                    groups[pair[g], m, k : k + 1, :] = v[NXP * g : NXP * g + 1, :]

        blocks = [q * NXP + jnp.where(w == 0, j, NXP - 1 - j) for q, w in zip(pair, ways) for j in range(NXP)]
        block_products(blocks, ways, keep_groups)

        def join(g):
            far = ways[g] != 1 - g
            slot = ways[g] + 2 * far.astype(jnp.int32)
            whole = tuple(groups[pair[g], k] for k in range(4))
            old = tuple(chain[slot, k] for k in range(4))
            outer = tuple(jnp.where(far, w, o) for w, o in zip(whole, old))
            inner = tuple(jnp.where(far, o, w) for w, o in zip(whole, old))
            for k, v in enumerate(scaled(times(outer, inner))):
                chain[slot, k] = v

        join(0)

        @pl.when(n < NZ // 2 - 1)
        def _():
            join(1)

    enter = []
    for way in range(2):
        top, bottom = chain[way + 2, 1], chain[way + 2, 3]
        enter.append((chain[way, 0] * top + chain[way, 1] * bottom) / (chain[way, 2] * top + chain[way, 3] * bottom))
    for j in range(NXP):
        for way in range(2):
            t = j if way == 0 else NXP - 1 - j
            g = enter[way]
            a, b, c, d, scale = [own_products[n, pl.ds(NXP * way + t, RADIX, stride=8), :] for n in range(5)]
            inv = 1.0 / (c * g + d)
            gin[way, t] = mirrored(g)
            abuf[way, t] = mirrored(scale * inv)
            enter[way] = (a * g + b) * inv

    wait_for(raw.at[pl.ds(0, NXP - 1)], recv_sem.at[0])
    entering = []
    for way, order in enumerate((range(NXP), range(NXP - 1, -1, -1))):
        run, mine = [jnp.zeros_like(one)] * 2, [jnp.zeros_like(one)] * 2
        for j in order:
            here = xi == j
            a = abuf[way, j]
            ae = a * (1.0 - gin[way, j])
            for part in range(2):
                end = raw[j, (2 * way + part) * RADIX : (2 * way + part + 1) * RADIX, :]
                start = raw[j, (2 - 2 * way + part) * RADIX : (3 - 2 * way + part) * RADIX, :]
                mine[part] = jnp.where(here, run[part], mine[part])
                run[part] = a * run[part] + (end + ae * start)
        for part in range(2):
            gz[way, part * RADIX : (part + 1) * RADIX, :] = run[part]
        entering.append(mine)

    to_z = []
    for q in z_peers:
        which = jnp.where(q > zi, 0, 1)
        to_z.append(remote(gz.at[which], zrecv.at[zi], send_sem.at[4], recv_sem.at[1], at_z(q)))
    for copy in to_z:
        copy.start()

    gbuf[...] = jnp.zeros_like(gbuf)

    @pl.loop(0, NZ - 1)
    def _(n):
        way = (n >= zi).astype(jnp.int32)
        q = jnp.where(n < zi, n, NZ - 1 - (n - zi))
        g = gbuf[way]
        inv = 1.0 / (groups[q, 2] * g + groups[q, 3])
        gbuf[way] = (groups[q, 0] * g + groups[q, 1]) * inv
        wbuf[q] = groups[q, 4] * inv

    def below(n, run):
        q = zi - 1 - n
        a = wbuf[q]
        wbuf[q] = mirrored(run)
        return run * a

    lax.fori_loop(0, zi, below, one)

    def above(n, run):
        q = zi + 1 + n
        a = wbuf[q]
        wbuf[q] = mirrored(run)
        return run * a

    lax.fori_loop(0, NZ - 1 - zi, above, one)
    pre, post = one, one
    for j in range(NXP):
        pre = pre * jnp.where(j < xi, abuf[0, j], 1.0)
        post = post * jnp.where(j > xi, abuf[1, j], 1.0)

    g_end = pivots(range(ROWS), low, upp, gin[0, xi], factors, 0)
    h_in = gin[1, xi]
    scale = 1.0 / (g_end + h_in * factors[2, ROWS - 1])

    for part in range(2):
        y = entering[0][part]
        for i in range(ROWS):
            y = factors[0, i] * y - factors[1, i] * rhs(i, part)
            known[part, i] = y
    reply = pre
    for i in range(ROWS):
        reply = factors[0, i] * reply
        known[2, i] = reply
    last_factor = factors[2, ROWS - 1]
    state = [(last_factor * entering[1][part] + known[part, ROWS - 1]) * scale for part in range(2)]
    state += [known[2, ROWS - 1] * scale, last_factor * scale * post]
    for i in range(ROWS - 1, -1, -1):
        if i < ROWS - 1:
            e = factors[2, i]
            state = [e * state[n] + known[n, i] for n in range(3)] + [e * state[3]]
        for n in range(4):
            known[n, i] = state[n]

    sy = [jnp.zeros_like(one)] * 2
    sz = [jnp.zeros_like(one)] * 2
    wait_for(zrecv.at[pl.ds(0, NZ - 1)], recv_sem.at[1])
    for q in z_peers:
        lower_side = q < zi
        w = wbuf[q]
        wy = jnp.where(lower_side, w, 0.0)
        wz = jnp.where(lower_side, 0.0, w)
        for part in range(2):
            v = zrecv[q, part * RADIX : (part + 1) * RADIX, :]
            sy[part] = sy[part] + wy * v
            sz[part] = sz[part] + wz * v

    for o in (1, 0):
        for i in range(8 * o, 8 * o + 8):
            for part, ref in enumerate((ure, uim)):
                x = known[part, i] + (known[2, i] * sy[part] + known[3, i] * sz[part])
                for h in range(2):
                    at = o * 128 + h * 64 + (i % 8) * 8
                    ref[at : at + 8, :] = x[8 * h : 8 * h + 8, :]
        rows = slice(128 * o, 128 * o + 128)
        back = product(jnp.concatenate([uim[rows, :], ure[rows, :]], axis=1), matrix[...])
        uim[rows, :] = back[:, :LANES]
        ure[rows, :] = back[:, LANES:]
        values = []
        for k in range(RADIX):
            re = ure[transposed(o, k), :]
            im = uim[transposed(o, k), :]
            c = twiddle[k : k + 1, :] * (1.0 / NX)
            s = twiddle[RADIX + k : RADIX + k + 1, :] * (1.0 / NX)
            values.append((re * c - im * s, im * c + re * s))
        values = butterflies(values, True)
        for a in range(RADIX):
            for part in range(2):
                obuf[a // 2, pl.ds(32 * o + 2 * part + a % 2, 8, stride=4), :] = values[a][part]
        for q in gx_peers:
            remote(octet(obuf, q, o), octet(fbuf, gx, o), send_sem.at[5], arrived.at[2 + o], at_gx(q)).start()
    own = pltpu.make_async_copy(obuf.at[gx], fbuf.at[gx], load_sem.at[0])
    own.start()
    wait_for(sbuf.at[pl.ds(0, PLANES - 1)], send_sem.at[0])
    wait_for(coef.at[pl.ds(0, NXP - 1)], send_sem.at[1])
    wait_for(coef.at[pl.ds(0, NXP * (NZ - 1))], send_sem.at[2])
    wait_for(raw.at[pl.ds(0, NXP - 1)], send_sem.at[3])
    wait_for(zrecv.at[pl.ds(0, NZ - 1)], send_sem.at[4])
    own.wait()
    wait_for(obuf.at[pl.ds(0, PLANES - 1)], send_sem.at[5])
    for o in range(2):
        wait_for_octet(fbuf, arrived.at[2 + o])


def assemble(fbuf, out, held, sem):
    count = 4 * ROWS // PARTS
    copies = []
    for n in range(PARTS):
        for q in range(PLANES):
            held[pl.ds(n * count * PLANES + q, count, stride=PLANES), :] = fbuf[q, n * count : (n + 1) * count, :]
        rows = pl.ds(n * count * PLANES, count * PLANES)
        copies.append(pltpu.make_async_copy(held.at[rows], out.at[rows], sem.at[n]))
        copies[-1].start()
    for copy in copies:
        copy.wait()


def local(source, lower, upper, span):
    matrix, twiddle = transform_constants()
    f32 = jnp.float32
    dma = pltpu.SemaphoreType.DMA
    vmem = lambda *shape: pltpu.VMEM(shape, f32)
    smem = lambda *shape: pltpu.SMEM(shape, f32)
    any_spec = pl.BlockSpec(memory_space=pl.ANY)
    shape = source.shape
    source = source.reshape(ROWS, 2, PLANES, 2, LANES).transpose(0, 1, 3, 2, 4).reshape(4 * ROWS * PLANES, LANES)
    planes = pl.pallas_call(
        kernel,
        out_shape=jax.ShapeDtypeStruct((PLANES, 64, LANES), f32),
        in_specs=[pl.BlockSpec(memory_space=pltpu.HBM)] * 6,
        out_specs=any_spec,
        scratch_shapes=[
            vmem(4 * ROWS * PLANES, LANES), vmem(PLANES, 64, LANES), vmem(PLANES, 64, LANES),
            vmem(256, LANES), vmem(256, LANES), vmem(256, 256),
            pltpu.VMEM((6 * 256, 256), jnp.bfloat16), vmem(2 * RADIX, LANES),
            smem(ROWS), smem(ROWS), smem(PLANES),
            vmem(BLOCKS, 1, LANES), vmem(4 * ROWS, 8, LANES), vmem(RADIX, LANES), vmem(5, 8 * RADIX, LANES),
            vmem(NZ, 5, RADIX, LANES), vmem(2, NXP, RADIX, LANES), vmem(NZ, RADIX, LANES),
            vmem(2, RADIX, LANES), vmem(2, NXP, RADIX, LANES), vmem(4, 4, RADIX, LANES),
            vmem(4, ROWS, RADIX, LANES), vmem(3, ROWS, RADIX, LANES), vmem(4, ROWS, RADIX, LANES),
            vmem(NXP, 64, LANES), vmem(2, 32, LANES), vmem(NZ, 32, LANES), vmem(PLANES, 64, LANES),
            dma((6,)), dma((6,)), dma((2,)), dma((4,)), dma((NXP,)), dma((NZ,)),
            pltpu.SemaphoreType.REGULAR, pltpu.SemaphoreType.REGULAR,
        ],
        compiler_params=pltpu.CompilerParams(
            collective_id=0, has_side_effects=True, vmem_limit_bytes=16 * 1024 * 1024),
    )(*[pltpu.with_memory_space_constraint(x, pltpu.HBM)
        for x in (source, lower, upper, span, jnp.asarray(matrix), jnp.asarray(twiddle))])
    result = pl.pallas_call(
        assemble,
        out_shape=jax.ShapeDtypeStruct((ROWS * 4 * PLANES, LANES), f32),
        in_specs=[pl.BlockSpec(memory_space=pltpu.VMEM)],
        out_specs=pl.BlockSpec(memory_space=pltpu.HBM),
        scratch_shapes=[vmem(ROWS * 4 * PLANES, LANES), dma((PARTS,))],
        compiler_params=pltpu.CompilerParams(vmem_limit_bytes=4 * 1024 * 1024),
    )(planes)
    result = result.reshape(ROWS, 2, 2, PLANES, LANES)
    return result.transpose(0, 1, 3, 2, 4).reshape(shape)


def solution(mesh):
    in_specs = (P("gy", None, None, "gx"), P("gy"), P("gy"), P())
    out_specs = P("gy", None, None, "gx")
    return jax.shard_map(local, mesh=mesh, in_specs=in_specs, out_specs=out_specs, check_vma=False)
```

```python
import math

import jax
import jax.numpy as jnp
import ml_dtypes
import numpy as np
from jax import lax
from jax.experimental import pallas as pl
from jax.experimental.pallas import tpu as pltpu
from jax.sharding import PartitionSpec as P

MESH = pl.DeviceIdType.MESH

ROWS = 16
PLANES = 8
NX = 2048
LANES = 128
RADIX = 16
NZ = 8
NXP = 4
BLOCKS = NZ * NXP
HALF = RADIX // 2 + 1
PARTS = 4


def transform_constants():
    lanes = np.arange(LANES)
    angle = 2.0 * np.pi * (np.outer(lanes, lanes) % LANES) / LANES
    c, s = np.cos(angle), np.sin(angle)
    matrix = np.block([[c, -s], [s, c]]).astype(np.float32)
    terms, rest = [], matrix
    for _ in range(3):
        terms.append(rest.astype(ml_dtypes.bfloat16))
        rest = rest - terms[-1].astype(np.float32)
    matrix = np.concatenate([terms[0], terms[1], terms[2], terms[0], terms[1], terms[0]])
    twist = 2.0 * np.pi * (np.outer(np.arange(RADIX), lanes) % NX) / NX
    twiddle = np.concatenate([np.cos(twist), np.sin(twist)]).astype(np.float32)
    return matrix, twiddle


def rotated(value, index, size, inverse):
    re, im = value
    index = index % size
    if index == 0:
        return value
    if 4 * index == size:
        return (-im, re) if inverse else (im, -re)
    c = math.cos(2.0 * math.pi * index / size)
    s = math.sin(2.0 * math.pi * index / size)
    if not inverse:
        s = -s
    return (re * c - im * s, re * s + im * c)


def butterflies(values, inverse):
    size = len(values)
    if size == 1:
        return values
    even = butterflies(values[0::2], inverse)
    odd = butterflies(values[1::2], inverse)
    odd = [rotated(o, k, size, inverse) for k, o in enumerate(odd)]
    low = [(e[0] + o[0], e[1] + o[1]) for e, o in zip(even, odd)]
    high = [(e[0] - o[0], e[1] - o[1]) for e, o in zip(even, odd)]
    return low + high


def product(x, matrix):
    high = x.astype(jnp.bfloat16)
    rest = x - high.astype(jnp.float32)
    middle = rest.astype(jnp.bfloat16)
    low = (rest - middle.astype(jnp.float32)).astype(jnp.bfloat16)
    terms = jnp.concatenate([high, high, high, middle, middle, low], axis=1)
    return jnp.dot(terms, matrix, preferred_element_type=jnp.float32)


def times(x, y):
    a, b, c, d = x
    e, f, g, h = y
    return (a * e + b * g, a * f + b * h, c * e + d * g, c * f + d * h)


def scaled(x):
    r = pl.reciprocal(x[2] + x[3], approx=True)
    return tuple(v * r for v in x)


def mirrored(x):
    sub = lax.broadcasted_iota(jnp.int32, (8, LANES), 0)
    lane = lax.broadcasted_iota(jnp.int32, (8, LANES), 1)
    top = x[0:8, :]
    turned = jnp.take_along_axis(top, LANES - 1 - lane, axis=1)
    turned = jnp.take_along_axis(turned, (8 - sub) % 8, axis=0)
    return jnp.concatenate([top, jnp.where(sub == 0, x[8:16, :], turned)], axis=0)


def transposed(o, k):
    return pl.ds(o * 128 + (k // 8) * 64 + k % 8, 8, stride=8)


def kernel(
    source, lower_hbm, upper_hbm, span_hbm, matrix_hbm, twiddle_hbm, fbuf,
    src, sbuf, rbuf, ure, uim, spec, matrix, twiddle, lower, upper, span,
    coef, splats, kbuf, own_products, groups, abuf, wbuf, gbuf, gin, chain, alone, factors, known,
    raw, gz, zrecv, obuf,
    load_sem, send_sem, crossed, arrived, cxr_sem, czr_sem, near_sem, far_sem,
):
    gx = lax.axis_index("gx")
    gy = lax.axis_index("gy")
    zi = gy // NXP
    xi = gy % NXP
    base = zi * NXP

    chip, core = gx // 2, gx % 2
    gx_peers = [lax.rem(chip + d, PLANES // 2) * 2 + lax.rem(core + c, 2)
                for d, c in ((2, 0), (2, 1), (1, 0), (3, 0), (1, 1), (3, 1), (0, 1))]
    x_peers = [lax.rem(xi + d, NXP) for d in (2, 1, 3)]
    z_peers = [lax.rem(zi + d, NZ) for d in (4, 3, 5, 2, 6, 1, 7)]

    def at_gx(q):
        return (q, gy)

    def at_x(q):
        return (gx, base + q)

    def at_z(q):
        return (gx, q * NXP + xi)

    z_near = [lax.rem(zi + d, NZ) for d in (1, NZ - 1)]
    z_far = [lax.rem(zi + d, NZ) for d in (2, NZ - 2)]
    near = [at_z(q) for q in z_near] + [at_x(q) for q in x_peers] + [at_gx(q) for q in gx_peers]
    loads = [pltpu.make_async_copy(there, here, load_sem.at[n]) for n, (there, here) in enumerate((
        (source, src), (lower_hbm, lower), (upper_hbm, upper), (span_hbm, span),
        (twiddle_hbm, twiddle), (matrix_hbm, matrix)))]
    loads[0].start()
    barrier = pltpu.get_barrier_semaphore()
    for device in near:
        pl.semaphore_signal(barrier, inc=1, device_id=device, device_id_type=MESH)
    for load in loads[1:]:
        load.start()

    loads[0].wait()
    for q in range(PLANES):
        sbuf[q] = src[pl.ds(q, 4 * ROWS, stride=PLANES), :]

    pl.semaphore_wait(barrier, len(near))

    def remote(src_ref, dst_ref, send, recv, device):
        return pltpu.make_async_remote_copy(
            src_ref=src_ref, dst_ref=dst_ref, send_sem=send, recv_sem=recv,
            device_id=device, device_id_type=MESH)

    def octet(ref, q, o):
        return ref.at[q, pl.ds(32 * o, 32)]

    for o in range(2):
        for q in gx_peers:
            remote(octet(sbuf, q, o), octet(rbuf, gx, o), send_sem.at[0], arrived.at[o], at_gx(q)).start()
    for q in z_near:
        pl.semaphore_signal(near_sem, inc=1, device_id=at_z(q), device_id_type=MESH)
    rbuf[gx] = sbuf[gx]

    for load in loads[1:4]:
        load.wait()
    first, last = gy == 0, gy == BLOCKS - 1
    low = [lower[i] for i in range(ROWS)]
    upp = [upper[i] for i in range(ROWS)]
    low[0] = jnp.where(first, 0.0, low[0])
    upp[-1] = jnp.where(last, 0.0, upp[-1])
    sums, lost = [], []
    for l, u in zip(low, upp):
        total = l + u
        rest = total - l
        sums.append(total)
        lost.append(-((l - (total - rest)) + (u - rest)))
    lane = lax.broadcasted_iota(jnp.int32, (1, LANES), 1)
    row = jnp.zeros((1, LANES), jnp.float32)
    for i, value in enumerate(low + upp + sums + lost + upp[::-1] + low[::-1] + sums[::-1] + lost[::-1]):
        row = jnp.where(lane == i, value, row)
    coef[gy] = row

    coef_x = [remote(coef.at[gy], coef.at[gy], send_sem.at[1], cxr_sem.at[xi], at_x(q)) for q in x_peers]
    for copy in coef_x:
        copy.start()

    k1 = lax.broadcasted_iota(jnp.int32, (RADIX, LANES), 0)
    k2 = lax.broadcasted_iota(jnp.int32, (RADIX, LANES), 1)
    mode = k1 + RADIX * k2
    signed = jnp.where(mode < NX // 2, mode, mode - NX).astype(jnp.float32)
    wave = 2.0 * signed / NX
    kappa = span[gx] * span[gx] + wave * wave
    one = jnp.ones((RADIX, LANES), jnp.float32)

    def pivots(order, ahead, behind, g, keep, into):
        for i in order:
            l, u = ahead[i], behind[i]
            s = (((sums[i] + kappa) - sums[i]) + lost[i]) + l * g
            inv = 1.0 / (u + s)
            g = s * inv
            keep[into, i] = l * inv
            keep[into + 1, i] = inv
            if keep is factors:
                keep[into + 2, i] = u * inv
        return g

    pivots(range(ROWS), low, upp, one, alone, 0)
    pivots(range(ROWS - 1, -1, -1), upp, low, one, alone, 2)

    pl.semaphore_wait(near_sem, 2)
    for q in z_far:
        pl.semaphore_signal(far_sem, inc=1, device_id=at_z(q), device_id_type=MESH)

    for q in x_peers:
        there = coef.at[base + q]
        remote(there, there, send_sem.at[1], cxr_sem.at[q], at_x(q)).wait_recv()
    pl.semaphore_wait(far_sem, 2)
    group = coef.at[pl.ds(base, NXP)]
    coef_z = [remote(group, group, send_sem.at[2], czr_sem.at[zi], at_z(q)) for q in z_peers]
    for copy in coef_z:
        copy.start()

    kbuf[...] = kappa

    def block_products(blocks, ways, finish):
        rows = jnp.concatenate([coef[t] for t in blocks], axis=0)
        sub = lax.broadcasted_iota(jnp.int32, (8, LANES), 0)
        turn = jnp.where(sub < NXP, ways[0], ways[1]) == 1
        rows = jnp.where(turn, pltpu.roll(rows, LANES // 2, 1), rows)
        scale = None
        for k in range(4 * ROWS):
            one = jnp.broadcast_to(rows[:, k : k + 1], (8, LANES))
            splats[k] = one
            if k < ROWS:
                scale = one if scale is None else scale * one
        for k in range(0, HALF, 3):
            waves = [jnp.broadcast_to(kbuf[n : n + 1, :], (8, LANES)) for n in range(k, k + 3)]
            state = [None] * 3
            for i in range(ROWS):
                l, u, total, gained = [splats[n * ROWS + i] for n in range(4)]
                for n in range(3):
                    rounded = ((total + waves[n]) - total) + gained
                    if i == 0:
                        state[n] = (l, rounded, l, u + rounded)
                        continue
                    a, b, c, d = state[n]
                    a = l * a + rounded * c
                    b = l * b + rounded * d
                    state[n] = (a, b, a + u * c, b + u * d)
            for n in range(3):
                finish(k + n, scaled(state[n] + (scale,)))

    def keep_own(k, values):
        for n, v in enumerate(values):
            own_products[n, 8 * k : 8 * k + 8, :] = v

    block_products([base + j for j in range(NXP)] * 2, (0, 1), keep_own)

    def wait_for(ref, sem):
        pltpu.make_async_copy(ref, ref, sem).wait()

    def wait_for_octet(ref, sem):
        wait_for(ref.at[pl.ds(0, PLANES - 1), pl.ds(0, 32)], sem)

    for o in range(2):
        wait_for_octet(rbuf, arrived.at[o])
        if o == 0:
            loads[4].wait()
            loads[5].wait()
        values = []
        for a in range(RADIX):
            values.append(tuple(rbuf[a // 2, pl.ds(32 * o + 2 * part + a % 2, 8, stride=4), :] for part in range(2)))
        values = butterflies(values, False)
        for k in range(RADIX):
            re, im = values[k]
            c, s = twiddle[k : k + 1, :], twiddle[RADIX + k : RADIX + k + 1, :]
            ure[transposed(o, k), :] = re * c + im * s
            uim[transposed(o, k), :] = im * c - re * s
        rows = slice(128 * o, 128 * o + 128)
        spec[rows, :] = product(jnp.concatenate([ure[rows, :], uim[rows, :]], axis=1), matrix[...])

    def rhs(i, part):
        lanes = slice(part * LANES, (part + 1) * LANES)
        at = [(i // 8) * 128 + h * 64 + (i % 8) * 8 for h in range(2)]
        return jnp.concatenate([spec[n : n + 8, lanes] for n in at], axis=0)

    def half(ref, q, h, rows):
        return ref.at[q, pl.ds(h * rows, rows)]

    for h in range(2):
        part_modes = slice(8 * h, 8 * h + 8)
        for way, order in enumerate((range(ROWS), range(ROWS - 1, -1, -1))):
            for part in range(2):
                y = None
                for i in order:
                    at = (i // 8) * 128 + h * 64 + (i % 8) * 8
                    r = spec[at : at + 8, part * LANES : (part + 1) * LANES] * alone[2 * way + 1, i, part_modes, :]
                    y = -r if y is None else alone[2 * way, i, part_modes, :] * y - r
                at = h * 32 + (2 * way + part) * 8
                raw[xi, at : at + 8, :] = y
        for q in x_peers:
            remote(half(raw, xi, h, 32), half(raw, xi, h, 32), send_sem.at[3], crossed.at[h], at_x(q)).start()

    for slot in range(4):
        for k in range(4):
            chain[slot, k] = jnp.zeros_like(one) if k in (1, 2) else one

    def next_block(x, shift):
        return tuple(pltpu.roll(v, 8 - shift, 0) for v in x)

    @pl.loop(0, NZ // 2)
    def _(n):
        pair = (lax.rem(zi + n + 1, NZ), lax.rem(zi + NZ - 1 - n, NZ))
        ways = [(q > zi).astype(jnp.int32) for q in pair]

        def arrive(q):
            there = coef.at[pl.ds(q * NXP, NXP)]
            remote(there, there, send_sem.at[2], czr_sem.at[q], at_z(q)).wait_recv()

        arrive(pair[0])

        @pl.when(n < NZ // 2 - 1)
        def _():
            arrive(pair[1])

        def keep_groups(k, values):
            for shift in (1, 2):
                later = next_block(values, shift)
                values = times(later[:4], values[:4]) + (later[4] * values[4],)
            values = scaled(values)
            for m, v in enumerate(values):
                for g in range(2):
                    groups[pair[g], m, k : k + 1, :] = v[NXP * g : NXP * g + 1, :]

        blocks = [q * NXP + jnp.where(w == 0, j, NXP - 1 - j) for q, w in zip(pair, ways) for j in range(NXP)]
        block_products(blocks, ways, keep_groups)

        def join(g):
            far = ways[g] != 1 - g
            slot = ways[g] + 2 * far.astype(jnp.int32)
            whole = tuple(groups[pair[g], k] for k in range(4))
            old = tuple(chain[slot, k] for k in range(4))
            outer = tuple(jnp.where(far, w, o) for w, o in zip(whole, old))
            inner = tuple(jnp.where(far, o, w) for w, o in zip(whole, old))
            for k, v in enumerate(scaled(times(outer, inner))):
                chain[slot, k] = v

        join(0)

        @pl.when(n < NZ // 2 - 1)
        def _():
            join(1)

    enter = []
    for way in range(2):
        top, bottom = chain[way + 2, 1], chain[way + 2, 3]
        enter.append((chain[way, 0] * top + chain[way, 1] * bottom) / (chain[way, 2] * top + chain[way, 3] * bottom))
    for j in range(NXP):
        for way in range(2):
            t = j if way == 0 else NXP - 1 - j
            g = enter[way]
            a, b, c, d, scale = [own_products[n, pl.ds(NXP * way + t, RADIX, stride=8), :] for n in range(5)]
            inv = 1.0 / (c * g + d)
            gin[way, t] = mirrored(g)
            abuf[way, t] = mirrored(scale * inv)
            enter[way] = (a * g + b) * inv

    entering = [[[], []], [[], []]]
    for h in range(2):
        part_modes = slice(8 * h, 8 * h + 8)
        wait_for(raw.at[pl.ds(0, NXP - 1), pl.ds(0, 32)], crossed.at[h])
        for way, order in enumerate((range(NXP), range(NXP - 1, -1, -1))):
            none = jnp.zeros((8, LANES), jnp.float32)
            run, mine = [none] * 2, [none] * 2
            for j in order:
                here = xi == j
                a = abuf[way, j, part_modes, :]
                ae = a * (1.0 - gin[way, j, part_modes, :])
                for part in range(2):
                    end, start = [raw[j, n : n + 8, :] for n in (
                        h * 32 + (2 * way + part) * 8, h * 32 + (2 - 2 * way + part) * 8)]
                    mine[part] = jnp.where(here, run[part], mine[part])
                    run[part] = a * run[part] + (end + ae * start)
            for part in range(2):
                at = h * 16 + part * 8
                gz[way, at : at + 8, :] = run[part]
                entering[way][part].append(mine[part])
        for q in z_peers:
            which = jnp.where(q > zi, 0, 1)
            remote(half(gz, which, h, 16), half(zrecv, zi, h, 16), send_sem.at[4], crossed.at[2 + h], at_z(q)).start()
    entering = [[jnp.concatenate(halves, axis=0) for halves in way] for way in entering]

    gbuf[...] = jnp.zeros_like(gbuf)

    @pl.loop(0, NZ - 1)
    def _(n):
        way = (n >= zi).astype(jnp.int32)
        q = jnp.where(n < zi, n, NZ - 1 - (n - zi))
        g = gbuf[way]
        inv = 1.0 / (groups[q, 2] * g + groups[q, 3])
        gbuf[way] = (groups[q, 0] * g + groups[q, 1]) * inv
        wbuf[q] = groups[q, 4] * inv

    def below(n, run):
        q = zi - 1 - n
        a = wbuf[q]
        wbuf[q] = mirrored(run)
        return run * a

    lax.fori_loop(0, zi, below, one)

    def above(n, run):
        q = zi + 1 + n
        a = wbuf[q]
        wbuf[q] = mirrored(run)
        return run * a

    lax.fori_loop(0, NZ - 1 - zi, above, one)
    pre, post = one, one
    for j in range(NXP):
        pre = pre * jnp.where(j < xi, abuf[0, j], 1.0)
        post = post * jnp.where(j > xi, abuf[1, j], 1.0)

    g_end = pivots(range(ROWS), low, upp, gin[0, xi], factors, 0)
    h_in = gin[1, xi]
    scale = 1.0 / (g_end + h_in * factors[2, ROWS - 1])

    for part in range(2):
        y = entering[0][part]
        for i in range(ROWS):
            y = factors[0, i] * y - factors[1, i] * rhs(i, part)
            known[part, i] = y
    reply = pre
    for i in range(ROWS):
        reply = factors[0, i] * reply
        known[2, i] = reply
    last_factor = factors[2, ROWS - 1]
    state = [(last_factor * entering[1][part] + known[part, ROWS - 1]) * scale for part in range(2)]
    state += [known[2, ROWS - 1] * scale, last_factor * scale * post]
    for i in range(ROWS - 1, -1, -1):
        if i < ROWS - 1:
            e = factors[2, i]
            state = [e * state[n] + known[n, i] for n in range(3)] + [e * state[3]]
        for n in range(4):
            known[n, i] = state[n]

    brought = [[], []]
    for h in range(2):
        wait_for(zrecv.at[pl.ds(0, NZ - 1), pl.ds(0, 16)], crossed.at[2 + h])
        none = jnp.zeros((8, LANES), jnp.float32)
        sums = [[none] * 2, [none] * 2]
        for q in z_peers:
            lower_side = q < zi
            w = wbuf[q, 8 * h : 8 * h + 8, :]
            wy = jnp.where(lower_side, w, 0.0)
            wz = jnp.where(lower_side, 0.0, w)
            for part in range(2):
                v = zrecv[q, h * 16 + part * 8 : h * 16 + part * 8 + 8, :]
                sums[0][part] = sums[0][part] + wy * v
                sums[1][part] = sums[1][part] + wz * v
        brought[0].append(sums[0])
        brought[1].append(sums[1])
    sy, sz = [[jnp.concatenate([side[0][part], side[1][part]], axis=0) for part in range(2)] for side in brought]

    for o in (1, 0):
        for i in range(8 * o, 8 * o + 8):
            for part, ref in enumerate((ure, uim)):
                x = known[part, i] + (known[2, i] * sy[part] + known[3, i] * sz[part])
                for h in range(2):
                    at = o * 128 + h * 64 + (i % 8) * 8
                    ref[at : at + 8, :] = x[8 * h : 8 * h + 8, :]
        rows = slice(128 * o, 128 * o + 128)
        back = product(jnp.concatenate([uim[rows, :], ure[rows, :]], axis=1), matrix[...])
        uim[rows, :] = back[:, :LANES]
        ure[rows, :] = back[:, LANES:]
        values = []
        for k in range(RADIX):
            re = ure[transposed(o, k), :]
            im = uim[transposed(o, k), :]
            c = twiddle[k : k + 1, :] * (1.0 / NX)
            s = twiddle[RADIX + k : RADIX + k + 1, :] * (1.0 / NX)
            values.append((re * c - im * s, im * c + re * s))
        values = butterflies(values, True)
        for a in range(RADIX):
            for part in range(2):
                obuf[a // 2, pl.ds(32 * o + 2 * part + a % 2, 8, stride=4), :] = values[a][part]
        for q in gx_peers:
            remote(octet(obuf, q, o), octet(fbuf, gx, o), send_sem.at[5], arrived.at[2 + o], at_gx(q)).start()
    own = pltpu.make_async_copy(obuf.at[gx], fbuf.at[gx], load_sem.at[0])
    own.start()
    wait_for(sbuf.at[pl.ds(0, PLANES - 1)], send_sem.at[0])
    wait_for(coef.at[pl.ds(0, NXP - 1)], send_sem.at[1])
    wait_for(coef.at[pl.ds(0, NXP * (NZ - 1))], send_sem.at[2])
    wait_for(raw.at[pl.ds(0, NXP - 1)], send_sem.at[3])
    wait_for(zrecv.at[pl.ds(0, NZ - 1)], send_sem.at[4])
    own.wait()
    wait_for(obuf.at[pl.ds(0, PLANES - 1)], send_sem.at[5])
    for o in range(2):
        wait_for_octet(fbuf, arrived.at[2 + o])


def assemble(fbuf, out, held, sem):
    count = 4 * ROWS // PARTS
    copies = []
    for n in range(PARTS):
        for q in range(PLANES):
            held[pl.ds(n * count * PLANES + q, count, stride=PLANES), :] = fbuf[q, n * count : (n + 1) * count, :]
        rows = pl.ds(n * count * PLANES, count * PLANES)
        copies.append(pltpu.make_async_copy(held.at[rows], out.at[rows], sem.at[n]))
        copies[-1].start()
    for copy in copies:
        copy.wait()


def local(source, lower, upper, span):
    matrix, twiddle = transform_constants()
    f32 = jnp.float32
    dma = pltpu.SemaphoreType.DMA
    vmem = lambda *shape: pltpu.VMEM(shape, f32)
    smem = lambda *shape: pltpu.SMEM(shape, f32)
    any_spec = pl.BlockSpec(memory_space=pl.ANY)
    shape = source.shape
    source = source.reshape(ROWS, 2, PLANES, 2, LANES).transpose(0, 1, 3, 2, 4).reshape(4 * ROWS * PLANES, LANES)
    planes = pl.pallas_call(
        kernel,
        out_shape=jax.ShapeDtypeStruct((PLANES, 64, LANES), f32),
        in_specs=[pl.BlockSpec(memory_space=pltpu.HBM)] * 6,
        out_specs=any_spec,
        scratch_shapes=[
            vmem(4 * ROWS * PLANES, LANES), vmem(PLANES, 64, LANES), vmem(PLANES, 64, LANES),
            vmem(256, LANES), vmem(256, LANES), vmem(256, 256),
            pltpu.VMEM((6 * 256, 256), jnp.bfloat16), vmem(2 * RADIX, LANES),
            smem(ROWS), smem(ROWS), smem(PLANES),
            vmem(BLOCKS, 1, LANES), vmem(4 * ROWS, 8, LANES), vmem(RADIX, LANES), vmem(5, 8 * RADIX, LANES),
            vmem(NZ, 5, RADIX, LANES), vmem(2, NXP, RADIX, LANES), vmem(NZ, RADIX, LANES),
            vmem(2, RADIX, LANES), vmem(2, NXP, RADIX, LANES), vmem(4, 4, RADIX, LANES),
            vmem(4, ROWS, RADIX, LANES), vmem(3, ROWS, RADIX, LANES), vmem(4, ROWS, RADIX, LANES),
            vmem(NXP, 64, LANES), vmem(2, 32, LANES), vmem(NZ, 32, LANES), vmem(PLANES, 64, LANES),
            dma((6,)), dma((6,)), dma((4,)), dma((4,)), dma((NXP,)), dma((NZ,)),
            pltpu.SemaphoreType.REGULAR, pltpu.SemaphoreType.REGULAR,
        ],
        compiler_params=pltpu.CompilerParams(
            collective_id=0, has_side_effects=True, vmem_limit_bytes=16 * 1024 * 1024),
    )(*[pltpu.with_memory_space_constraint(x, pltpu.HBM)
        for x in (source, lower, upper, span, jnp.asarray(matrix), jnp.asarray(twiddle))])
    result = pl.pallas_call(
        assemble,
        out_shape=jax.ShapeDtypeStruct((ROWS * 4 * PLANES, LANES), f32),
        in_specs=[pl.BlockSpec(memory_space=pltpu.VMEM)],
        out_specs=pl.BlockSpec(memory_space=pltpu.HBM),
        scratch_shapes=[vmem(ROWS * 4 * PLANES, LANES), dma((PARTS,))],
        compiler_params=pltpu.CompilerParams(vmem_limit_bytes=4 * 1024 * 1024),
    )(planes)
    result = result.reshape(ROWS, 2, 2, PLANES, LANES)
    return result.transpose(0, 1, 3, 2, 4).reshape(shape)


def solution(mesh):
    in_specs = (P("gy", None, None, "gx"), P("gy"), P("gy"), P())
    out_specs = P("gy", None, None, "gx")
    return jax.shard_map(local, mesh=mesh, in_specs=in_specs, out_specs=out_specs, check_vma=False)
```

```python
import math

import jax
import jax.numpy as jnp
import ml_dtypes
import numpy as np
from jax import lax
from jax.experimental import pallas as pl
from jax.experimental.pallas import tpu as pltpu
from jax.sharding import PartitionSpec as P

MESH = pl.DeviceIdType.MESH

ROWS = 16
PLANES = 8
NX = 2048
LANES = 128
RADIX = 16
NZ = 8
NXP = 4
BLOCKS = NZ * NXP
HALF = RADIX // 2 + 1
PARTS = 4


def transform_constants():
    lanes = np.arange(LANES)
    angle = 2.0 * np.pi * (np.outer(lanes, lanes) % LANES) / LANES
    c, s = np.cos(angle), np.sin(angle)
    matrix = np.block([[c, -s], [s, c]]).astype(np.float32)
    terms, rest = [], matrix
    for _ in range(3):
        terms.append(rest.astype(ml_dtypes.bfloat16))
        rest = rest - terms[-1].astype(np.float32)
    matrix = np.concatenate([terms[0], terms[1], terms[2], terms[0], terms[1], terms[0]])
    twist = 2.0 * np.pi * (np.outer(np.arange(RADIX), lanes) % NX) / NX
    twiddle = np.concatenate([np.cos(twist), np.sin(twist)]).astype(np.float32)
    return matrix, twiddle


def rotated(value, index, size, inverse):
    re, im = value
    index = index % size
    if index == 0:
        return value
    if 4 * index == size:
        return (-im, re) if inverse else (im, -re)
    c = math.cos(2.0 * math.pi * index / size)
    s = math.sin(2.0 * math.pi * index / size)
    if not inverse:
        s = -s
    return (re * c - im * s, re * s + im * c)


def butterflies(values, inverse):
    size = len(values)
    if size == 1:
        return values
    even = butterflies(values[0::2], inverse)
    odd = butterflies(values[1::2], inverse)
    odd = [rotated(o, k, size, inverse) for k, o in enumerate(odd)]
    low = [(e[0] + o[0], e[1] + o[1]) for e, o in zip(even, odd)]
    high = [(e[0] - o[0], e[1] - o[1]) for e, o in zip(even, odd)]
    return low + high


def product(x, matrix):
    high = x.astype(jnp.bfloat16)
    rest = x - high.astype(jnp.float32)
    middle = rest.astype(jnp.bfloat16)
    low = (rest - middle.astype(jnp.float32)).astype(jnp.bfloat16)
    terms = jnp.concatenate([high, high, high, middle, middle, low], axis=1)
    return jnp.dot(terms, matrix, preferred_element_type=jnp.float32)


def times(x, y):
    a, b, c, d = x
    e, f, g, h = y
    return (a * e + b * g, a * f + b * h, c * e + d * g, c * f + d * h)


def scaled(x):
    r = pl.reciprocal(x[2] + x[3], approx=True)
    return tuple(v * r for v in x)


def mirrored(x):
    sub = lax.broadcasted_iota(jnp.int32, (8, LANES), 0)
    lane = lax.broadcasted_iota(jnp.int32, (8, LANES), 1)
    top = x[0:8, :]
    turned = jnp.take_along_axis(top, LANES - 1 - lane, axis=1)
    turned = jnp.take_along_axis(turned, (8 - sub) % 8, axis=0)
    return jnp.concatenate([top, jnp.where(sub == 0, x[8:16, :], turned)], axis=0)


def transposed(o, k):
    return pl.ds(o * 128 + (k // 8) * 64 + k % 8, 8, stride=8)


def kernel(
    source, lower_hbm, upper_hbm, span_hbm, matrix_hbm, twiddle_hbm, fbuf,
    src, sbuf, rbuf, ure, uim, spec, matrix, twiddle, lower, upper, span,
    coef, splats, kbuf, own_products, groups, abuf, wbuf, gbuf, gin, chain, alone, weights, factors, known,
    raw, gz, zrecv, obuf,
    load_sem, send_sem, crossed, arrived, cxr_sem, czr_sem, near_sem, far_sem,
):
    gx = lax.axis_index("gx")
    gy = lax.axis_index("gy")
    zi = gy // NXP
    xi = gy % NXP
    base = zi * NXP

    chip, core = gx // 2, gx % 2
    gx_peers = [lax.rem(chip + d, PLANES // 2) * 2 + lax.rem(core + c, 2)
                for d, c in ((2, 0), (2, 1), (1, 0), (3, 0), (1, 1), (3, 1), (0, 1))]
    x_peers = [lax.rem(xi + d, NXP) for d in (2, 1, 3)]
    z_peers = [lax.rem(zi + d, NZ) for d in (4, 3, 5, 2, 6, 1, 7)]

    def at_gx(q):
        return (q, gy)

    def at_x(q):
        return (gx, base + q)

    def at_z(q):
        return (gx, q * NXP + xi)

    z_near = [lax.rem(zi + d, NZ) for d in (1, NZ - 1)]
    z_far = [lax.rem(zi + d, NZ) for d in (2, NZ - 2)]
    near = [at_gx(q) for q in gx_peers] + [at_x(q) for q in x_peers] + [at_z(q) for q in z_near]
    loads = [pltpu.make_async_copy(there, here, load_sem.at[n]) for n, (there, here) in enumerate((
        (source, src), (lower_hbm, lower), (upper_hbm, upper), (span_hbm, span),
        (twiddle_hbm, twiddle), (matrix_hbm, matrix)))]
    loads[0].start()
    barrier = pltpu.get_barrier_semaphore()
    for device in near:
        pl.semaphore_signal(barrier, inc=1, device_id=device, device_id_type=MESH)
    for load in loads[1:]:
        load.start()

    loads[0].wait()
    for q in range(PLANES):
        sbuf[q] = src[pl.ds(q, 4 * ROWS, stride=PLANES), :]

    pl.semaphore_wait(barrier, len(near))

    def remote(src_ref, dst_ref, send, recv, device):
        return pltpu.make_async_remote_copy(
            src_ref=src_ref, dst_ref=dst_ref, send_sem=send, recv_sem=recv,
            device_id=device, device_id_type=MESH)

    def octet(ref, q, o):
        return ref.at[q, pl.ds(32 * o, 32)]

    for o in range(2):
        for q in gx_peers:
            remote(octet(sbuf, q, o), octet(rbuf, gx, o), send_sem.at[0], arrived.at[o], at_gx(q)).start()
    for q in z_near:
        pl.semaphore_signal(near_sem, inc=1, device_id=at_z(q), device_id_type=MESH)
    rbuf[gx] = sbuf[gx]

    for load in loads[1:4]:
        load.wait()
    first, last = gy == 0, gy == BLOCKS - 1
    low = [lower[i] for i in range(ROWS)]
    upp = [upper[i] for i in range(ROWS)]
    low[0] = jnp.where(first, 0.0, low[0])
    upp[-1] = jnp.where(last, 0.0, upp[-1])
    sums, lost = [], []
    for l, u in zip(low, upp):
        total = l + u
        rest = total - l
        sums.append(total)
        lost.append(-((l - (total - rest)) + (u - rest)))
    lane = lax.broadcasted_iota(jnp.int32, (1, LANES), 1)
    row = jnp.zeros((1, LANES), jnp.float32)
    for i, value in enumerate(low + upp + sums + lost + upp[::-1] + low[::-1] + sums[::-1] + lost[::-1]):
        row = jnp.where(lane == i, value, row)
    coef[gy] = row

    coef_x = [remote(coef.at[gy], coef.at[gy], send_sem.at[1], cxr_sem.at[xi], at_x(q)) for q in x_peers]
    for copy in coef_x:
        copy.start()

    k1 = lax.broadcasted_iota(jnp.int32, (RADIX, LANES), 0)
    k2 = lax.broadcasted_iota(jnp.int32, (RADIX, LANES), 1)
    mode = k1 + RADIX * k2
    signed = jnp.where(mode < NX // 2, mode, mode - NX).astype(jnp.float32)
    wave = 2.0 * signed / NX
    kappa = span[gx] * span[gx] + wave * wave
    one = jnp.ones((RADIX, LANES), jnp.float32)

    def pivots(order, ahead, behind, g, keep, into):
        for i in order:
            l, u = ahead[i], behind[i]
            s = (((sums[i] + kappa) - sums[i]) + lost[i]) + l * g
            inv = 1.0 / (u + s)
            g = s * inv
            keep[into, i] = l * inv
            keep[into + 1, i] = inv
            if keep is factors:
                keep[into + 2, i] = u * inv
        return g

    pivots(range(ROWS), low, upp, one, alone, 0)
    pivots(range(ROWS - 1, -1, -1), upp, low, one, alone, 2)
    for way, order in enumerate((range(ROWS - 1, -1, -1), range(ROWS))):
        run = -one
        for i in order:
            weights[way, i] = run * alone[2 * way + 1, i]
            run = run * alone[2 * way, i]

    pl.semaphore_wait(near_sem, 2)
    for q in z_far:
        pl.semaphore_signal(far_sem, inc=1, device_id=at_z(q), device_id_type=MESH)

    for q in x_peers:
        there = coef.at[base + q]
        remote(there, there, send_sem.at[1], cxr_sem.at[q], at_x(q)).wait_recv()
    pl.semaphore_wait(far_sem, 2)
    group = coef.at[pl.ds(base, NXP)]
    coef_z = [remote(group, group, send_sem.at[2], czr_sem.at[zi], at_z(q)) for q in z_peers]
    for copy in coef_z:
        copy.start()

    kbuf[...] = kappa

    def block_products(blocks, ways, finish):
        rows = jnp.concatenate([coef[t] for t in blocks], axis=0)
        sub = lax.broadcasted_iota(jnp.int32, (8, LANES), 0)
        turn = jnp.where(sub < NXP, ways[0], ways[1]) == 1
        rows = jnp.where(turn, pltpu.roll(rows, LANES // 2, 1), rows)
        scale = None
        for k in range(4 * ROWS):
            one = jnp.broadcast_to(rows[:, k : k + 1], (8, LANES))
            splats[k] = one
            if k < ROWS:
                scale = one if scale is None else scale * one
        for k in range(0, HALF, 3):
            waves = [jnp.broadcast_to(kbuf[n : n + 1, :], (8, LANES)) for n in range(k, k + 3)]
            state = [None] * 3
            for i in range(ROWS):
                l, u, total, gained = [splats[n * ROWS + i] for n in range(4)]
                for n in range(3):
                    rounded = ((total + waves[n]) - total) + gained
                    if i == 0:
                        state[n] = (l, rounded, l, u + rounded)
                        continue
                    a, b, c, d = state[n]
                    a = l * a + rounded * c
                    b = l * b + rounded * d
                    state[n] = (a, b, a + u * c, b + u * d)
            for n in range(3):
                finish(k + n, scaled(state[n] + (scale,)))

    def keep_own(k, values):
        for n, v in enumerate(values):
            own_products[n, 8 * k : 8 * k + 8, :] = v

    block_products([base + j for j in range(NXP)] * 2, (0, 1), keep_own)

    def wait_for(ref, sem):
        pltpu.make_async_copy(ref, ref, sem).wait()

    def wait_for_octet(ref, sem):
        wait_for(ref.at[pl.ds(0, PLANES - 1), pl.ds(0, 32)], sem)

    alone_ends = [[None] * 2, [None] * 2]
    for o in range(2):
        wait_for_octet(rbuf, arrived.at[o])
        if o == 0:
            loads[4].wait()
            loads[5].wait()
        values = []
        for a in range(RADIX):
            values.append(tuple(rbuf[a // 2, pl.ds(32 * o + 2 * part + a % 2, 8, stride=4), :] for part in range(2)))
        values = butterflies(values, False)
        for k in range(RADIX):
            re, im = values[k]
            c, s = twiddle[k : k + 1, :], twiddle[RADIX + k : RADIX + k + 1, :]
            ure[transposed(o, k), :] = re * c + im * s
            uim[transposed(o, k), :] = im * c - re * s
        rows = slice(128 * o, 128 * o + 128)
        result = product(jnp.concatenate([ure[rows, :], uim[rows, :]], axis=1), matrix[...])
        spec[rows, :] = result
        for part in range(2):
            lanes = slice(part * LANES, (part + 1) * LANES)
            for i in range(8):
                r = jnp.concatenate([result[h * 64 + i * 8 : h * 64 + i * 8 + 8, lanes] for h in range(2)], axis=0)
                for way in range(2):
                    share = weights[way, 8 * o + i] * r
                    now = alone_ends[way][part]
                    alone_ends[way][part] = share if now is None else now + share

    def rhs(i, part):
        lanes = slice(part * LANES, (part + 1) * LANES)
        at = [(i // 8) * 128 + h * 64 + (i % 8) * 8 for h in range(2)]
        return jnp.concatenate([spec[n : n + 8, lanes] for n in at], axis=0)

    def half(ref, q, h, rows):
        return ref.at[q, pl.ds(h * rows, rows)]

    for h in range(2):
        for way in range(2):
            for part in range(2):
                at = h * 32 + (2 * way + part) * 8
                raw[xi, at : at + 8, :] = alone_ends[way][part][8 * h : 8 * h + 8, :]
        for q in x_peers:
            remote(half(raw, xi, h, 32), half(raw, xi, h, 32), send_sem.at[3], crossed.at[h], at_x(q)).start()

    for slot in range(4):
        for k in range(4):
            chain[slot, k] = jnp.zeros_like(one) if k in (1, 2) else one

    def next_block(x, shift):
        return tuple(pltpu.roll(v, 8 - shift, 0) for v in x)

    @pl.loop(0, NZ // 2)
    def _(n):
        pair = (lax.rem(zi + n + 1, NZ), lax.rem(zi + NZ - 1 - n, NZ))
        ways = [(q > zi).astype(jnp.int32) for q in pair]

        def arrive(q):
            there = coef.at[pl.ds(q * NXP, NXP)]
            remote(there, there, send_sem.at[2], czr_sem.at[q], at_z(q)).wait_recv()

        arrive(pair[0])

        @pl.when(n < NZ // 2 - 1)
        def _():
            arrive(pair[1])

        def keep_groups(k, values):
            for shift in (1, 2):
                later = next_block(values, shift)
                values = times(later[:4], values[:4]) + (later[4] * values[4],)
            values = scaled(values)
            for m, v in enumerate(values):
                for g in range(2):
                    groups[pair[g], m, k : k + 1, :] = v[NXP * g : NXP * g + 1, :]

        blocks = [q * NXP + jnp.where(w == 0, j, NXP - 1 - j) for q, w in zip(pair, ways) for j in range(NXP)]
        block_products(blocks, ways, keep_groups)

        def join(g):
            far = ways[g] != 1 - g
            slot = ways[g] + 2 * far.astype(jnp.int32)
            whole = tuple(groups[pair[g], k] for k in range(4))
            old = tuple(chain[slot, k] for k in range(4))
            outer = tuple(jnp.where(far, w, o) for w, o in zip(whole, old))
            inner = tuple(jnp.where(far, o, w) for w, o in zip(whole, old))
            for k, v in enumerate(scaled(times(outer, inner))):
                chain[slot, k] = v

        join(0)

        @pl.when(n < NZ // 2 - 1)
        def _():
            join(1)

    enter = []
    for way in range(2):
        top, bottom = chain[way + 2, 1], chain[way + 2, 3]
        enter.append((chain[way, 0] * top + chain[way, 1] * bottom) / (chain[way, 2] * top + chain[way, 3] * bottom))
    for j in range(NXP):
        for way in range(2):
            t = j if way == 0 else NXP - 1 - j
            g = enter[way]
            a, b, c, d, scale = [own_products[n, pl.ds(NXP * way + t, RADIX, stride=8), :] for n in range(5)]
            inv = 1.0 / (c * g + d)
            gin[way, t] = mirrored(g)
            abuf[way, t] = mirrored(scale * inv)
            enter[way] = (a * g + b) * inv

    entering = [[[], []], [[], []]]
    for h in range(2):
        part_modes = slice(8 * h, 8 * h + 8)
        wait_for(raw.at[pl.ds(0, NXP - 1), pl.ds(0, 32)], crossed.at[h])
        for way, order in enumerate((range(NXP), range(NXP - 1, -1, -1))):
            none = jnp.zeros((8, LANES), jnp.float32)
            run, mine = [none] * 2, [none] * 2
            for j in order:
                here = xi == j
                a = abuf[way, j, part_modes, :]
                ae = a * (1.0 - gin[way, j, part_modes, :])
                for part in range(2):
                    end, start = [raw[j, n : n + 8, :] for n in (
                        h * 32 + (2 * way + part) * 8, h * 32 + (2 - 2 * way + part) * 8)]
                    mine[part] = jnp.where(here, run[part], mine[part])
                    run[part] = a * run[part] + (end + ae * start)
            for part in range(2):
                at = h * 16 + part * 8
                gz[way, at : at + 8, :] = run[part]
                entering[way][part].append(mine[part])
        for q in z_peers:
            which = jnp.where(q > zi, 0, 1)
            remote(half(gz, which, h, 16), half(zrecv, zi, h, 16), send_sem.at[4], crossed.at[2 + h], at_z(q)).start()
    entering = [[jnp.concatenate(halves, axis=0) for halves in way] for way in entering]

    gbuf[...] = jnp.zeros_like(gbuf)

    @pl.loop(0, NZ - 1)
    def _(n):
        way = (n >= zi).astype(jnp.int32)
        q = jnp.where(n < zi, n, NZ - 1 - (n - zi))
        g = gbuf[way]
        inv = 1.0 / (groups[q, 2] * g + groups[q, 3])
        gbuf[way] = (groups[q, 0] * g + groups[q, 1]) * inv
        wbuf[q] = groups[q, 4] * inv

    def below(n, run):
        q = zi - 1 - n
        a = wbuf[q]
        wbuf[q] = mirrored(run)
        return run * a

    lax.fori_loop(0, zi, below, one)

    def above(n, run):
        q = zi + 1 + n
        a = wbuf[q]
        wbuf[q] = mirrored(run)
        return run * a

    lax.fori_loop(0, NZ - 1 - zi, above, one)
    pre, post = one, one
    for j in range(NXP):
        pre = pre * jnp.where(j < xi, abuf[0, j], 1.0)
        post = post * jnp.where(j > xi, abuf[1, j], 1.0)

    g_end = pivots(range(ROWS), low, upp, gin[0, xi], factors, 0)
    h_in = gin[1, xi]
    scale = 1.0 / (g_end + h_in * factors[2, ROWS - 1])

    for part in range(2):
        y = entering[0][part]
        for i in range(ROWS):
            y = factors[0, i] * y - factors[1, i] * rhs(i, part)
            known[part, i] = y
    reply = pre
    for i in range(ROWS):
        reply = factors[0, i] * reply
        known[2, i] = reply
    last_factor = factors[2, ROWS - 1]
    state = [(last_factor * entering[1][part] + known[part, ROWS - 1]) * scale for part in range(2)]
    state += [known[2, ROWS - 1] * scale, last_factor * scale * post]
    for i in range(ROWS - 1, -1, -1):
        if i < ROWS - 1:
            e = factors[2, i]
            state = [e * state[n] + known[n, i] for n in range(3)] + [e * state[3]]
        for n in range(4):
            known[n, i] = state[n]

    brought = [[], []]
    for h in range(2):
        wait_for(zrecv.at[pl.ds(0, NZ - 1), pl.ds(0, 16)], crossed.at[2 + h])
        none = jnp.zeros((8, LANES), jnp.float32)
        sums = [[none] * 2, [none] * 2]
        for q in z_peers:
            lower_side = q < zi
            w = wbuf[q, 8 * h : 8 * h + 8, :]
            wy = jnp.where(lower_side, w, 0.0)
            wz = jnp.where(lower_side, 0.0, w)
            for part in range(2):
                v = zrecv[q, h * 16 + part * 8 : h * 16 + part * 8 + 8, :]
                sums[0][part] = sums[0][part] + wy * v
                sums[1][part] = sums[1][part] + wz * v
        brought[0].append(sums[0])
        brought[1].append(sums[1])
    sy, sz = [[jnp.concatenate([side[0][part], side[1][part]], axis=0) for part in range(2)] for side in brought]

    for i in range(ROWS):
        for part, ref in enumerate((ure, uim)):
            x = known[part, i] + (known[2, i] * sy[part] + known[3, i] * sz[part])
            for h in range(2):
                at = (i // 8) * 128 + h * 64 + (i % 8) * 8
                ref[at : at + 8, :] = x[8 * h : 8 * h + 8, :]
    back = product(jnp.concatenate([uim[...], ure[...]], axis=1), matrix[...])
    uim[...] = back[:, :LANES]
    ure[...] = back[:, LANES:]
    for o in range(2):
        values = []
        for k in range(RADIX):
            re = ure[transposed(o, k), :]
            im = uim[transposed(o, k), :]
            c = twiddle[k : k + 1, :] * (1.0 / NX)
            s = twiddle[RADIX + k : RADIX + k + 1, :] * (1.0 / NX)
            values.append((re * c - im * s, im * c + re * s))
        values = butterflies(values, True)
        for a in range(RADIX):
            for part in range(2):
                obuf[a // 2, pl.ds(32 * o + 2 * part + a % 2, 8, stride=4), :] = values[a][part]
        for q in gx_peers:
            remote(octet(obuf, q, o), octet(fbuf, gx, o), send_sem.at[5], arrived.at[2 + o], at_gx(q)).start()
    own = pltpu.make_async_copy(obuf.at[gx], fbuf.at[gx], load_sem.at[0])
    own.start()
    wait_for(sbuf.at[pl.ds(0, PLANES - 1)], send_sem.at[0])
    wait_for(coef.at[pl.ds(0, NXP - 1)], send_sem.at[1])
    wait_for(coef.at[pl.ds(0, NXP * (NZ - 1))], send_sem.at[2])
    wait_for(raw.at[pl.ds(0, NXP - 1)], send_sem.at[3])
    wait_for(zrecv.at[pl.ds(0, NZ - 1)], send_sem.at[4])
    own.wait()
    wait_for(obuf.at[pl.ds(0, PLANES - 1)], send_sem.at[5])
    for o in range(2):
        wait_for_octet(fbuf, arrived.at[2 + o])


def assemble(fbuf, out, held, sem):
    count = 4 * ROWS // PARTS
    copies = []
    for n in range(PARTS):
        for q in range(PLANES):
            held[pl.ds(n * count * PLANES + q, count, stride=PLANES), :] = fbuf[q, n * count : (n + 1) * count, :]
        rows = pl.ds(n * count * PLANES, count * PLANES)
        copies.append(pltpu.make_async_copy(held.at[rows], out.at[rows], sem.at[n]))
        copies[-1].start()
    for copy in copies:
        copy.wait()


def local(source, lower, upper, span):
    matrix, twiddle = transform_constants()
    f32 = jnp.float32
    dma = pltpu.SemaphoreType.DMA
    vmem = lambda *shape: pltpu.VMEM(shape, f32)
    smem = lambda *shape: pltpu.SMEM(shape, f32)
    any_spec = pl.BlockSpec(memory_space=pl.ANY)
    shape = source.shape
    source = source.reshape(ROWS, 2, PLANES, 2, LANES).transpose(0, 1, 3, 2, 4).reshape(4 * ROWS * PLANES, LANES)
    planes = pl.pallas_call(
        kernel,
        out_shape=jax.ShapeDtypeStruct((PLANES, 64, LANES), f32),
        in_specs=[pl.BlockSpec(memory_space=pltpu.HBM)] * 6,
        out_specs=any_spec,
        scratch_shapes=[
            vmem(4 * ROWS * PLANES, LANES), vmem(PLANES, 64, LANES), vmem(PLANES, 64, LANES),
            vmem(256, LANES), vmem(256, LANES), vmem(256, 256),
            pltpu.VMEM((6 * 256, 256), jnp.bfloat16), vmem(2 * RADIX, LANES),
            smem(ROWS), smem(ROWS), smem(PLANES),
            vmem(BLOCKS, 1, LANES), vmem(4 * ROWS, 8, LANES), vmem(RADIX, LANES), vmem(5, 8 * RADIX, LANES),
            vmem(NZ, 5, RADIX, LANES), vmem(2, NXP, RADIX, LANES), vmem(NZ, RADIX, LANES),
            vmem(2, RADIX, LANES), vmem(2, NXP, RADIX, LANES), vmem(4, 4, RADIX, LANES),
            vmem(4, ROWS, RADIX, LANES), vmem(2, ROWS, RADIX, LANES), vmem(3, ROWS, RADIX, LANES),
            vmem(4, ROWS, RADIX, LANES),
            vmem(NXP, 64, LANES), vmem(2, 32, LANES), vmem(NZ, 32, LANES), vmem(PLANES, 64, LANES),
            dma((6,)), dma((6,)), dma((4,)), dma((4,)), dma((NXP,)), dma((NZ,)),
            pltpu.SemaphoreType.REGULAR, pltpu.SemaphoreType.REGULAR,
        ],
        compiler_params=pltpu.CompilerParams(
            collective_id=0, has_side_effects=True, vmem_limit_bytes=16 * 1024 * 1024),
    )(*[pltpu.with_memory_space_constraint(x, pltpu.HBM)
        for x in (source, lower, upper, span, jnp.asarray(matrix), jnp.asarray(twiddle))])
    result = pl.pallas_call(
        assemble,
        out_shape=jax.ShapeDtypeStruct((ROWS * 4 * PLANES, LANES), f32),
        in_specs=[pl.BlockSpec(memory_space=pltpu.VMEM)],
        out_specs=pl.BlockSpec(memory_space=pltpu.HBM),
        scratch_shapes=[vmem(ROWS * 4 * PLANES, LANES), dma((PARTS,))],
        compiler_params=pltpu.CompilerParams(vmem_limit_bytes=4 * 1024 * 1024),
    )(planes)
    result = result.reshape(ROWS, 2, 2, PLANES, LANES)
    return result.transpose(0, 1, 3, 2, 4).reshape(shape)


def solution(mesh):
    in_specs = (P("gy", None, None, "gx"), P("gy"), P("gy"), P())
    out_specs = P("gy", None, None, "gx")
    return jax.shard_map(local, mesh=mesh, in_specs=in_specs, out_specs=out_specs, check_vma=False)
```

```python
import math

import jax
import jax.numpy as jnp
import ml_dtypes
import numpy as np
from jax import lax
from jax.experimental import pallas as pl
from jax.experimental.pallas import tpu as pltpu
from jax.sharding import PartitionSpec as P

MESH = pl.DeviceIdType.MESH

ROWS = 16
PLANES = 8
NX = 2048
LANES = 128
RADIX = 16
NZ = 8
NXP = 4
BLOCKS = NZ * NXP
HALF = RADIX // 2 + 1
PARTS = 4


def transform_constants():
    lanes = np.arange(LANES)
    angle = 2.0 * np.pi * (np.outer(lanes, lanes) % LANES) / LANES
    c, s = np.cos(angle), np.sin(angle)
    matrix = np.block([[c, -s], [s, c]]).astype(np.float32)
    terms, rest = [], matrix
    for _ in range(3):
        terms.append(rest.astype(ml_dtypes.bfloat16))
        rest = rest - terms[-1].astype(np.float32)
    matrix = np.concatenate([terms[0], terms[1], terms[2], terms[0], terms[1], terms[0]])
    twist = 2.0 * np.pi * (np.outer(np.arange(RADIX), lanes) % NX) / NX
    twiddle = np.concatenate([np.cos(twist), np.sin(twist)]).astype(np.float32)
    return matrix, twiddle


def rotated(value, index, size, inverse):
    re, im = value
    index = index % size
    if index == 0:
        return value
    if 4 * index == size:
        return (-im, re) if inverse else (im, -re)
    c = math.cos(2.0 * math.pi * index / size)
    s = math.sin(2.0 * math.pi * index / size)
    if not inverse:
        s = -s
    return (re * c - im * s, re * s + im * c)


def butterflies(values, inverse):
    size = len(values)
    if size == 1:
        return values
    even = butterflies(values[0::2], inverse)
    odd = butterflies(values[1::2], inverse)
    odd = [rotated(o, k, size, inverse) for k, o in enumerate(odd)]
    low = [(e[0] + o[0], e[1] + o[1]) for e, o in zip(even, odd)]
    high = [(e[0] - o[0], e[1] - o[1]) for e, o in zip(even, odd)]
    return low + high


def product(x, matrix):
    high = x.astype(jnp.bfloat16)
    rest = x - high.astype(jnp.float32)
    middle = rest.astype(jnp.bfloat16)
    low = (rest - middle.astype(jnp.float32)).astype(jnp.bfloat16)
    terms = jnp.concatenate([high, high, high, middle, middle, low], axis=1)
    return jnp.dot(terms, matrix, preferred_element_type=jnp.float32)


def times(x, y):
    a, b, c, d = x
    e, f, g, h = y
    return (a * e + b * g, a * f + b * h, c * e + d * g, c * f + d * h)


def scaled(x):
    r = pl.reciprocal(x[2] + x[3], approx=True)
    return tuple(v * r for v in x)


def mirrored(x):
    sub = lax.broadcasted_iota(jnp.int32, (8, LANES), 0)
    lane = lax.broadcasted_iota(jnp.int32, (8, LANES), 1)
    top = x[0:8, :]
    turned = jnp.take_along_axis(top, LANES - 1 - lane, axis=1)
    turned = jnp.take_along_axis(turned, (8 - sub) % 8, axis=0)
    return jnp.concatenate([top, jnp.where(sub == 0, x[8:16, :], turned)], axis=0)


def transposed(o, k):
    return pl.ds(o * 128 + (k // 8) * 64 + k % 8, 8, stride=8)


def kernel(
    source, lower_hbm, upper_hbm, span_hbm, matrix_hbm, twiddle_hbm, fbuf,
    src, sbuf, rbuf, ure, uim, spec, matrix, twiddle, lower, upper, span,
    coef, splats, kbuf, own_products, groups, abuf, wbuf, gbuf, gin, chain, alone, weights, factors, known,
    raw, gz, zrecv, obuf,
    load_sem, send_sem, crossed, arrived, cxr_sem, czr_sem, near_sem, far_sem,
):
    gx = lax.axis_index("gx")
    gy = lax.axis_index("gy")
    zi = gy // NXP
    xi = gy % NXP
    base = zi * NXP

    chip, core = gx // 2, gx % 2
    gx_peers = [lax.rem(chip + d, PLANES // 2) * 2 + lax.rem(core + c, 2)
                for d, c in ((2, 0), (2, 1), (1, 0), (3, 0), (1, 1), (3, 1), (0, 1))]
    x_peers = [lax.rem(xi + d, NXP) for d in (2, 1, 3)]
    z_peers = [lax.rem(zi + d, NZ) for d in (4, 3, 5, 2, 6, 1, 7)]

    def at_gx(q):
        return (q, gy)

    def at_x(q):
        return (gx, base + q)

    def at_z(q):
        return (gx, q * NXP + xi)

    z_near = [lax.rem(zi + d, NZ) for d in (1, NZ - 1)]
    z_far = [lax.rem(zi + d, NZ) for d in (2, NZ - 2)]
    near = [at_gx(q) for q in gx_peers] + [at_x(q) for q in x_peers] + [at_z(q) for q in z_near]
    loads = [pltpu.make_async_copy(there, here, load_sem.at[n]) for n, (there, here) in enumerate((
        (source, src), (lower_hbm, lower), (upper_hbm, upper), (span_hbm, span),
        (twiddle_hbm, twiddle), (matrix_hbm, matrix)))]
    loads[0].start()
    barrier = pltpu.get_barrier_semaphore()
    for device in near:
        pl.semaphore_signal(barrier, inc=1, device_id=device, device_id_type=MESH)
    for load in loads[1:]:
        load.start()

    loads[0].wait()
    for q in range(PLANES):
        sbuf[q] = src[pl.ds(q, 4 * ROWS, stride=PLANES), :]

    for load in loads[1:4]:
        load.wait()
    first, last = gy == 0, gy == BLOCKS - 1
    low = [lower[i] for i in range(ROWS)]
    upp = [upper[i] for i in range(ROWS)]
    low[0] = jnp.where(first, 0.0, low[0])
    upp[-1] = jnp.where(last, 0.0, upp[-1])
    sums, lost = [], []
    for l, u in zip(low, upp):
        total = l + u
        rest = total - l
        sums.append(total)
        lost.append(-((l - (total - rest)) + (u - rest)))
    lane = lax.broadcasted_iota(jnp.int32, (1, LANES), 1)
    row = jnp.zeros((1, LANES), jnp.float32)
    for i, value in enumerate(low + upp + sums + lost + upp[::-1] + low[::-1] + sums[::-1] + lost[::-1]):
        row = jnp.where(lane == i, value, row)
    coef[gy] = row

    pl.semaphore_wait(barrier, len(near))

    def remote(src_ref, dst_ref, send, recv, device):
        return pltpu.make_async_remote_copy(
            src_ref=src_ref, dst_ref=dst_ref, send_sem=send, recv_sem=recv,
            device_id=device, device_id_type=MESH)

    coef_x = [remote(coef.at[gy], coef.at[gy], send_sem.at[1], cxr_sem.at[xi], at_x(q)) for q in x_peers]
    for copy in coef_x:
        copy.start()

    for q in z_near:
        pl.semaphore_signal(near_sem, inc=1, device_id=at_z(q), device_id_type=MESH)

    def octet(ref, q, o):
        return ref.at[q, pl.ds(32 * o, 32)]

    for o in range(2):
        for q in gx_peers:
            remote(octet(sbuf, q, o), octet(rbuf, gx, o), send_sem.at[0], arrived.at[o], at_gx(q)).start()
    rbuf[gx] = sbuf[gx]


    k1 = lax.broadcasted_iota(jnp.int32, (RADIX, LANES), 0)
    k2 = lax.broadcasted_iota(jnp.int32, (RADIX, LANES), 1)
    mode = k1 + RADIX * k2
    signed = jnp.where(mode < NX // 2, mode, mode - NX).astype(jnp.float32)
    wave = 2.0 * signed / NX
    kappa = span[gx] * span[gx] + wave * wave
    one = jnp.ones((RADIX, LANES), jnp.float32)

    def pivots(order, ahead, behind, g, keep, into):
        for i in order:
            l, u = ahead[i], behind[i]
            s = (((sums[i] + kappa) - sums[i]) + lost[i]) + l * g
            inv = 1.0 / (u + s)
            g = s * inv
            keep[into, i] = l * inv
            keep[into + 1, i] = inv
            if keep is factors:
                keep[into + 2, i] = u * inv
        return g

    pivots(range(ROWS), low, upp, one, alone, 0)
    pivots(range(ROWS - 1, -1, -1), upp, low, one, alone, 2)
    for way, order in enumerate((range(ROWS - 1, -1, -1), range(ROWS))):
        run = -one
        for i in order:
            weights[way, i] = run * alone[2 * way + 1, i]
            run = run * alone[2 * way, i]

    pl.semaphore_wait(near_sem, 2)
    for q in z_far:
        pl.semaphore_signal(far_sem, inc=1, device_id=at_z(q), device_id_type=MESH)

    for q in x_peers:
        there = coef.at[base + q]
        remote(there, there, send_sem.at[1], cxr_sem.at[q], at_x(q)).wait_recv()
    pl.semaphore_wait(far_sem, 2)
    group = coef.at[pl.ds(base, NXP)]
    coef_z = [remote(group, group, send_sem.at[2], czr_sem.at[zi], at_z(q)) for q in z_peers]
    for copy in coef_z:
        copy.start()

    kbuf[...] = kappa

    def block_products(blocks, ways, finish, modes=None):
        rows = jnp.concatenate([coef[t] for t in blocks], axis=0)
        sub = lax.broadcasted_iota(jnp.int32, (8, LANES), 0)
        turn = jnp.where(sub < NXP, ways[0], ways[1]) == 1
        rows = jnp.where(turn, pltpu.roll(rows, LANES // 2, 1), rows)
        scale = None
        for k in range(4 * ROWS):
            one = jnp.broadcast_to(rows[:, k : k + 1], (8, LANES))
            splats[k] = one
            if k < ROWS:
                scale = one if scale is None else scale * one
        for group in modes or [[(n, n) for n in range(k, k + 3)] for k in range(0, HALF, 3)]:
            waves = []
            for n, m in group:
                waves.append(jnp.broadcast_to(kbuf[n : n + 1, :], (8, LANES)))
                if m != n:
                    other = jnp.broadcast_to(kbuf[m : m + 1, :], (8, LANES))
                    waves[-1] = jnp.where(sub < NXP, waves[-1], other)
            state = [None] * len(group)
            for i in range(ROWS):
                l, u, total, gained = [splats[n * ROWS + i] for n in range(4)]
                for n in range(len(group)):
                    rounded = ((total + waves[n]) - total) + gained
                    if i == 0:
                        state[n] = (l, rounded, l, u + rounded)
                        continue
                    a, b, c, d = state[n]
                    a = l * a + rounded * c
                    b = l * b + rounded * d
                    state[n] = (a, b, a + u * c, b + u * d)
            for n, parts in enumerate(group):
                finish(parts, scaled(state[n] + (scale,)))

    def keep_own(parts, values):
        for n, v in enumerate(values):
            own_products[n, 8 * parts[0] : 8 * parts[0] + 8, :] = v

    block_products([base + j for j in range(NXP)] * 2, (0, 1), keep_own)

    def wait_for(ref, sem):
        pltpu.make_async_copy(ref, ref, sem).wait()

    def wait_for_octet(ref, sem):
        wait_for(ref.at[pl.ds(0, PLANES - 1), pl.ds(0, 32)], sem)

    alone_ends = [[None] * 2, [None] * 2]
    for o in range(2):
        wait_for_octet(rbuf, arrived.at[o])
        if o == 0:
            loads[4].wait()
            loads[5].wait()
        values = []
        for a in range(RADIX):
            values.append(tuple(rbuf[a // 2, pl.ds(32 * o + 2 * part + a % 2, 8, stride=4), :] for part in range(2)))
        values = butterflies(values, False)
        for k in range(RADIX):
            re, im = values[k]
            c, s = twiddle[k : k + 1, :], twiddle[RADIX + k : RADIX + k + 1, :]
            ure[transposed(o, k), :] = re * c + im * s
            uim[transposed(o, k), :] = im * c - re * s
        rows = slice(128 * o, 128 * o + 128)
        result = product(jnp.concatenate([ure[rows, :], uim[rows, :]], axis=1), matrix[...])
        spec[rows, :] = result
        for part in range(2):
            lanes = slice(part * LANES, (part + 1) * LANES)
            for i in range(8):
                r = jnp.concatenate([result[h * 64 + i * 8 : h * 64 + i * 8 + 8, lanes] for h in range(2)], axis=0)
                for way in range(2):
                    share = weights[way, 8 * o + i] * r
                    now = alone_ends[way][part]
                    alone_ends[way][part] = share if now is None else now + share

    def rhs(i, part):
        lanes = slice(part * LANES, (part + 1) * LANES)
        at = [(i // 8) * 128 + h * 64 + (i % 8) * 8 for h in range(2)]
        return jnp.concatenate([spec[n : n + 8, lanes] for n in at], axis=0)

    def half(ref, q, h, rows):
        return ref.at[q, pl.ds(h * rows, rows)]

    for h in range(2):
        for way in range(2):
            for part in range(2):
                at = h * 32 + (2 * way + part) * 8
                raw[xi, at : at + 8, :] = alone_ends[way][part][8 * h : 8 * h + 8, :]
        for q in x_peers:
            remote(half(raw, xi, h, 32), half(raw, xi, h, 32), send_sem.at[3], crossed.at[h], at_x(q)).start()

    for slot in range(4):
        for k in range(4):
            chain[slot, k] = jnp.zeros_like(one) if k in (1, 2) else one

    def next_block(x, shift):
        return tuple(pltpu.roll(v, 8 - shift, 0) for v in x)

    def arrive(q):
        there = coef.at[pl.ds(q * NXP, NXP)]
        remote(there, there, send_sem.at[2], czr_sem.at[q], at_z(q)).wait_recv()

    def keep_groups(pair):
        def keep(parts, values):
            for shift in (1, 2):
                later = next_block(values, shift)
                values = times(later[:4], values[:4]) + (later[4] * values[4],)
            values = scaled(values)
            for m, v in enumerate(values):
                for g in range(2):
                    groups[pair[g], m, parts[g] : parts[g] + 1, :] = v[NXP * g : NXP * g + 1, :]

        return keep

    def join(q, way, upward):
        far = way != int(upward)
        slot = way + 2 * far.astype(jnp.int32)
        whole = tuple(groups[q, k] for k in range(4))
        old = tuple(chain[slot, k] for k in range(4))
        outer = tuple(jnp.where(far, w, o) for w, o in zip(whole, old))
        inner = tuple(jnp.where(far, o, w) for w, o in zip(whole, old))
        for k, v in enumerate(scaled(times(outer, inner))):
            chain[slot, k] = v

    def in_order(q, way):
        return [q * NXP + jnp.where(way == 0, j, NXP - 1 - j) for j in range(NXP)]

    @pl.loop(0, NZ // 2 - 1)
    def _(n):
        pair = (lax.rem(zi + n + 1, NZ), lax.rem(zi + NZ - 1 - n, NZ))
        ways = [(q > zi).astype(jnp.int32) for q in pair]
        for q in pair:
            arrive(q)
        block_products(in_order(pair[0], ways[0]) + in_order(pair[1], ways[1]), ways, keep_groups(pair))
        for q, way, upward in zip(pair, ways, (True, False)):
            join(q, way, upward)

    across = lax.rem(zi + NZ // 2, NZ)
    way = (across > zi).astype(jnp.int32)
    arrive(across)
    block_products(in_order(across, way) * 2, (way, way), keep_groups((across, across)),
                   [[(0, 5), (1, 6), (2, 7)], [(3, 8), (4, 4)]])
    join(across, way, True)

    enter = []
    for way in range(2):
        top, bottom = chain[way + 2, 1], chain[way + 2, 3]
        enter.append((chain[way, 0] * top + chain[way, 1] * bottom) / (chain[way, 2] * top + chain[way, 3] * bottom))
    for j in range(NXP):
        for way in range(2):
            t = j if way == 0 else NXP - 1 - j
            g = enter[way]
            a, b, c, d, scale = [own_products[n, pl.ds(NXP * way + t, RADIX, stride=8), :] for n in range(5)]
            inv = 1.0 / (c * g + d)
            gin[way, t] = mirrored(g)
            abuf[way, t] = mirrored(scale * inv)
            enter[way] = (a * g + b) * inv

    entering = [[[], []], [[], []]]
    for h in range(2):
        part_modes = slice(8 * h, 8 * h + 8)
        wait_for(raw.at[pl.ds(0, NXP - 1), pl.ds(0, 32)], crossed.at[h])
        for way, order in enumerate((range(NXP), range(NXP - 1, -1, -1))):
            none = jnp.zeros((8, LANES), jnp.float32)
            run, mine = [none] * 2, [none] * 2
            for j in order:
                here = xi == j
                a = abuf[way, j, part_modes, :]
                ae = a * (1.0 - gin[way, j, part_modes, :])
                for part in range(2):
                    end, start = [raw[j, n : n + 8, :] for n in (
                        h * 32 + (2 * way + part) * 8, h * 32 + (2 - 2 * way + part) * 8)]
                    mine[part] = jnp.where(here, run[part], mine[part])
                    run[part] = a * run[part] + (end + ae * start)
            for part in range(2):
                at = h * 16 + part * 8
                gz[way, at : at + 8, :] = run[part]
                entering[way][part].append(mine[part])
        for q in z_peers:
            which = jnp.where(q > zi, 0, 1)
            remote(half(gz, which, h, 16), half(zrecv, zi, h, 16), send_sem.at[4], crossed.at[2 + h], at_z(q)).start()
    entering = [[jnp.concatenate(halves, axis=0) for halves in way] for way in entering]

    gbuf[...] = jnp.zeros_like(gbuf)

    @pl.loop(0, NZ - 1)
    def _(n):
        way = (n >= zi).astype(jnp.int32)
        q = jnp.where(n < zi, n, NZ - 1 - (n - zi))
        g = gbuf[way]
        inv = 1.0 / (groups[q, 2] * g + groups[q, 3])
        gbuf[way] = (groups[q, 0] * g + groups[q, 1]) * inv
        wbuf[q] = groups[q, 4] * inv

    def below(n, run):
        q = zi - 1 - n
        a = wbuf[q]
        wbuf[q] = mirrored(run)
        return run * a

    lax.fori_loop(0, zi, below, one)

    def above(n, run):
        q = zi + 1 + n
        a = wbuf[q]
        wbuf[q] = mirrored(run)
        return run * a

    lax.fori_loop(0, NZ - 1 - zi, above, one)
    pre, post = one, one
    for j in range(NXP):
        pre = pre * jnp.where(j < xi, abuf[0, j], 1.0)
        post = post * jnp.where(j > xi, abuf[1, j], 1.0)

    g_end = pivots(range(ROWS), low, upp, gin[0, xi], factors, 0)
    h_in = gin[1, xi]
    scale = 1.0 / (g_end + h_in * factors[2, ROWS - 1])

    for part in range(2):
        y = entering[0][part]
        for i in range(ROWS):
            y = factors[0, i] * y - factors[1, i] * rhs(i, part)
            known[part, i] = y
    reply = pre
    for i in range(ROWS):
        reply = factors[0, i] * reply
        known[2, i] = reply
    last_factor = factors[2, ROWS - 1]
    state = [(last_factor * entering[1][part] + known[part, ROWS - 1]) * scale for part in range(2)]
    state += [known[2, ROWS - 1] * scale, last_factor * scale * post]
    for i in range(ROWS - 1, -1, -1):
        if i < ROWS - 1:
            e = factors[2, i]
            state = [e * state[n] + known[n, i] for n in range(3)] + [e * state[3]]
        for n in range(4):
            known[n, i] = state[n]

    brought = [[], []]
    for h in range(2):
        wait_for(zrecv.at[pl.ds(0, NZ - 1), pl.ds(0, 16)], crossed.at[2 + h])
        none = jnp.zeros((8, LANES), jnp.float32)
        sums = [[none] * 2, [none] * 2]
        for q in z_peers:
            lower_side = q < zi
            w = wbuf[q, 8 * h : 8 * h + 8, :]
            wy = jnp.where(lower_side, w, 0.0)
            wz = jnp.where(lower_side, 0.0, w)
            for part in range(2):
                v = zrecv[q, h * 16 + part * 8 : h * 16 + part * 8 + 8, :]
                sums[0][part] = sums[0][part] + wy * v
                sums[1][part] = sums[1][part] + wz * v
        brought[0].append(sums[0])
        brought[1].append(sums[1])
    sy, sz = [[jnp.concatenate([side[0][part], side[1][part]], axis=0) for part in range(2)] for side in brought]

    for o in (1, 0):
        for i in range(8 * o, 8 * o + 8):
            for part, ref in enumerate((ure, uim)):
                x = known[part, i] + (known[2, i] * sy[part] + known[3, i] * sz[part])
                for h in range(2):
                    at = o * 128 + h * 64 + (i % 8) * 8
                    ref[at : at + 8, :] = x[8 * h : 8 * h + 8, :]
        rows = slice(128 * o, 128 * o + 128)
        back = product(jnp.concatenate([uim[rows, :], ure[rows, :]], axis=1), matrix[...])
        uim[rows, :] = back[:, :LANES]
        ure[rows, :] = back[:, LANES:]
        values = []
        for k in range(RADIX):
            re = ure[transposed(o, k), :]
            im = uim[transposed(o, k), :]
            c = twiddle[k : k + 1, :] * (1.0 / NX)
            s = twiddle[RADIX + k : RADIX + k + 1, :] * (1.0 / NX)
            values.append((re * c - im * s, im * c + re * s))
        values = butterflies(values, True)
        for a in range(RADIX):
            for part in range(2):
                obuf[a // 2, pl.ds(32 * o + 2 * part + a % 2, 8, stride=4), :] = values[a][part]
        for q in gx_peers:
            remote(octet(obuf, q, o), octet(fbuf, gx, o), send_sem.at[5], arrived.at[2 + o], at_gx(q)).start()
    own = pltpu.make_async_copy(obuf.at[gx], fbuf.at[gx], load_sem.at[0])
    own.start()
    wait_for(sbuf.at[pl.ds(0, PLANES - 1)], send_sem.at[0])
    wait_for(coef.at[pl.ds(0, NXP - 1)], send_sem.at[1])
    wait_for(coef.at[pl.ds(0, NXP * (NZ - 1))], send_sem.at[2])
    wait_for(raw.at[pl.ds(0, NXP - 1)], send_sem.at[3])
    wait_for(zrecv.at[pl.ds(0, NZ - 1)], send_sem.at[4])
    own.wait()
    wait_for(obuf.at[pl.ds(0, PLANES - 1)], send_sem.at[5])
    for o in range(2):
        wait_for_octet(fbuf, arrived.at[2 + o])


def assemble(fbuf, out, held, sem):
    count = 4 * ROWS // PARTS
    copies = []
    for n in range(PARTS):
        for q in range(PLANES):
            held[pl.ds(n * count * PLANES + q, count, stride=PLANES), :] = fbuf[q, n * count : (n + 1) * count, :]
        rows = pl.ds(n * count * PLANES, count * PLANES)
        copies.append(pltpu.make_async_copy(held.at[rows], out.at[rows], sem.at[n]))
        copies[-1].start()
    for copy in copies:
        copy.wait()


def local(source, lower, upper, span):
    matrix, twiddle = transform_constants()
    f32 = jnp.float32
    dma = pltpu.SemaphoreType.DMA
    vmem = lambda *shape: pltpu.VMEM(shape, f32)
    smem = lambda *shape: pltpu.SMEM(shape, f32)
    any_spec = pl.BlockSpec(memory_space=pl.ANY)
    shape = source.shape
    source = source.reshape(ROWS, 2, PLANES, 2, LANES).transpose(0, 1, 3, 2, 4).reshape(4 * ROWS * PLANES, LANES)
    planes = pl.pallas_call(
        kernel,
        out_shape=jax.ShapeDtypeStruct((PLANES, 64, LANES), f32),
        in_specs=[pl.BlockSpec(memory_space=pltpu.HBM)] * 6,
        out_specs=any_spec,
        scratch_shapes=[
            vmem(4 * ROWS * PLANES, LANES), vmem(PLANES, 64, LANES), vmem(PLANES, 64, LANES),
            vmem(256, LANES), vmem(256, LANES), vmem(256, 256),
            pltpu.VMEM((6 * 256, 256), jnp.bfloat16), vmem(2 * RADIX, LANES),
            smem(ROWS), smem(ROWS), smem(PLANES),
            vmem(BLOCKS, 1, LANES), vmem(4 * ROWS, 8, LANES), vmem(RADIX, LANES), vmem(5, 8 * RADIX, LANES),
            vmem(NZ, 5, RADIX, LANES), vmem(2, NXP, RADIX, LANES), vmem(NZ, RADIX, LANES),
            vmem(2, RADIX, LANES), vmem(2, NXP, RADIX, LANES), vmem(4, 4, RADIX, LANES),
            vmem(4, ROWS, RADIX, LANES), vmem(2, ROWS, RADIX, LANES), vmem(3, ROWS, RADIX, LANES),
            vmem(4, ROWS, RADIX, LANES),
            vmem(NXP, 64, LANES), vmem(2, 32, LANES), vmem(NZ, 32, LANES), vmem(PLANES, 64, LANES),
            dma((6,)), dma((6,)), dma((4,)), dma((4,)), dma((NXP,)), dma((NZ,)),
            pltpu.SemaphoreType.REGULAR, pltpu.SemaphoreType.REGULAR,
        ],
        compiler_params=pltpu.CompilerParams(
            collective_id=0, has_side_effects=True, vmem_limit_bytes=16 * 1024 * 1024),
    )(*[pltpu.with_memory_space_constraint(x, pltpu.HBM)
        for x in (source, lower, upper, span, jnp.asarray(matrix), jnp.asarray(twiddle))])
    result = pl.pallas_call(
        assemble,
        out_shape=jax.ShapeDtypeStruct((ROWS * 4 * PLANES, LANES), f32),
        in_specs=[pl.BlockSpec(memory_space=pltpu.VMEM)],
        out_specs=pl.BlockSpec(memory_space=pltpu.HBM),
        scratch_shapes=[vmem(ROWS * 4 * PLANES, LANES), dma((PARTS,))],
        compiler_params=pltpu.CompilerParams(vmem_limit_bytes=4 * 1024 * 1024),
    )(planes)
    result = result.reshape(ROWS, 2, 2, PLANES, LANES)
    return result.transpose(0, 1, 3, 2, 4).reshape(shape)


def solution(mesh):
    in_specs = (P("gy", None, None, "gx"), P("gy"), P("gy"), P())
    out_specs = P("gy", None, None, "gx")
    return jax.shard_map(local, mesh=mesh, in_specs=in_specs, out_specs=out_specs, check_vma=False)
```

```python
import math

import jax
import jax.numpy as jnp
import ml_dtypes
import numpy as np
from jax import lax
from jax.experimental import pallas as pl
from jax.experimental.pallas import tpu as pltpu
from jax.sharding import PartitionSpec as P

MESH = pl.DeviceIdType.MESH

ROWS = 16
PLANES = 8
NX = 2048
LANES = 128
RADIX = 16
NZ = 8
NXP = 4
BLOCKS = NZ * NXP
HALF = RADIX // 2 + 1
PARTS = 4


def transform_constants():
    lanes = np.arange(LANES)
    angle = 2.0 * np.pi * (np.outer(lanes, lanes) % LANES) / LANES
    c, s = np.cos(angle), np.sin(angle)
    matrix = np.block([[c, -s], [s, c]]).astype(np.float32)
    terms, rest = [], matrix
    for _ in range(3):
        terms.append(rest.astype(ml_dtypes.bfloat16))
        rest = rest - terms[-1].astype(np.float32)
    matrix = np.concatenate([terms[0], terms[1], terms[2], terms[0], terms[1], terms[0]])
    twist = 2.0 * np.pi * (np.outer(np.arange(RADIX), lanes) % NX) / NX
    twiddle = np.concatenate([np.cos(twist), np.sin(twist)]).astype(np.float32)
    return matrix, twiddle


def rotated(value, index, size, inverse):
    re, im = value
    index = index % size
    if index == 0:
        return value
    if 4 * index == size:
        return (-im, re) if inverse else (im, -re)
    c = math.cos(2.0 * math.pi * index / size)
    s = math.sin(2.0 * math.pi * index / size)
    if not inverse:
        s = -s
    return (re * c - im * s, re * s + im * c)


def butterflies(values, inverse):
    size = len(values)
    if size == 1:
        return values
    even = butterflies(values[0::2], inverse)
    odd = butterflies(values[1::2], inverse)
    odd = [rotated(o, k, size, inverse) for k, o in enumerate(odd)]
    low = [(e[0] + o[0], e[1] + o[1]) for e, o in zip(even, odd)]
    high = [(e[0] - o[0], e[1] - o[1]) for e, o in zip(even, odd)]
    return low + high


def product(x, matrix):
    high = x.astype(jnp.bfloat16)
    rest = x - high.astype(jnp.float32)
    middle = rest.astype(jnp.bfloat16)
    low = (rest - middle.astype(jnp.float32)).astype(jnp.bfloat16)
    terms = jnp.concatenate([high, high, high, middle, middle, low], axis=1)
    return jnp.dot(terms, matrix, preferred_element_type=jnp.float32)


def times(x, y):
    a, b, c, d = x
    e, f, g, h = y
    return (a * e + b * g, a * f + b * h, c * e + d * g, c * f + d * h)


def scaled(x):
    r = pl.reciprocal(x[2] + x[3], approx=True)
    return tuple(v * r for v in x)


def mirrored(x):
    sub = lax.broadcasted_iota(jnp.int32, (8, LANES), 0)
    lane = lax.broadcasted_iota(jnp.int32, (8, LANES), 1)
    top = x[0:8, :]
    turned = jnp.take_along_axis(top, LANES - 1 - lane, axis=1)
    turned = jnp.take_along_axis(turned, (8 - sub) % 8, axis=0)
    return jnp.concatenate([top, jnp.where(sub == 0, x[8:16, :], turned)], axis=0)


def transposed(o, k):
    return pl.ds(o * 128 + (k // 8) * 64 + k % 8, 8, stride=8)


def kernel(
    source, lower_hbm, upper_hbm, span_hbm, matrix_hbm, twiddle_hbm, fbuf,
    src, sbuf, rbuf, ure, uim, spec, matrix, twiddle, lower, upper, span,
    coef, splats, kbuf, own_products, groups, abuf, wbuf, gbuf, gin, chain, alone, weights, factors, known,
    raw, gz, zrecv, obuf,
    load_sem, send_sem, crossed, arrived, cxr_sem, czr_sem, near_sem, far_sem,
):
    gx = lax.axis_index("gx")
    gy = lax.axis_index("gy")
    zi = gy // NXP
    xi = gy % NXP
    base = zi * NXP

    chip, core = gx // 2, gx % 2
    gx_peers = [lax.rem(chip + d, PLANES // 2) * 2 + lax.rem(core + c, 2)
                for d, c in ((2, 0), (2, 1), (1, 0), (3, 0), (1, 1), (3, 1), (0, 1))]
    x_peers = [lax.rem(xi + d, NXP) for d in (2, 1, 3)]
    z_peers = [lax.rem(zi + d, NZ) for d in (4, 3, 5, 2, 6, 1, 7)]

    def at_gx(q):
        return (q, gy)

    def at_x(q):
        return (gx, base + q)

    def at_z(q):
        return (gx, q * NXP + xi)

    z_near = [lax.rem(zi + d, NZ) for d in (1, NZ - 1)]
    z_far = [lax.rem(zi + d, NZ) for d in (2, NZ - 2)]
    near = [at_gx(q) for q in gx_peers] + [at_x(q) for q in x_peers] + [at_z(q) for q in z_near]
    loads = [pltpu.make_async_copy(there, here, load_sem.at[n]) for n, (there, here) in enumerate((
        (source, src), (lower_hbm, lower), (upper_hbm, upper), (span_hbm, span),
        (twiddle_hbm, twiddle), (matrix_hbm, matrix)))]
    loads[0].start()
    barrier = pltpu.get_barrier_semaphore()
    for device in near:
        pl.semaphore_signal(barrier, inc=1, device_id=device, device_id_type=MESH)
    for load in loads[1:]:
        load.start()

    loads[0].wait()
    for q in range(PLANES):
        sbuf[q] = src[pl.ds(q, 4 * ROWS, stride=PLANES), :]

    for load in loads[1:4]:
        load.wait()
    first, last = gy == 0, gy == BLOCKS - 1
    low = [lower[i] for i in range(ROWS)]
    upp = [upper[i] for i in range(ROWS)]
    low[0] = jnp.where(first, 0.0, low[0])
    upp[-1] = jnp.where(last, 0.0, upp[-1])
    sums, lost = [], []
    for l, u in zip(low, upp):
        total = l + u
        rest = total - l
        sums.append(total)
        lost.append(-((l - (total - rest)) + (u - rest)))
    lane = lax.broadcasted_iota(jnp.int32, (1, LANES), 1)
    row = jnp.zeros((1, LANES), jnp.float32)
    for i, value in enumerate(low + upp + sums + lost + upp[::-1] + low[::-1] + sums[::-1] + lost[::-1]):
        row = jnp.where(lane == i, value, row)
    coef[gy] = row

    pl.semaphore_wait(barrier, len(near))

    def remote(src_ref, dst_ref, send, recv, device):
        return pltpu.make_async_remote_copy(
            src_ref=src_ref, dst_ref=dst_ref, send_sem=send, recv_sem=recv,
            device_id=device, device_id_type=MESH)

    coef_x = [remote(coef.at[gy], coef.at[gy], send_sem.at[1], cxr_sem.at[xi], at_x(q)) for q in x_peers]
    for copy in coef_x:
        copy.start()

    for q in z_near:
        pl.semaphore_signal(near_sem, inc=1, device_id=at_z(q), device_id_type=MESH)

    def octet(ref, q, o):
        return ref.at[q, pl.ds(32 * o, 32)]

    for some in (gx_peers[:2], gx_peers[2:6], gx_peers[6:]):
        for o in range(2):
            for q in some:
                remote(octet(sbuf, q, o), octet(rbuf, gx, o), send_sem.at[0], arrived.at[o], at_gx(q)).start()
    rbuf[gx] = sbuf[gx]


    k1 = lax.broadcasted_iota(jnp.int32, (RADIX, LANES), 0)
    k2 = lax.broadcasted_iota(jnp.int32, (RADIX, LANES), 1)
    mode = k1 + RADIX * k2
    signed = jnp.where(mode < NX // 2, mode, mode - NX).astype(jnp.float32)
    wave = 2.0 * signed / NX
    kappa = span[gx] * span[gx] + wave * wave
    one = jnp.ones((RADIX, LANES), jnp.float32)

    def pivots(order, ahead, behind, g, keep, into):
        for i in order:
            l, u = ahead[i], behind[i]
            s = (((sums[i] + kappa) - sums[i]) + lost[i]) + l * g
            inv = 1.0 / (u + s)
            g = s * inv
            keep[into, i] = l * inv
            keep[into + 1, i] = inv
            if keep is factors:
                keep[into + 2, i] = u * inv
        return g

    pivots(range(ROWS), low, upp, one, alone, 0)
    pivots(range(ROWS - 1, -1, -1), upp, low, one, alone, 2)
    for way, order in enumerate((range(ROWS - 1, -1, -1), range(ROWS))):
        run = -one
        for i in order:
            weights[way, i] = run * alone[2 * way + 1, i]
            run = run * alone[2 * way, i]

    pl.semaphore_wait(near_sem, 2)
    for q in z_far:
        pl.semaphore_signal(far_sem, inc=1, device_id=at_z(q), device_id_type=MESH)

    for q in x_peers:
        there = coef.at[base + q]
        remote(there, there, send_sem.at[1], cxr_sem.at[q], at_x(q)).wait_recv()
    pl.semaphore_wait(far_sem, 2)
    group = coef.at[pl.ds(base, NXP)]
    coef_z = [remote(group, group, send_sem.at[2], czr_sem.at[zi], at_z(q)) for q in z_peers]
    for copy in coef_z:
        copy.start()

    kbuf[...] = kappa

    def block_products(blocks, ways, finish, modes=None):
        rows = jnp.concatenate([coef[t] for t in blocks], axis=0)
        sub = lax.broadcasted_iota(jnp.int32, (8, LANES), 0)
        turn = jnp.where(sub < NXP, ways[0], ways[1]) == 1
        rows = jnp.where(turn, pltpu.roll(rows, LANES // 2, 1), rows)
        scale = None
        for k in range(4 * ROWS):
            one = jnp.broadcast_to(rows[:, k : k + 1], (8, LANES))
            splats[k] = one
            if k < ROWS:
                scale = one if scale is None else scale * one
        for group in modes or [[(n, n) for n in range(k, k + 3)] for k in range(0, HALF, 3)]:
            waves = []
            for n, m in group:
                waves.append(jnp.broadcast_to(kbuf[n : n + 1, :], (8, LANES)))
                if m != n:
                    other = jnp.broadcast_to(kbuf[m : m + 1, :], (8, LANES))
                    waves[-1] = jnp.where(sub < NXP, waves[-1], other)
            state = [None] * len(group)
            for i in range(ROWS):
                l, u, total, gained = [splats[n * ROWS + i] for n in range(4)]
                for n in range(len(group)):
                    rounded = ((total + waves[n]) - total) + gained
                    if i == 0:
                        state[n] = (l, rounded, l, u + rounded)
                        continue
                    a, b, c, d = state[n]
                    a = l * a + rounded * c
                    b = l * b + rounded * d
                    state[n] = (a, b, a + u * c, b + u * d)
            for n, parts in enumerate(group):
                finish(parts, scaled(state[n] + (scale,)))

    def keep_own(parts, values):
        for n, v in enumerate(values):
            own_products[n, 8 * parts[0] : 8 * parts[0] + 8, :] = v

    block_products([base + j for j in range(NXP)] * 2, (0, 1), keep_own)

    def wait_for(ref, sem):
        pltpu.make_async_copy(ref, ref, sem).wait()

    def wait_for_octet(ref, sem):
        wait_for(ref.at[pl.ds(0, PLANES - 1), pl.ds(0, 32)], sem)

    alone_ends = [[None] * 2, [None] * 2]
    for o in range(2):
        wait_for_octet(rbuf, arrived.at[o])
        if o == 0:
            loads[4].wait()
            loads[5].wait()
        values = []
        for a in range(RADIX):
            values.append(tuple(rbuf[a // 2, pl.ds(32 * o + 2 * part + a % 2, 8, stride=4), :] for part in range(2)))
        values = butterflies(values, False)
        for k in range(RADIX):
            re, im = values[k]
            c, s = twiddle[k : k + 1, :], twiddle[RADIX + k : RADIX + k + 1, :]
            ure[transposed(o, k), :] = re * c + im * s
            uim[transposed(o, k), :] = im * c - re * s
        rows = slice(128 * o, 128 * o + 128)
        result = product(jnp.concatenate([ure[rows, :], uim[rows, :]], axis=1), matrix[...])
        spec[rows, :] = result
        for part in range(2):
            lanes = slice(part * LANES, (part + 1) * LANES)
            for i in range(8):
                r = jnp.concatenate([result[h * 64 + i * 8 : h * 64 + i * 8 + 8, lanes] for h in range(2)], axis=0)
                for way in range(2):
                    share = weights[way, 8 * o + i] * r
                    now = alone_ends[way][part]
                    alone_ends[way][part] = share if now is None else now + share

    def rhs(i, part):
        lanes = slice(part * LANES, (part + 1) * LANES)
        at = [(i // 8) * 128 + h * 64 + (i % 8) * 8 for h in range(2)]
        return jnp.concatenate([spec[n : n + 8, lanes] for n in at], axis=0)

    def half(ref, q, h, rows):
        return ref.at[q, pl.ds(h * rows, rows)]

    for h in range(2):
        for way in range(2):
            for part in range(2):
                at = h * 32 + (2 * way + part) * 8
                raw[xi, at : at + 8, :] = alone_ends[way][part][8 * h : 8 * h + 8, :]
        for q in x_peers:
            remote(half(raw, xi, h, 32), half(raw, xi, h, 32), send_sem.at[3], crossed.at[h], at_x(q)).start()

    for slot in range(4):
        for k in range(4):
            chain[slot, k] = jnp.zeros_like(one) if k in (1, 2) else one

    def next_block(x, shift):
        return tuple(pltpu.roll(v, 8 - shift, 0) for v in x)

    def arrive(q):
        there = coef.at[pl.ds(q * NXP, NXP)]
        remote(there, there, send_sem.at[2], czr_sem.at[q], at_z(q)).wait_recv()

    def keep_groups(pair):
        def keep(parts, values):
            for shift in (1, 2):
                later = next_block(values, shift)
                values = times(later[:4], values[:4]) + (later[4] * values[4],)
            values = scaled(values)
            for m, v in enumerate(values):
                for g in range(2):
                    groups[pair[g], m, parts[g] : parts[g] + 1, :] = v[NXP * g : NXP * g + 1, :]

        return keep

    def join(q, way, upward):
        far = way != int(upward)
        slot = way + 2 * far.astype(jnp.int32)
        whole = tuple(groups[q, k] for k in range(4))
        old = tuple(chain[slot, k] for k in range(4))
        outer = tuple(jnp.where(far, w, o) for w, o in zip(whole, old))
        inner = tuple(jnp.where(far, o, w) for w, o in zip(whole, old))
        for k, v in enumerate(scaled(times(outer, inner))):
            chain[slot, k] = v

    def in_order(q, way):
        return [q * NXP + jnp.where(way == 0, j, NXP - 1 - j) for j in range(NXP)]

    @pl.loop(0, NZ // 2 - 1)
    def _(n):
        pair = (lax.rem(zi + n + 1, NZ), lax.rem(zi + NZ - 1 - n, NZ))
        ways = [(q > zi).astype(jnp.int32) for q in pair]
        for q in pair:
            arrive(q)
        block_products(in_order(pair[0], ways[0]) + in_order(pair[1], ways[1]), ways, keep_groups(pair))
        for q, way, upward in zip(pair, ways, (True, False)):
            join(q, way, upward)

    across = lax.rem(zi + NZ // 2, NZ)
    way = (across > zi).astype(jnp.int32)
    arrive(across)
    block_products(in_order(across, way) * 2, (way, way), keep_groups((across, across)),
                   [[(0, 5), (1, 6), (2, 7)], [(3, 8), (4, 4)]])
    join(across, way, True)

    enter = []
    for way in range(2):
        top, bottom = chain[way + 2, 1], chain[way + 2, 3]
        enter.append((chain[way, 0] * top + chain[way, 1] * bottom) / (chain[way, 2] * top + chain[way, 3] * bottom))
    for j in range(NXP):
        for way in range(2):
            t = j if way == 0 else NXP - 1 - j
            g = enter[way]
            a, b, c, d, scale = [own_products[n, pl.ds(NXP * way + t, RADIX, stride=8), :] for n in range(5)]
            inv = 1.0 / (c * g + d)
            gin[way, t] = mirrored(g)
            abuf[way, t] = mirrored(scale * inv)
            enter[way] = (a * g + b) * inv

    entering = [[[], []], [[], []]]
    for h in range(2):
        part_modes = slice(8 * h, 8 * h + 8)
        wait_for(raw.at[pl.ds(0, NXP - 1), pl.ds(0, 32)], crossed.at[h])
        for way, order in enumerate((range(NXP), range(NXP - 1, -1, -1))):
            none = jnp.zeros((8, LANES), jnp.float32)
            run, mine = [none] * 2, [none] * 2
            for j in order:
                here = xi == j
                a = abuf[way, j, part_modes, :]
                ae = a * (1.0 - gin[way, j, part_modes, :])
                for part in range(2):
                    end, start = [raw[j, n : n + 8, :] for n in (
                        h * 32 + (2 * way + part) * 8, h * 32 + (2 - 2 * way + part) * 8)]
                    mine[part] = jnp.where(here, run[part], mine[part])
                    run[part] = a * run[part] + (end + ae * start)
            for part in range(2):
                at = h * 16 + part * 8
                gz[way, at : at + 8, :] = run[part]
                entering[way][part].append(mine[part])
        for q in z_peers:
            which = jnp.where(q > zi, 0, 1)
            remote(half(gz, which, h, 16), half(zrecv, zi, h, 16), send_sem.at[4], crossed.at[2 + h], at_z(q)).start()
    entering = [[jnp.concatenate(halves, axis=0) for halves in way] for way in entering]

    gbuf[...] = jnp.zeros_like(gbuf)

    @pl.loop(0, NZ - 1)
    def _(n):
        way = (n >= zi).astype(jnp.int32)
        q = jnp.where(n < zi, n, NZ - 1 - (n - zi))
        g = gbuf[way]
        inv = 1.0 / (groups[q, 2] * g + groups[q, 3])
        gbuf[way] = (groups[q, 0] * g + groups[q, 1]) * inv
        wbuf[q] = groups[q, 4] * inv

    def below(n, run):
        q = zi - 1 - n
        a = wbuf[q]
        wbuf[q] = mirrored(run)
        return run * a

    lax.fori_loop(0, zi, below, one)

    def above(n, run):
        q = zi + 1 + n
        a = wbuf[q]
        wbuf[q] = mirrored(run)
        return run * a

    lax.fori_loop(0, NZ - 1 - zi, above, one)
    pre, post = one, one
    for j in range(NXP):
        pre = pre * jnp.where(j < xi, abuf[0, j], 1.0)
        post = post * jnp.where(j > xi, abuf[1, j], 1.0)

    g_end = pivots(range(ROWS), low, upp, gin[0, xi], factors, 0)
    h_in = gin[1, xi]
    scale = 1.0 / (g_end + h_in * factors[2, ROWS - 1])

    for part in range(2):
        y = entering[0][part]
        for i in range(ROWS):
            y = factors[0, i] * y - factors[1, i] * rhs(i, part)
            known[part, i] = y
    reply = pre
    for i in range(ROWS):
        reply = factors[0, i] * reply
        known[2, i] = reply
    last_factor = factors[2, ROWS - 1]
    state = [(last_factor * entering[1][part] + known[part, ROWS - 1]) * scale for part in range(2)]
    state += [known[2, ROWS - 1] * scale, last_factor * scale * post]
    for i in range(ROWS - 1, -1, -1):
        if i < ROWS - 1:
            e = factors[2, i]
            state = [e * state[n] + known[n, i] for n in range(3)] + [e * state[3]]
        for n in range(4):
            known[n, i] = state[n]

    brought = [[], []]
    for h in range(2):
        wait_for(zrecv.at[pl.ds(0, NZ - 1), pl.ds(0, 16)], crossed.at[2 + h])
        none = jnp.zeros((8, LANES), jnp.float32)
        sums = [[none] * 2, [none] * 2]
        for q in z_peers:
            lower_side = q < zi
            w = wbuf[q, 8 * h : 8 * h + 8, :]
            wy = jnp.where(lower_side, w, 0.0)
            wz = jnp.where(lower_side, 0.0, w)
            for part in range(2):
                v = zrecv[q, h * 16 + part * 8 : h * 16 + part * 8 + 8, :]
                sums[0][part] = sums[0][part] + wy * v
                sums[1][part] = sums[1][part] + wz * v
        brought[0].append(sums[0])
        brought[1].append(sums[1])
    sy, sz = [[jnp.concatenate([side[0][part], side[1][part]], axis=0) for part in range(2)] for side in brought]

    def send_back(q, o):
        remote(octet(obuf, q, o), octet(fbuf, gx, o), send_sem.at[5], arrived.at[2 + o], at_gx(q)).start()

    for i in range(ROWS):
        for part, ref in enumerate((ure, uim)):
            x = known[part, i] + (known[2, i] * sy[part] + known[3, i] * sz[part])
            for h in range(2):
                at = (i // 8) * 128 + h * 64 + (i % 8) * 8
                ref[at : at + 8, :] = x[8 * h : 8 * h + 8, :]
    back = product(jnp.concatenate([uim[...], ure[...]], axis=1), matrix[...])
    uim[...] = back[:, :LANES]
    ure[...] = back[:, LANES:]
    for o in range(2):
        values = []
        for k in range(RADIX):
            re = ure[transposed(o, k), :]
            im = uim[transposed(o, k), :]
            c = twiddle[k : k + 1, :] * (1.0 / NX)
            s = twiddle[RADIX + k : RADIX + k + 1, :] * (1.0 / NX)
            values.append((re * c - im * s, im * c + re * s))
        values = butterflies(values, True)
        for a in range(RADIX):
            for part in range(2):
                obuf[a // 2, pl.ds(32 * o + 2 * part + a % 2, 8, stride=4), :] = values[a][part]
        for q in gx_peers[:2]:
            send_back(q, o)
    for o in range(2):
        for q in gx_peers[2:]:
            send_back(q, o)
    own = pltpu.make_async_copy(obuf.at[gx], fbuf.at[gx], load_sem.at[0])
    own.start()
    wait_for(sbuf.at[pl.ds(0, PLANES - 1)], send_sem.at[0])
    wait_for(coef.at[pl.ds(0, NXP - 1)], send_sem.at[1])
    wait_for(coef.at[pl.ds(0, NXP * (NZ - 1))], send_sem.at[2])
    wait_for(raw.at[pl.ds(0, NXP - 1)], send_sem.at[3])
    wait_for(zrecv.at[pl.ds(0, NZ - 1)], send_sem.at[4])
    own.wait()
    wait_for(obuf.at[pl.ds(0, PLANES - 1)], send_sem.at[5])
    for o in range(2):
        wait_for_octet(fbuf, arrived.at[2 + o])


def assemble(fbuf, out, held, sem):
    count = 4 * ROWS // PARTS
    copies = []
    for n in range(PARTS):
        for q in range(PLANES):
            held[pl.ds(n * count * PLANES + q, count, stride=PLANES), :] = fbuf[q, n * count : (n + 1) * count, :]
        rows = pl.ds(n * count * PLANES, count * PLANES)
        copies.append(pltpu.make_async_copy(held.at[rows], out.at[rows], sem.at[n]))
        copies[-1].start()
    for copy in copies:
        copy.wait()


def local(source, lower, upper, span):
    matrix, twiddle = transform_constants()
    f32 = jnp.float32
    dma = pltpu.SemaphoreType.DMA
    vmem = lambda *shape: pltpu.VMEM(shape, f32)
    smem = lambda *shape: pltpu.SMEM(shape, f32)
    any_spec = pl.BlockSpec(memory_space=pl.ANY)
    shape = source.shape
    source = source.reshape(ROWS, 2, PLANES, 2, LANES).transpose(0, 1, 3, 2, 4).reshape(4 * ROWS * PLANES, LANES)
    planes = pl.pallas_call(
        kernel,
        out_shape=jax.ShapeDtypeStruct((PLANES, 64, LANES), f32),
        in_specs=[pl.BlockSpec(memory_space=pltpu.HBM)] * 6,
        out_specs=any_spec,
        scratch_shapes=[
            vmem(4 * ROWS * PLANES, LANES), vmem(PLANES, 64, LANES), vmem(PLANES, 64, LANES),
            vmem(256, LANES), vmem(256, LANES), vmem(256, 256),
            pltpu.VMEM((6 * 256, 256), jnp.bfloat16), vmem(2 * RADIX, LANES),
            smem(ROWS), smem(ROWS), smem(PLANES),
            vmem(BLOCKS, 1, LANES), vmem(4 * ROWS, 8, LANES), vmem(RADIX, LANES), vmem(5, 8 * RADIX, LANES),
            vmem(NZ, 5, RADIX, LANES), vmem(2, NXP, RADIX, LANES), vmem(NZ, RADIX, LANES),
            vmem(2, RADIX, LANES), vmem(2, NXP, RADIX, LANES), vmem(4, 4, RADIX, LANES),
            vmem(4, ROWS, RADIX, LANES), vmem(2, ROWS, RADIX, LANES), vmem(3, ROWS, RADIX, LANES),
            vmem(4, ROWS, RADIX, LANES),
            vmem(NXP, 64, LANES), vmem(2, 32, LANES), vmem(NZ, 32, LANES), vmem(PLANES, 64, LANES),
            dma((6,)), dma((6,)), dma((4,)), dma((4,)), dma((NXP,)), dma((NZ,)),
            pltpu.SemaphoreType.REGULAR, pltpu.SemaphoreType.REGULAR,
        ],
        compiler_params=pltpu.CompilerParams(
            collective_id=0, has_side_effects=True, vmem_limit_bytes=16 * 1024 * 1024),
    )(*[pltpu.with_memory_space_constraint(x, pltpu.HBM)
        for x in (source, lower, upper, span, jnp.asarray(matrix), jnp.asarray(twiddle))])
    result = pl.pallas_call(
        assemble,
        out_shape=jax.ShapeDtypeStruct((ROWS * 4 * PLANES, LANES), f32),
        in_specs=[pl.BlockSpec(memory_space=pltpu.VMEM)],
        out_specs=pl.BlockSpec(memory_space=pltpu.HBM),
        scratch_shapes=[vmem(ROWS * 4 * PLANES, LANES), dma((PARTS,))],
        compiler_params=pltpu.CompilerParams(vmem_limit_bytes=4 * 1024 * 1024),
    )(planes)
    result = result.reshape(ROWS, 2, 2, PLANES, LANES)
    return result.transpose(0, 1, 3, 2, 4).reshape(shape)


def solution(mesh):
    in_specs = (P("gy", None, None, "gx"), P("gy"), P("gy"), P())
    out_specs = P("gy", None, None, "gx")
    return jax.shard_map(local, mesh=mesh, in_specs=in_specs, out_specs=out_specs, check_vma=False)
```

```python
import math

import jax
import jax.numpy as jnp
import ml_dtypes
import numpy as np
from jax import lax
from jax.experimental import pallas as pl
from jax.experimental.pallas import tpu as pltpu
from jax.sharding import PartitionSpec as P

MESH = pl.DeviceIdType.MESH

ROWS = 16
PLANES = 8
NX = 2048
LANES = 128
RADIX = 16
NZ = 8
NXP = 4
BLOCKS = NZ * NXP
HALF = RADIX // 2 + 1
PARTS = 4


def transform_constants():
    lanes = np.arange(LANES)
    angle = 2.0 * np.pi * (np.outer(lanes, lanes) % LANES) / LANES
    c, s = np.cos(angle), np.sin(angle)
    matrix = np.block([[c, -s], [s, c]]).astype(np.float32)
    terms, rest = [], matrix
    for _ in range(3):
        terms.append(rest.astype(ml_dtypes.bfloat16))
        rest = rest - terms[-1].astype(np.float32)
    matrix = np.concatenate([terms[0], terms[1], terms[2], terms[0], terms[1], terms[0]])
    twist = 2.0 * np.pi * (np.outer(np.arange(RADIX), lanes) % NX) / NX
    twiddle = np.concatenate([np.cos(twist), np.sin(twist)]).astype(np.float32)
    return matrix, twiddle


def rotated(value, index, size, inverse):
    re, im = value
    index = index % size
    if index == 0:
        return value
    if 4 * index == size:
        return (-im, re) if inverse else (im, -re)
    c = math.cos(2.0 * math.pi * index / size)
    s = math.sin(2.0 * math.pi * index / size)
    if not inverse:
        s = -s
    return (re * c - im * s, re * s + im * c)


def butterflies(values, inverse):
    size = len(values)
    if size == 1:
        return values
    even = butterflies(values[0::2], inverse)
    odd = butterflies(values[1::2], inverse)
    odd = [rotated(o, k, size, inverse) for k, o in enumerate(odd)]
    low = [(e[0] + o[0], e[1] + o[1]) for e, o in zip(even, odd)]
    high = [(e[0] - o[0], e[1] - o[1]) for e, o in zip(even, odd)]
    return low + high


def product(x, matrix):
    high = x.astype(jnp.bfloat16)
    rest = x - high.astype(jnp.float32)
    middle = rest.astype(jnp.bfloat16)
    low = (rest - middle.astype(jnp.float32)).astype(jnp.bfloat16)
    terms = jnp.concatenate([high, high, high, middle, middle, low], axis=1)
    return jnp.dot(terms, matrix, preferred_element_type=jnp.float32)


def times(x, y):
    a, b, c, d = x
    e, f, g, h = y
    return (a * e + b * g, a * f + b * h, c * e + d * g, c * f + d * h)


def scaled(x):
    r = pl.reciprocal(x[2] + x[3], approx=True)
    return tuple(v * r for v in x)


def mirrored(x):
    sub = lax.broadcasted_iota(jnp.int32, (8, LANES), 0)
    lane = lax.broadcasted_iota(jnp.int32, (8, LANES), 1)
    top = x[0:8, :]
    turned = jnp.take_along_axis(top, LANES - 1 - lane, axis=1)
    turned = jnp.take_along_axis(turned, (8 - sub) % 8, axis=0)
    return jnp.concatenate([top, jnp.where(sub == 0, x[8:16, :], turned)], axis=0)


def transposed(o, k):
    return pl.ds(o * 128 + (k // 8) * 64 + k % 8, 8, stride=8)


def kernel(
    source, lower_hbm, upper_hbm, span_hbm, matrix_hbm, twiddle_hbm, fbuf,
    src, sbuf, rbuf, ure, uim, spec, matrix, twiddle, lower, upper, span,
    coef, splats, kbuf, own_products, groups, abuf, wbuf, gbuf, gin, chain, alone, weights, factors, known,
    raw, gz, zrecv, obuf,
    load_sem, send_sem, crossed, arrived, cxr_sem, czr_sem, near_sem, far_sem,
):
    gx = lax.axis_index("gx")
    gy = lax.axis_index("gy")
    zi = gy // NXP
    xi = gy % NXP
    base = zi * NXP

    chip, core = gx // 2, gx % 2
    gx_peers = [lax.rem(chip + d, PLANES // 2) * 2 + lax.rem(core + c, 2)
                for d, c in ((2, 0), (2, 1), (1, 0), (3, 0), (1, 1), (3, 1), (0, 1))]
    x_peers = [lax.rem(xi + d, NXP) for d in (2, 1, 3)]
    z_peers = [lax.rem(zi + d, NZ) for d in (4, 3, 5, 2, 6, 1, 7)]

    def at_gx(q):
        return (q, gy)

    def at_x(q):
        return (gx, base + q)

    def at_z(q):
        return (gx, q * NXP + xi)

    z_near = [lax.rem(zi + d, NZ) for d in (1, NZ - 1)]
    z_far = [lax.rem(zi + d, NZ) for d in (2, NZ - 2)]
    near = [at_gx(q) for q in gx_peers] + [at_x(q) for q in x_peers] + [at_z(q) for q in z_near]
    loads = [pltpu.make_async_copy(there, here, load_sem.at[n]) for n, (there, here) in enumerate((
        (source, src), (lower_hbm, lower), (upper_hbm, upper), (span_hbm, span),
        (twiddle_hbm, twiddle), (matrix_hbm, matrix)))]
    loads[0].start()
    barrier = pltpu.get_barrier_semaphore()
    for device in near:
        pl.semaphore_signal(barrier, inc=1, device_id=device, device_id_type=MESH)
    for load in loads[1:]:
        load.start()

    loads[0].wait()
    for q in range(PLANES):
        sbuf[q] = src[pl.ds(q, 4 * ROWS, stride=PLANES), :]

    for load in loads[1:4]:
        load.wait()
    first, last = gy == 0, gy == BLOCKS - 1
    low = [lower[i] for i in range(ROWS)]
    upp = [upper[i] for i in range(ROWS)]
    low[0] = jnp.where(first, 0.0, low[0])
    upp[-1] = jnp.where(last, 0.0, upp[-1])
    sums, lost = [], []
    for l, u in zip(low, upp):
        total = l + u
        rest = total - l
        sums.append(total)
        lost.append(-((l - (total - rest)) + (u - rest)))
    lane = lax.broadcasted_iota(jnp.int32, (1, LANES), 1)
    row = jnp.zeros((1, LANES), jnp.float32)
    for i, value in enumerate(low + upp + sums + lost + upp[::-1] + low[::-1] + sums[::-1] + lost[::-1]):
        row = jnp.where(lane == i, value, row)
    coef[gy] = row

    pl.semaphore_wait(barrier, len(near))

    def remote(src_ref, dst_ref, send, recv, device):
        return pltpu.make_async_remote_copy(
            src_ref=src_ref, dst_ref=dst_ref, send_sem=send, recv_sem=recv,
            device_id=device, device_id_type=MESH)

    def wait_for(ref, sem):
        pltpu.make_async_copy(ref, ref, sem).wait()

    coef_x = [remote(coef.at[gy], coef.at[gy], send_sem.at[1], cxr_sem, at_x(q)) for q in x_peers]
    for copy in coef_x:
        copy.start()

    for q in z_near:
        pl.semaphore_signal(near_sem, inc=1, device_id=at_z(q), device_id_type=MESH)

    def octet(ref, q, o):
        return ref.at[q, pl.ds(32 * o, 32)]

    for some in (gx_peers[:2], gx_peers[2:6], gx_peers[6:]):
        for o in range(2):
            for q in some:
                remote(octet(sbuf, q, o), octet(rbuf, gx, o), send_sem.at[0], arrived.at[o], at_gx(q)).start()
    rbuf[gx] = sbuf[gx]


    k1 = lax.broadcasted_iota(jnp.int32, (RADIX, LANES), 0)
    k2 = lax.broadcasted_iota(jnp.int32, (RADIX, LANES), 1)
    mode = k1 + RADIX * k2
    signed = jnp.where(mode < NX // 2, mode, mode - NX).astype(jnp.float32)
    wave = 2.0 * signed / NX
    kappa = span[gx] * span[gx] + wave * wave
    one = jnp.ones((RADIX, LANES), jnp.float32)

    def pivots(order, ahead, behind, g, keep, into):
        for i in order:
            l, u = ahead[i], behind[i]
            s = (((sums[i] + kappa) - sums[i]) + lost[i]) + l * g
            inv = 1.0 / (u + s)
            g = s * inv
            keep[into, i] = l * inv
            keep[into + 1, i] = inv
            if keep is factors:
                keep[into + 2, i] = u * inv
        return g

    pivots(range(ROWS), low, upp, one, alone, 0)
    pivots(range(ROWS - 1, -1, -1), upp, low, one, alone, 2)
    for way, order in enumerate((range(ROWS - 1, -1, -1), range(ROWS))):
        run = -one
        for i in order:
            weights[way, i] = run * alone[2 * way + 1, i]
            run = run * alone[2 * way, i]

    pl.semaphore_wait(near_sem, 2)
    for q in z_far:
        pl.semaphore_signal(far_sem, inc=1, device_id=at_z(q), device_id_type=MESH)

    wait_for(coef.at[pl.ds(0, NXP - 1)], cxr_sem)
    pl.semaphore_wait(far_sem, 2)
    group = coef.at[pl.ds(base, NXP)]
    coef_z = [remote(group, group, send_sem.at[2], czr_sem.at[zi], at_z(q)) for q in z_peers]
    for copy in coef_z:
        copy.start()

    kbuf[...] = kappa

    def block_products(blocks, ways, finish, modes=None):
        rows = jnp.concatenate([coef[t] for t in blocks], axis=0)
        sub = lax.broadcasted_iota(jnp.int32, (8, LANES), 0)
        turn = jnp.where(sub < NXP, ways[0], ways[1]) == 1
        rows = jnp.where(turn, pltpu.roll(rows, LANES // 2, 1), rows)
        scale = None
        for k in range(4 * ROWS):
            one = jnp.broadcast_to(rows[:, k : k + 1], (8, LANES))
            splats[k] = one
            if k < ROWS:
                scale = one if scale is None else scale * one
        for group in modes or [[(n, n) for n in range(k, k + 3)] for k in range(0, HALF, 3)]:
            waves = []
            for n, m in group:
                waves.append(jnp.broadcast_to(kbuf[n : n + 1, :], (8, LANES)))
                if m != n:
                    other = jnp.broadcast_to(kbuf[m : m + 1, :], (8, LANES))
                    waves[-1] = jnp.where(sub < NXP, waves[-1], other)
            state = [None] * len(group)
            for i in range(ROWS):
                l, u, total, gained = [splats[n * ROWS + i] for n in range(4)]
                for n in range(len(group)):
                    rounded = ((total + waves[n]) - total) + gained
                    if i == 0:
                        state[n] = (l, rounded, l, u + rounded)
                        continue
                    a, b, c, d = state[n]
                    a = l * a + rounded * c
                    b = l * b + rounded * d
                    state[n] = (a, b, a + u * c, b + u * d)
            for n, parts in enumerate(group):
                finish(parts, scaled(state[n] + (scale,)))

    def keep_own(parts, values):
        for n, v in enumerate(values):
            own_products[n, 8 * parts[0] : 8 * parts[0] + 8, :] = v

    block_products([base + j for j in range(NXP)] * 2, (0, 1), keep_own)

    def wait_for_octet(ref, sem):
        wait_for(ref.at[pl.ds(0, PLANES - 1), pl.ds(0, 32)], sem)

    alone_ends = [[None] * 2, [None] * 2]
    for o in range(2):
        wait_for_octet(rbuf, arrived.at[o])
        if o == 0:
            loads[4].wait()
            loads[5].wait()
        values = []
        for a in range(RADIX):
            values.append(tuple(rbuf[a // 2, pl.ds(32 * o + 2 * part + a % 2, 8, stride=4), :] for part in range(2)))
        values = butterflies(values, False)
        for k in range(RADIX):
            re, im = values[k]
            c, s = twiddle[k : k + 1, :], twiddle[RADIX + k : RADIX + k + 1, :]
            ure[transposed(o, k), :] = re * c + im * s
            uim[transposed(o, k), :] = im * c - re * s
        rows = slice(128 * o, 128 * o + 128)
        result = product(jnp.concatenate([ure[rows, :], uim[rows, :]], axis=1), matrix[...])
        spec[rows, :] = result
        for part in range(2):
            lanes = slice(part * LANES, (part + 1) * LANES)
            for i in range(8):
                r = jnp.concatenate([result[h * 64 + i * 8 : h * 64 + i * 8 + 8, lanes] for h in range(2)], axis=0)
                for way in range(2):
                    share = weights[way, 8 * o + i] * r
                    now = alone_ends[way][part]
                    alone_ends[way][part] = share if now is None else now + share

    def rhs(i, part):
        lanes = slice(part * LANES, (part + 1) * LANES)
        at = [(i // 8) * 128 + h * 64 + (i % 8) * 8 for h in range(2)]
        return jnp.concatenate([spec[n : n + 8, lanes] for n in at], axis=0)

    def half(ref, q, h, rows):
        return ref.at[q, pl.ds(h * rows, rows)]

    for h in range(2):
        for way in range(2):
            for part in range(2):
                at = h * 32 + (2 * way + part) * 8
                raw[xi, at : at + 8, :] = alone_ends[way][part][8 * h : 8 * h + 8, :]
    for some in (x_peers[:1], x_peers[1:]):
        for h in range(2):
            for q in some:
                remote(half(raw, xi, h, 32), half(raw, xi, h, 32), send_sem.at[3], crossed.at[h], at_x(q)).start()

    for slot in range(4):
        for k in range(4):
            chain[slot, k] = jnp.zeros_like(one) if k in (1, 2) else one

    def next_block(x, shift):
        return tuple(pltpu.roll(v, 8 - shift, 0) for v in x)

    def arrive(q):
        there = coef.at[pl.ds(q * NXP, NXP)]
        remote(there, there, send_sem.at[2], czr_sem.at[q], at_z(q)).wait_recv()

    def keep_groups(pair):
        def keep(parts, values):
            for shift in (1, 2):
                later = next_block(values, shift)
                values = times(later[:4], values[:4]) + (later[4] * values[4],)
            values = scaled(values)
            for m, v in enumerate(values):
                for g in range(2):
                    groups[pair[g], m, parts[g] : parts[g] + 1, :] = v[NXP * g : NXP * g + 1, :]

        return keep

    def join(q, way, upward):
        far = way != int(upward)
        slot = way + 2 * far.astype(jnp.int32)
        whole = tuple(groups[q, k] for k in range(4))
        old = tuple(chain[slot, k] for k in range(4))
        outer = tuple(jnp.where(far, w, o) for w, o in zip(whole, old))
        inner = tuple(jnp.where(far, o, w) for w, o in zip(whole, old))
        for k, v in enumerate(scaled(times(outer, inner))):
            chain[slot, k] = v

    def in_order(q, way):
        return [q * NXP + jnp.where(way == 0, j, NXP - 1 - j) for j in range(NXP)]

    @pl.loop(0, NZ // 2 - 1)
    def _(n):
        pair = (lax.rem(zi + n + 1, NZ), lax.rem(zi + NZ - 1 - n, NZ))
        ways = [(q > zi).astype(jnp.int32) for q in pair]
        for q in pair:
            arrive(q)
        block_products(in_order(pair[0], ways[0]) + in_order(pair[1], ways[1]), ways, keep_groups(pair))
        for q, way, upward in zip(pair, ways, (True, False)):
            join(q, way, upward)

    across = lax.rem(zi + NZ // 2, NZ)
    way = (across > zi).astype(jnp.int32)
    arrive(across)
    block_products(in_order(across, way) * 2, (way, way), keep_groups((across, across)),
                   [[(0, 5), (1, 6), (2, 7)], [(3, 8), (4, 4)]])
    join(across, way, True)

    enter = []
    for way in range(2):
        top, bottom = chain[way + 2, 1], chain[way + 2, 3]
        enter.append((chain[way, 0] * top + chain[way, 1] * bottom) / (chain[way, 2] * top + chain[way, 3] * bottom))
    for j in range(NXP):
        for way in range(2):
            t = j if way == 0 else NXP - 1 - j
            g = enter[way]
            a, b, c, d, scale = [own_products[n, pl.ds(NXP * way + t, RADIX, stride=8), :] for n in range(5)]
            inv = 1.0 / (c * g + d)
            gin[way, t] = mirrored(g)
            abuf[way, t] = mirrored(scale * inv)
            enter[way] = (a * g + b) * inv

    entering = [[[], []], [[], []]]
    for h in range(2):
        part_modes = slice(8 * h, 8 * h + 8)
        wait_for(raw.at[pl.ds(0, NXP - 1), pl.ds(0, 32)], crossed.at[h])
        for way, order in enumerate((range(NXP), range(NXP - 1, -1, -1))):
            none = jnp.zeros((8, LANES), jnp.float32)
            run, mine = [none] * 2, [none] * 2
            for j in order:
                here = xi == j
                a = abuf[way, j, part_modes, :]
                ae = a * (1.0 - gin[way, j, part_modes, :])
                for part in range(2):
                    end, start = [raw[j, n : n + 8, :] for n in (
                        h * 32 + (2 * way + part) * 8, h * 32 + (2 - 2 * way + part) * 8)]
                    mine[part] = jnp.where(here, run[part], mine[part])
                    run[part] = a * run[part] + (end + ae * start)
            for part in range(2):
                at = h * 16 + part * 8
                gz[way, at : at + 8, :] = run[part]
                entering[way][part].append(mine[part])
        for q in z_peers:
            which = jnp.where(q > zi, 0, 1)
            remote(half(gz, which, h, 16), half(zrecv, zi, h, 16), send_sem.at[4], crossed.at[2 + h], at_z(q)).start()
    entering = [[jnp.concatenate(halves, axis=0) for halves in way] for way in entering]

    gbuf[...] = jnp.zeros_like(gbuf)

    @pl.loop(0, NZ - 1)
    def _(n):
        way = (n >= zi).astype(jnp.int32)
        q = jnp.where(n < zi, n, NZ - 1 - (n - zi))
        g = gbuf[way]
        inv = 1.0 / (groups[q, 2] * g + groups[q, 3])
        gbuf[way] = (groups[q, 0] * g + groups[q, 1]) * inv
        wbuf[q] = groups[q, 4] * inv

    def below(n, run):
        q = zi - 1 - n
        a = wbuf[q]
        wbuf[q] = mirrored(run)
        return run * a

    lax.fori_loop(0, zi, below, one)

    def above(n, run):
        q = zi + 1 + n
        a = wbuf[q]
        wbuf[q] = mirrored(run)
        return run * a

    lax.fori_loop(0, NZ - 1 - zi, above, one)
    pre, post = one, one
    for j in range(NXP):
        pre = pre * jnp.where(j < xi, abuf[0, j], 1.0)
        post = post * jnp.where(j > xi, abuf[1, j], 1.0)

    g_end = pivots(range(ROWS), low, upp, gin[0, xi], factors, 0)
    h_in = gin[1, xi]
    scale = 1.0 / (g_end + h_in * factors[2, ROWS - 1])

    for part in range(2):
        y = entering[0][part]
        for i in range(ROWS):
            y = factors[0, i] * y - factors[1, i] * rhs(i, part)
            known[part, i] = y
    reply = pre
    for i in range(ROWS):
        reply = factors[0, i] * reply
        known[2, i] = reply
    last_factor = factors[2, ROWS - 1]
    state = [(last_factor * entering[1][part] + known[part, ROWS - 1]) * scale for part in range(2)]
    state += [known[2, ROWS - 1] * scale, last_factor * scale * post]
    for i in range(ROWS - 1, -1, -1):
        if i < ROWS - 1:
            e = factors[2, i]
            state = [e * state[n] + known[n, i] for n in range(3)] + [e * state[3]]
        for n in range(4):
            known[n, i] = state[n]

    brought = [[], []]
    for h in range(2):
        wait_for(zrecv.at[pl.ds(0, NZ - 1), pl.ds(0, 16)], crossed.at[2 + h])
        none = jnp.zeros((8, LANES), jnp.float32)
        sums = [[none] * 2, [none] * 2]
        for q in z_peers:
            lower_side = q < zi
            w = wbuf[q, 8 * h : 8 * h + 8, :]
            wy = jnp.where(lower_side, w, 0.0)
            wz = jnp.where(lower_side, 0.0, w)
            for part in range(2):
                v = zrecv[q, h * 16 + part * 8 : h * 16 + part * 8 + 8, :]
                sums[0][part] = sums[0][part] + wy * v
                sums[1][part] = sums[1][part] + wz * v
        brought[0].append(sums[0])
        brought[1].append(sums[1])
    sy, sz = [[jnp.concatenate([side[0][part], side[1][part]], axis=0) for part in range(2)] for side in brought]

    def send_back(q, o):
        remote(octet(obuf, q, o), octet(fbuf, gx, o), send_sem.at[5], arrived.at[2 + o], at_gx(q)).start()

    for i in range(ROWS):
        for part, ref in enumerate((ure, uim)):
            x = known[part, i] + (known[2, i] * sy[part] + known[3, i] * sz[part])
            for h in range(2):
                at = (i // 8) * 128 + h * 64 + (i % 8) * 8
                ref[at : at + 8, :] = x[8 * h : 8 * h + 8, :]
    back = product(jnp.concatenate([uim[...], ure[...]], axis=1), matrix[...])
    uim[...] = back[:, :LANES]
    ure[...] = back[:, LANES:]
    for o in range(2):
        values = []
        for k in range(RADIX):
            re = ure[transposed(o, k), :]
            im = uim[transposed(o, k), :]
            c = twiddle[k : k + 1, :] * (1.0 / NX)
            s = twiddle[RADIX + k : RADIX + k + 1, :] * (1.0 / NX)
            values.append((re * c - im * s, im * c + re * s))
        values = butterflies(values, True)
        for a in range(RADIX):
            for part in range(2):
                obuf[a // 2, pl.ds(32 * o + 2 * part + a % 2, 8, stride=4), :] = values[a][part]
        for q in gx_peers[:2]:
            send_back(q, o)
    for o in range(2):
        for q in gx_peers[2:]:
            send_back(q, o)
    own = pltpu.make_async_copy(obuf.at[gx], fbuf.at[gx], load_sem.at[0])
    own.start()
    wait_for(sbuf.at[pl.ds(0, PLANES - 1)], send_sem.at[0])
    wait_for(coef.at[pl.ds(0, NXP - 1)], send_sem.at[1])
    wait_for(coef.at[pl.ds(0, NXP * (NZ - 1))], send_sem.at[2])
    wait_for(raw.at[pl.ds(0, NXP - 1)], send_sem.at[3])
    wait_for(zrecv.at[pl.ds(0, NZ - 1)], send_sem.at[4])
    own.wait()
    wait_for(obuf.at[pl.ds(0, PLANES - 1)], send_sem.at[5])
    for o in range(2):
        wait_for_octet(fbuf, arrived.at[2 + o])


def assemble(fbuf, out, held, sem):
    count = 4 * ROWS // PARTS
    copies = []
    for n in range(PARTS):
        for q in range(PLANES):
            held[pl.ds(n * count * PLANES + q, count, stride=PLANES), :] = fbuf[q, n * count : (n + 1) * count, :]
        rows = pl.ds(n * count * PLANES, count * PLANES)
        copies.append(pltpu.make_async_copy(held.at[rows], out.at[rows], sem.at[n]))
        copies[-1].start()
    for copy in copies:
        copy.wait()


def local(source, lower, upper, span):
    matrix, twiddle = transform_constants()
    f32 = jnp.float32
    dma = pltpu.SemaphoreType.DMA
    vmem = lambda *shape: pltpu.VMEM(shape, f32)
    smem = lambda *shape: pltpu.SMEM(shape, f32)
    any_spec = pl.BlockSpec(memory_space=pl.ANY)
    shape = source.shape
    source = source.reshape(ROWS, 2, PLANES, 2, LANES).transpose(0, 1, 3, 2, 4).reshape(4 * ROWS * PLANES, LANES)
    planes = pl.pallas_call(
        kernel,
        out_shape=jax.ShapeDtypeStruct((PLANES, 64, LANES), f32),
        in_specs=[pl.BlockSpec(memory_space=pltpu.HBM)] * 6,
        out_specs=any_spec,
        scratch_shapes=[
            vmem(4 * ROWS * PLANES, LANES), vmem(PLANES, 64, LANES), vmem(PLANES, 64, LANES),
            vmem(256, LANES), vmem(256, LANES), vmem(256, 256),
            pltpu.VMEM((6 * 256, 256), jnp.bfloat16), vmem(2 * RADIX, LANES),
            smem(ROWS), smem(ROWS), smem(PLANES),
            vmem(BLOCKS, 1, LANES), vmem(4 * ROWS, 8, LANES), vmem(RADIX, LANES), vmem(5, 8 * RADIX, LANES),
            vmem(NZ, 5, RADIX, LANES), vmem(2, NXP, RADIX, LANES), vmem(NZ, RADIX, LANES),
            vmem(2, RADIX, LANES), vmem(2, NXP, RADIX, LANES), vmem(4, 4, RADIX, LANES),
            vmem(4, ROWS, RADIX, LANES), vmem(2, ROWS, RADIX, LANES), vmem(3, ROWS, RADIX, LANES),
            vmem(4, ROWS, RADIX, LANES),
            vmem(NXP, 64, LANES), vmem(2, 32, LANES), vmem(NZ, 32, LANES), vmem(PLANES, 64, LANES),
            dma((6,)), dma((6,)), dma((4,)), dma((4,)), dma, dma((NZ,)),
            pltpu.SemaphoreType.REGULAR, pltpu.SemaphoreType.REGULAR,
        ],
        compiler_params=pltpu.CompilerParams(
            collective_id=0, has_side_effects=True, vmem_limit_bytes=16 * 1024 * 1024),
    )(*[pltpu.with_memory_space_constraint(x, pltpu.HBM)
        for x in (source, lower, upper, span, jnp.asarray(matrix), jnp.asarray(twiddle))])
    result = pl.pallas_call(
        assemble,
        out_shape=jax.ShapeDtypeStruct((ROWS * 4 * PLANES, LANES), f32),
        in_specs=[pl.BlockSpec(memory_space=pltpu.VMEM)],
        out_specs=pl.BlockSpec(memory_space=pltpu.HBM),
        scratch_shapes=[vmem(ROWS * 4 * PLANES, LANES), dma((PARTS,))],
        compiler_params=pltpu.CompilerParams(vmem_limit_bytes=4 * 1024 * 1024),
    )(planes)
    result = result.reshape(ROWS, 2, 2, PLANES, LANES)
    return result.transpose(0, 1, 3, 2, 4).reshape(shape)


def solution(mesh):
    in_specs = (P("gy", None, None, "gx"), P("gy"), P("gy"), P())
    out_specs = P("gy", None, None, "gx")
    return jax.shard_map(local, mesh=mesh, in_specs=in_specs, out_specs=out_specs, check_vma=False)
```
